32 devices in a mesh: rep: 4 (over z), ex: 8 (over y, x, core).
Axes of the slice: x: 2, y: 2, z: 4, core: 2. Of those that a mesh axis runs over, the one named last changes fastest.
Arguments:
- tokens: bfloat16 [25088, 768], P(('rep', 'ex')), may hold values from -6 to 6
- gain_one: float32 [768], replicated, may hold values from 0.5 to 1.5
- shift_one: float32 [768], replicated, may hold values from -0.625 to 0.625
- w_qkv: bfloat16 [768, 2304], replicated, may hold values from -0.21875 to 0.21875
- w_out: bfloat16 [768, 768], replicated, may hold values from -1.75 to 1.75
- gain_two: float32 [768], replicated, may hold values from 0.5 to 1.5
- shift_two: float32 [768], replicated, may hold values from -0.625 to 0.625
- w_router: bfloat16 [768, 8], replicated, may hold values from -0.15625 to 0.15625
- w_in: bfloat16 [8, 768, 3072], P('ex'), may hold values from -0.21875 to 0.21875
- bias_in: float32 [8, 3072], P('ex'), may hold values from -0.625 to 0.625
- w_back: bfloat16 [8, 3072, 768], P('ex'), may hold values from -0.5 to 0.5
- bias_back: float32 [8, 768], P('ex'), may hold values from -2 to 2
- cotangent: bfloat16 [25088, 768], P(('rep', 'ex')), may hold values from -6 to 6
- routes: int32 [25088, 2], P(('rep', 'ex')), may hold values from 0 to 7, all different within a row
- priority: int32 [32, 784], P(('rep', 'ex')), may hold values from 0 to 783, each once within a row
- image_kind: int32 [32], P(('rep', 'ex')), may hold values from 0 to 1
Outputs:
- result: bfloat16 [25088, 768], P(('rep', 'ex'))
- grad_tokens: bfloat16 [25088, 768], P(('rep', 'ex'))
- grad_gain_one: float32 [768], replicated
- grad_shift_one: float32 [768], replicated
- grad_w_qkv: float32 [768, 2304], replicated
- grad_w_out: float32 [768, 768], replicated
- grad_gain_two: float32 [768], replicated
- grad_shift_two: float32 [768], replicated
- grad_w_router: float32 [768, 8], replicated
- grad_w_in: float32 [8, 768, 3072], P('ex', 'rep')
- grad_bias_in: float32 [8, 3072], P('ex', 'rep')
- grad_w_back: float32 [8, 3072, 768], P('ex', 'rep')
- grad_bias_back: float32 [8, 768], P('ex', 'rep')
The draws below stay inside these ranges and needn't reach their ends.
Inputs may be any that keep to these rules, and one draw needn't show every extreme that they name: `routes`: each row names two different experts. `priority`: each device's row holds every rank once. `image_kind`: 0: a set holds four images of 196 patches; 1: one image of 576 patches, one of 196, then 3 * 196 - 576 padding rows that attend only to one another.
All inputs are finite; a program needn't handle non-finite values.
Results may differ from the reference program's by a relative error of at most 0.015.
Values may be sent and summed in bfloat16 or wider, within the bound.
No kernel may reach another device: no remote copies, remote signals or barrier semaphores. Data moves between devices by JAX's collectives and lax.ppermute only.
A program may use at most 256 MiB of HBM per device.

```python
from functools import partial
import jax
import jax.numpy as jnp
from jax import lax

D = 768
HEADS = 12
HEAD_DIM = 64
FF = 3072
PATCH_S = 196
PATCH_L = 576
SETS = 1
TOK_DEV = 784
TOKENS = 25088
EXPERTS = 8
CAP = 206
N_REP = 4
N_EX = 8


def place_ends(values, key, least, high):
    dims = values.shape
    spot = [jax.random.randint(jax.random.fold_in(key, axis), (), 0, dims[axis]) for axis in range(len(dims))]
    values = values.at[tuple(spot)].set(least)
    longest = dims.index(max(dims))
    spot[longest] = (spot[longest] + 1) % dims[longest]
    return values.at[tuple(spot)].set(high)


def block_scale(own_key, shape, pieces, least, high):
    loudness, own = 1.0, jax.random.fold_in(own_key, 6)
    for dim, shards_of in pieces:
        steps = jnp.exp(jax.random.uniform(jax.random.fold_in(own, dim), (shards_of,), jnp.float32, least / len(pieces), high / len(pieces)))
        loudness = loudness * jnp.repeat(steps, shape[dim] // shards_of).reshape([-1 if axis == dim else 1 for axis in range(len(shape))])
    return loudness


def different_ones(stream_key, rows, number_of, top, lift):
    sequence = jax.random.permutation(jax.random.fold_in(stream_key, 1), number_of)
    favour = sequence
    for power in range(3):
        favour = favour * favour // number_of
    favour = favour * lift // number_of
    chance = jax.random.randint(jax.random.fold_in(stream_key, 2), (rows, number_of), 0, 4096) + favour
    fixed_rows = jax.random.permutation(jax.random.fold_in(stream_key, 3), rows)[jnp.arange(number_of) % rows]
    chance = jnp.where(jnp.arange(rows)[:, None] == fixed_rows[None, :], 1 << 14, chance)
    merit = chance * number_of + jnp.arange(number_of)
    return lax.top_k(merit.astype(jnp.int32), top)[1].astype(jnp.int32)


def noise(stream_key, shape, scale, limit, cuts=(), kind=jnp.bfloat16):
    entries = scale * jax.random.normal(stream_key, shape, jnp.float32)
    if cuts:
        entries = entries * block_scale(stream_key, shape, cuts, -0.22, 0.18)
    return jnp.clip(entries, -limit, limit).astype(kind)


def setup_inputs(seed: int = 0) -> dict:
    key_list = jax.random.split(jax.random.key(seed), 17)
    return {
        "tokens": noise(key_list[0], (TOKENS, D), 1.0, 6.0, ((0, 32),)),
        "gain_one": jnp.clip(1.0 + 0.1 * jax.random.normal(key_list[1], (D,), jnp.float32), 0.5, 1.5),
        "shift_one": noise(key_list[2], (D,), 0.1, 0.625, (), jnp.float32),
        "w_qkv": noise(key_list[3], (D, 3 * D), D ** -0.5, 0.21875),
        "w_out": noise(key_list[4], (D, D), (max(D // 64, 1)) ** -0.5, 1.75),
        "gain_two": jnp.clip(1.0 + 0.1 * jax.random.normal(key_list[5], (D,), jnp.float32), 0.5, 1.5),
        "shift_two": noise(key_list[6], (D,), 0.1, 0.625, (), jnp.float32),
        "w_router": noise(key_list[7], (D, EXPERTS), (D * 16 // 9) ** -0.5, 0.15625),
        "w_in": noise(key_list[8], (EXPERTS, D, FF), D ** -0.5, 0.21875, ((0, 8),)),
        "bias_in": noise(key_list[9], (EXPERTS, FF), 0.1, 0.625, ((0, 8),), jnp.float32),
        "w_back": noise(key_list[10], (EXPERTS, FF, D), (max(FF * 3 // (EXPERTS * EXPERTS), 1)) ** -0.5, 0.5, ((0, 8),)),
        "bias_back": noise(key_list[11], (EXPERTS, D), (0.04 * EXPERTS), 2.0, ((0, 8),), jnp.float32),
        "cotangent": noise(key_list[12], (TOKENS, D), 1.0, 6.0, ((0, 32),)),
        "routes": different_ones(key_list[13], TOKENS, EXPERTS, 2, 2048),
        "priority": jax.vmap(lambda own: jax.random.permutation(own, TOK_DEV))(jax.random.split(key_list[14], (N_REP * N_EX))).reshape((N_REP * N_EX, TOK_DEV)).astype(jnp.int32),
        "image_kind": place_ends(jax.random.randint(key_list[15], (N_REP * N_EX * SETS,), 0, 2), jax.random.fold_in(key_list[15], 1), 0, 1).astype(jnp.int32),
    }


@jax.custom_vjp
def low(v):
    return lax.optimization_barrier(v.astype(jnp.bfloat16)).astype(jnp.float32)

@jax.custom_vjp
def low_back(v):
    return v

def low_keep(v):
    return (low(v), None)

def low_pass(kept, grad):
    return (grad,)

def back_keep(v):
    return (v, None)

def back_low(kept, grad):
    return (low(grad),)
low.defvjp(low_keep, low_pass)
low_back.defvjp(back_keep, back_low)
EPS = 1e-06
NEG = -1e+30
HIGH = lax.Precision.HIGHEST

def norm_rows(values, gain, shift):
    average = lax.optimization_barrier(jnp.mean(values, axis=-1, keepdims=True))
    centered = values - average
    variance = lax.optimization_barrier(jnp.mean(centered * centered, axis=-1, keepdims=True))
    return centered * lax.rsqrt(variance + EPS) * gain + shift

def set_segments(set_kind):
    positions = jnp.arange(4 * PATCH_S, dtype=jnp.int32)
    small_ids = positions // PATCH_S
    large_ids = jnp.where(positions < PATCH_L, 0, jnp.where(positions < PATCH_L + PATCH_S, 1, 2)).astype(jnp.int32)
    return jnp.where(set_kind == 1, large_ids, small_ids)

def device_slots(chosen, ranking, experts, slot_cap):
    tok_count = chosen.shape[0]
    pair_order = jnp.concatenate([ranking, ranking + tok_count]).astype(jnp.int32)
    target = jnp.concatenate([chosen[:, 0], chosen[:, 1]]).astype(jnp.int32)
    by_rank = jnp.zeros((2 * tok_count,), jnp.int32).at[pair_order].set(target)
    labels = jnp.arange(experts, dtype=jnp.int32)
    one_hot = (by_rank[:, None] == labels[None, :]).astype(jnp.int32)
    before = jnp.cumsum(one_hot, axis=0) - one_hot
    placed = lax.optimization_barrier(jnp.sum(before * one_hot, axis=1))
    position = placed[pair_order]
    kept_mask = position < slot_cap
    slot_ids = jnp.where(kept_mask, target * slot_cap + position, -1).astype(jnp.int32)
    pair_ids = jnp.arange(2 * tok_count, dtype=jnp.int32)
    landing = jnp.where(kept_mask, slot_ids, experts * slot_cap).astype(jnp.int32)
    source = jnp.full((experts * slot_cap,), -1, jnp.int32).at[landing].set(pair_ids, mode='drop')
    return (source, slot_ids.reshape(2, tok_count).T)

def pick_rows(table, slot_ids):
    return jnp.where(slot_ids[:, None] >= 0, table[jnp.maximum(slot_ids, 0)], 0.0)

def attend_set(normed, segment, w_qkv, w_out):
    row_total = normed.shape[0]
    packed = low(low_back(jnp.dot(low(normed), w_qkv, precision=HIGH)))
    by_heads = packed.reshape(row_total, 3, HEADS, HEAD_DIM)
    queries = by_heads[:, 0]
    keys_part = by_heads[:, 1]
    values = by_heads[:, 2]
    scores = jnp.einsum('qhd,khd->hqk', queries, keys_part, precision=HIGH) * HEAD_DIM ** (-0.5)
    scores = low_back(scores)
    linked = segment[:, None] == segment[None, :]
    scores = jnp.where(linked[None], scores, NEG)
    weights = jax.nn.softmax(scores, axis=-1)
    head_mix = jnp.einsum('hqk,khd->qhd', low(weights), values, precision=HIGH).reshape(row_total, D)
    head_mix = low(low_back(head_mix))
    return low_back(jnp.dot(head_mix, w_out, precision=HIGH))

def reference(tokens, gain_one, shift_one, w_qkv, w_out, gain_two, shift_two, w_router, w_in, bias_in, w_back, bias_back, cotangent, routes, priority, image_kind):
    devices = N_REP * N_EX
    slotter = jax.vmap(partial(device_slots, experts=EXPERTS, slot_cap=CAP))
    source, slot_index = slotter(routes.reshape(devices, TOK_DEV, 2), priority)
    kept_mask = (slot_index >= 0).astype(jnp.float32)
    chosen = routes.reshape(devices, TOK_DEV, 2)

    def forward(inputs, g_one, s_one, wq, wo, g_two, s_two, wr, wi, bi, wb, bb):
        normed_one = norm_rows(inputs, g_one, s_one)
        sets = normed_one.reshape(-1, 4 * PATCH_S, D)

        def one_set(packed_in):
            normed, set_kind = packed_in
            return attend_set(normed, set_segments(set_kind), wq, wo)
        branch = lax.map(jax.checkpoint(one_set), (sets, image_kind)).reshape(-1, D)
        residual = inputs + branch
        lowered = low(norm_rows(residual, g_two, s_two))
        logits = low_back(jnp.dot(lowered, wr, precision=HIGH))
        router_probs = jax.nn.softmax(logits, axis=-1)
        local_rows = lowered.reshape(devices, TOK_DEV, D)
        pair_rows = jnp.concatenate([local_rows, local_rows], axis=1)
        buffer = low_back(jax.vmap(pick_rows)(pair_rows, source))
        grouped = buffer.reshape(N_REP, N_EX, EXPERTS, CAP, D).transpose(2, 0, 1, 3, 4).reshape(EXPERTS, -1, D)

        def one_expert(packed_in):
            table, first_w, first_b, second_w, second_b = packed_in
            pre_act = low_back(jnp.dot(table, first_w, precision=HIGH) + first_b)
            hidden = low(jax.nn.gelu(pre_act, approximate=False))
            return low(low_back(jnp.dot(hidden, second_w, precision=HIGH) + second_b))
        produced = lax.map(jax.checkpoint(one_expert), (grouped, wi, bi, wb, bb))
        returned = produced.reshape(EXPERTS, N_REP, N_EX, CAP, D).transpose(1, 2, 0, 3, 4).reshape(devices, EXPERTS * CAP, D)
        pair_out = jax.vmap(pick_rows)(returned, slot_index.reshape(devices, -1)).reshape(devices, TOK_DEV, 2, D)
        gate_values = jnp.take_along_axis(router_probs.reshape(devices, TOK_DEV, EXPERTS), chosen, axis=2) * kept_mask
        combined = lax.optimization_barrier(jnp.sum(gate_values[..., None] * pair_out, axis=2)).reshape(-1, D)
        return residual + combined
    float_args = tuple((member.astype(jnp.float32) for member in (tokens, gain_one, shift_one, w_qkv, w_out, gain_two, shift_two, w_router, w_in, bias_in, w_back, bias_back)))
    output, pullback = jax.vjp(forward, *float_args)
    grads = pullback(cotangent.astype(jnp.float32))
    return (output.astype(jnp.bfloat16), grads[0].astype(jnp.bfloat16), grads[1], grads[2], grads[3], grads[4], grads[5], grads[6], grads[7], grads[8], grads[9], grads[10], grads[11])
```

```python
import functools

import jax
import jax.numpy as jnp
from jax import lax
from jax.experimental import pallas as pl
from jax.experimental.pallas import tpu as pltpu
from jax.sharding import PartitionSpec as P

HEADS = 12
HEAD_DIM = 64
PATCH_S = 196
PATCH_L = 576
GROUP = 4
LANES = GROUP * HEAD_DIM

EPS = 1e-06
NEG = -1e30
SCALE = HEAD_DIM ** (-0.5)
LOG2E = 1.4426950408889634
INV_ROOT_TAU = 0.3989422804014327
PHI_RATE = 0.3
PHI_FIT = (
    0.11962929778234231,
    0.1207539739440115,
    0.09991336806177473,
    0.1285620774229096,
    -0.05368457415108751,
    0.20635459820469867,
    -0.1572037608415104,
    0.03567494667893269,
)
F32 = jnp.float32
BF16 = jnp.bfloat16


def dot_nn(a, b):
    return lax.dot_general(a, b, (((1,), (0,)), ((), ())), preferred_element_type=F32)


def dot_nt(a, b):
    return lax.dot_general(a, b, (((1,), (1,)), ((), ())), preferred_element_type=F32)


def dot_tn(a, b):
    return lax.dot_general(a, b, (((0,), (0,)), ((), ())), preferred_element_type=F32)


def iota(shape, dim):
    return lax.broadcasted_iota(jnp.int32, shape, dim)


def call(body, out_shape, in_specs=None, out_specs=None, grid=None, scratch=(), cost=None, name=None):
    args = dict(out_shape=out_shape, scratch_shapes=list(scratch), name=name)
    if grid is not None:
        args["grid"] = grid
    if in_specs is not None:
        args["in_specs"] = in_specs
    if out_specs is not None:
        args["out_specs"] = out_specs
    if cost is not None:
        args["cost_estimate"] = pl.CostEstimate(
            flops=int(cost[0]), bytes_accessed=int(cost[1]), transcendentals=int(cost[2])
        )
    return pl.pallas_call(
        body,
        compiler_params=pltpu.CompilerParams(vmem_limit_bytes=60 * 1024 * 1024),
        **args,
    )


def whole(shape, memory_space=None):
    zeros = (0,) * len(shape)
    if memory_space is not None:
        return pl.BlockSpec(shape, lambda *_: zeros, memory_space=memory_space)
    return pl.BlockSpec(shape, lambda *_: zeros)


def norm_stats(values):
    average = jnp.mean(values, axis=-1, keepdims=True)
    centered = values - average
    variance = jnp.mean(centered * centered, axis=-1, keepdims=True)
    inverse = lax.rsqrt(variance + EPS)
    return centered * inverse, inverse


def norm_grad(grad, scaled, inverse, gain):
    through = grad * gain
    first = jnp.mean(through, axis=-1, keepdims=True)
    second = jnp.mean(through * scaled, axis=-1, keepdims=True)
    return inverse * (through - first - scaled * second)


def row_chunk(rows):
    for size in (112, 128, 64, 48, 32, 16):
        if rows % size == 0:
            return size
    return rows


def prep_body(experts, cap, cap_pad, routes_ref, prio_ref, cot_ref, slot_ref, col_ref, out_ref):
    toks = cot_ref.shape[0]
    prio = prio_ref[...].astype(F32)
    prio_col = jnp.sum(
        jnp.where(iota((toks, toks), 0) == iota((toks, toks), 1), prio, 0.0), axis=1, keepdims=True
    )
    below = jnp.where(prio_col < prio, 1.0, 0.0).astype(BF16)
    labels = iota((experts, toks), 0)
    first = routes_ref[0:1, :]
    second = routes_ref[1:2, :]
    hot_one = jnp.where(labels == first, 1.0, 0.0)
    hot_two = jnp.where(labels == second, 1.0, 0.0)
    count_one = dot_nn(hot_one.astype(BF16), below)
    count_two = dot_nn(hot_two.astype(BF16), below)
    total_one = jnp.sum(hot_one, axis=1, keepdims=True)
    place_one = jnp.sum(hot_one * count_one, axis=0, keepdims=True)
    place_two = jnp.sum(hot_two * (count_two + total_one), axis=0, keepdims=True)
    slot_one = jnp.where(
        place_one < cap, first * cap_pad + place_one.astype(jnp.int32), -1
    )
    slot_two = jnp.where(
        place_two < cap, second * cap_pad + place_two.astype(jnp.int32), -1
    )
    slot_ref[0:1, :] = slot_one
    slot_ref[1:2, :] = slot_two
    eye = iota((toks, toks), 0) == iota((toks, toks), 1)
    col_one = jnp.sum(jnp.where(eye, slot_one, 0), axis=1, keepdims=True)
    col_two = jnp.sum(jnp.where(eye, slot_two, 0), axis=1, keepdims=True)
    lane = iota((toks, 128), 1)
    col_ref[...] = jnp.where(lane == 0, col_one, jnp.where(lane == 1, col_two, -1))

    def block(expert, carry):
        spots = iota((cap_pad, toks), 0) + expert * cap_pad
        hot = jnp.where((spots == slot_one) | (spots == slot_two), 1.0, 0.0).astype(BF16)
        out_ref[expert] = dot_nn(hot, cot_ref[...]).astype(BF16)
        return carry

    lax.fori_loop(0, experts, block, 0)


def region_bias(kind, start, size, lower, upper, by_rows=True):
    first = iota((size, size), 0) + start
    second = iota((size, size), 1) + start
    if kind == 1:
        seg = lambda p: jnp.where(p < PATCH_L, 0, jnp.where(p < PATCH_L + PATCH_S, 1, 2))
    else:
        seg = lambda p: (
            jnp.where(p >= PATCH_S, 1, 0)
            + jnp.where(p >= 2 * PATCH_S, 1, 0)
            + jnp.where(p >= 3 * PATCH_S, 1, 0)
        )
    linked = seg(first) == seg(second)
    inside = (first >= lower) & (first < upper)
    return jnp.where(linked & inside, 0.0, NEG)


def kind_regions(kind, toks):
    if kind == 1:
        return ((0, PATCH_L, 0, PATCH_L, False), (PATCH_L, toks - PATCH_L, PATCH_L, toks, True))
    half = 2 * PATCH_S
    size = -(-half // 16) * 16
    begin = toks - size
    return ((0, size, 0, half, True), (begin, size, half, toks, True))


def forward_body(
    experts,
    cap_pad,
    kind_ref,
    x_ref,
    gain_one_ref,
    shift_one_ref,
    wq_ref,
    wk_ref,
    wv_ref,
    wo_ref,
    gain_two_ref,
    shift_two_ref,
    router_ref,
    routes_ref,
    slot_ref,
    qkv_ref,
    mix_ref,
    lse_ref,
    low_ref,
    residual_ref,
    lowered_ref,
    probs_ref,
    send_ref,
    acc_ref,
    out_ref,
    lse_scr,
    kept_ref,
):
    step = pl.program_id(0)
    steps = pl.num_programs(0)
    toks, width = x_ref.shape
    chunk = row_chunk(toks)

    @pl.when(step == 0)
    def _():
        def rows(i, carry):
            spot = pl.ds(pl.multiple_of(i * chunk, 16), chunk)
            scaled, _ = norm_stats(x_ref[spot, :].astype(F32))
            low_ref[spot, :] = (scaled * gain_one_ref[...] + shift_one_ref[...]).astype(BF16)
            return carry

        lax.fori_loop(0, toks // chunk, rows, 0)
        lse_scr[...] = jnp.zeros_like(lse_scr)

    low = low_ref[...]
    qkv_ref[0, :, 0:LANES] = dot_nn(low, wq_ref[...]).astype(BF16)
    qkv_ref[0, :, LANES : 2 * LANES] = dot_nn(low, wk_ref[...]).astype(BF16)
    qkv_ref[0, :, 2 * LANES : 3 * LANES] = dot_nn(low, wv_ref[...]).astype(BF16)

    def attend(kind):
        for start, size, lower, upper, masked in kind_regions(kind, toks):
            bias = region_bias(kind, start, size, lower, upper) if masked else None
            spot = slice(start, start + size)
            out_ref[lower:upper, :] = jnp.zeros((upper - lower, LANES), F32)

            def head(h, carry):
                mine = (iota((1, LANES), 1) // HEAD_DIM) == h
                queries = jnp.where(mine, qkv_ref[0, spot, 0:LANES], 0) * jnp.asarray(SCALE, BF16)
                scores = dot_nt(queries, qkv_ref[0, spot, LANES : 2 * LANES])
                if bias is not None:
                    scores = scores + bias
                top = jnp.max(scores, axis=-1, keepdims=True)
                weights = jnp.exp(scores - top)
                total = jnp.sum(weights, axis=-1, keepdims=True)
                values = jnp.where(mine, qkv_ref[0, spot, 2 * LANES : 3 * LANES], 0)
                mixed = dot_nn(weights.astype(BF16), values) * (1.0 / total)
                logsum = top + jnp.log(total)
                cut = slice(lower - start, upper - start)
                out_ref[lower:upper, :] += mixed[cut]
                lane = iota((upper - lower, 128), 1) == step * GROUP + h
                lse_scr[lower:upper, :] = jnp.where(lane, logsum[cut], lse_scr[lower:upper, :])
                return carry

            lax.fori_loop(0, GROUP, head, 0)

    @pl.when(kind_ref[0] == 1)
    def _():
        attend(1)

    @pl.when(kind_ref[0] != 1)
    def _():
        attend(0)

    mix = out_ref[...].astype(BF16)
    mix_ref[...] = mix
    branch = dot_nn(mix, wo_ref[...])

    @pl.when(step == 0)
    def _():
        acc_ref[...] = x_ref[...].astype(F32) + branch

    @pl.when(step > 0)
    def _():
        acc_ref[...] += branch

    @pl.when(step == steps - 1)
    def _():
        lse_ref[...] = lse_scr[...].T[0 : lse_ref.shape[0], 0:toks]

        def rows(i, carry):
            spot = pl.ds(pl.multiple_of(i * chunk, 16), chunk)
            residual = acc_ref[spot, :]
            residual_ref[spot, :] = residual
            scaled, _ = norm_stats(residual)
            lowered_ref[spot, :] = (scaled * gain_two_ref[...] + shift_two_ref[...]).astype(BF16)
            return carry

        lax.fori_loop(0, toks // chunk, rows, 0)
        lowered = lowered_ref[...]
        logits = dot_nt(router_ref[...], lowered)
        top = jnp.max(logits, axis=0, keepdims=True)
        raised = jnp.exp(logits - top)
        probs = raised / jnp.sum(raised, axis=0, keepdims=True)
        probs_ref[...] = probs
        labels = iota((experts, toks), 0)
        slot_one = slot_ref[0:1, :]
        slot_two = slot_ref[1:2, :]
        gate_one = jnp.sum(jnp.where(labels == routes_ref[0:1, :], probs, 0.0), axis=0, keepdims=True)
        gate_two = jnp.sum(jnp.where(labels == routes_ref[1:2, :], probs, 0.0), axis=0, keepdims=True)
        gate_one = jnp.where(slot_one >= 0, gate_one, 0.0)
        gate_two = jnp.where(slot_two >= 0, gate_two, 0.0)
        which = iota((16, toks), 0)

        def parts(gate):
            high = gate.astype(BF16).astype(F32)
            rest = gate - high
            return jnp.where(which == 0, high, jnp.where(which == 1, rest, 0.0)).astype(BF16)

        kept_ref[0] = parts(gate_one)
        kept_ref[1] = parts(gate_two)
        wide = -(-cap_pad // 128) * 128

        def block(expert, carry):
            spots = iota((wide, toks), 0) + expert * cap_pad
            hot_one = jnp.where(spots == slot_one, 1.0, 0.0)
            hot_two = jnp.where(spots == slot_two, 1.0, 0.0)
            gates = dot_nt(kept_ref[0], hot_one.astype(BF16)) + dot_nt(
                kept_ref[1], hot_two.astype(BF16)
            )
            picked = dot_nn((hot_one + hot_two)[0:cap_pad].astype(BF16), lowered)
            gates = jnp.concatenate([gates, jnp.zeros((16, width - wide), F32)], axis=1)
            row = iota((cap_pad, width), 0)
            picked = jnp.where(
                row == cap_pad - 2, gates[0:1], jnp.where(row == cap_pad - 1, gates[1:2], picked)
            )
            send_ref[expert] = picked.astype(BF16)
            return carry

        lax.fori_loop(0, experts, block, 0)


def phi_parts(v):
    a = jnp.abs(v)
    bell = jnp.exp(-0.5 * (v * v))
    t = 1.0 / (1.0 + PHI_RATE * a)
    poly = PHI_FIT[-1] * t
    for part in PHI_FIT[-2::-1]:
        poly = (poly + part) * t
    tail = poly * bell
    return jnp.where(v > 0, 1.0 - tail, tail), bell


def expert_body(
    x_ref,
    u_ref,
    w_ref,
    bias_ref,
    back_ref,
    z_ref,
    hidden_ref,
    grad_ref,
    g_ref,
    gg_ref,
    bin_ref,
    bback_ref,
    gate_scr,
    acc_scr,
):
    step = pl.program_id(0)
    blocks, cap_pad, width = x_ref.shape
    wide = gg_ref.shape[2]
    tile = w_ref.shape[1]

    @pl.when(step == 0)
    def _():
        bback_ref[...] = jnp.zeros_like(bback_ref)

        def block(b, carry):
            tail = x_ref[b, cap_pad - 16 : cap_pad, 0:wide].astype(F32)
            gate_row = tail[14:15] + tail[15:16]
            same = iota((cap_pad, wide), 0) == iota((cap_pad, wide), 1)
            gate = jnp.sum(jnp.where(same, gate_row, 0.0), axis=1, keepdims=True)
            gate_scr[b] = jnp.broadcast_to(gate, (cap_pad, 128))
            rows = u_ref[b].astype(F32)
            made = (rows * gate).astype(BF16)
            g_ref[b] = made
            bback_ref[0:1, :] += jnp.sum(made.astype(F32), axis=0, keepdims=True)
            part = rows * back_ref[...]
            total = part[:, 0:128]
            for i in range(1, width // 128):
                total = total + part[:, i * 128 : (i + 1) * 128]
            acc_scr[b] = total
            return carry

        lax.fori_loop(0, blocks, block, 0)

    bin_ref[...] = jnp.zeros_like(bin_ref)

    def block(b, carry):
        pre = dot_nn(x_ref[b], w_ref[...]) + bias_ref[...]
        cdf, bell = phi_parts(pre)
        hidden = (pre * cdf).astype(BF16)
        hidden_ref[b] = hidden
        z = z_ref[b].astype(F32)
        part = hidden.astype(F32) * z
        total = acc_scr[b]
        for i in range(tile // 128):
            total = total + part[:, i * 128 : (i + 1) * 128]
        acc_scr[b] = total
        slope = cdf + pre * (bell * INV_ROOT_TAU)
        gate = jnp.concatenate([gate_scr[b]] * (tile // 128), axis=1)
        grad = (gate * z * slope).astype(BF16)
        grad_ref[b] = grad
        bin_ref[0:1, :] += jnp.sum(grad.astype(F32), axis=0, keepdims=True)
        return carry

    lax.fori_loop(0, blocks, block, 0)

    @pl.when(step == pl.num_programs(0) - 1)
    def _():
        def last(b, carry):
            column = jnp.sum(acc_scr[b], axis=1, keepdims=True)
            same = iota((cap_pad, wide), 0) == iota((cap_pad, wide), 1)
            gg_ref[b, 0:1, :] = jnp.sum(jnp.where(same, column, 0.0), axis=0, keepdims=True)
            return carry

        lax.fori_loop(0, blocks, last, 0)


def combine_body(experts, kept_ref, gates_ref, residual_ref, back_ref, result_ref):
    blocks, cap_pad, width = back_ref.shape
    toks = residual_ref.shape[0]
    chunk = row_chunk(toks)
    flat = back_ref[...].reshape(blocks * cap_pad, width)

    def rows(i, carry):
        spot = pl.ds(pl.multiple_of(i * chunk, 16), chunk)
        spots = iota((chunk, blocks * cap_pad), 1)
        hot = jnp.where(spots == kept_ref[spot, 0:1], gates_ref[spot, 0:1], 0.0) + jnp.where(
            spots == kept_ref[spot, 1:2], gates_ref[spot, 1:2], 0.0
        )
        result_ref[spot, :] = (residual_ref[spot, :] + dot_nn(hot.astype(BF16), flat)).astype(BF16)
        return carry

    lax.fori_loop(0, toks // chunk, rows, 0)


def row_grad_body(
    experts,
    col_ref,
    slot_ref,
    routes_ref,
    probs_ref,
    lowered_ref,
    residual_ref,
    cot_ref,
    gain_ref,
    router_ref,
    back_ref,
    grad_ref,
    low_ref,
    small_ref,
    route_grad_ref,
    logit_ref,
):
    blocks, cap_pad, width = back_ref.shape
    toks = lowered_ref.shape[0]
    chunk = row_chunk(toks)
    labels = iota((experts, toks), 0)
    slot_one = slot_ref[0:1, :]
    slot_two = slot_ref[1:2, :]
    wide = -(-cap_pad // 128) * 128
    gate_one = jnp.zeros((16, toks), F32)
    gate_two = jnp.zeros((16, toks), F32)

    def block(expert, carry):
        one, two = carry
        spots = iota((cap_pad, toks), 0) + expert * cap_pad
        tail = back_ref[expert, cap_pad - 16 : cap_pad, 0:cap_pad]
        hot_one = jnp.where(spots == slot_one, 1.0, 0.0).astype(BF16)
        hot_two = jnp.where(spots == slot_two, 1.0, 0.0).astype(BF16)
        return one + dot_nn(tail, hot_one), two + dot_nn(tail, hot_two)

    gate_one, gate_two = lax.fori_loop(0, experts, block, (gate_one, gate_two))
    gate_one = gate_one[14:15] + gate_one[15:16]
    gate_two = gate_two[14:15] + gate_two[15:16]
    probs = probs_ref[...]
    grad_probs = jnp.where(labels == routes_ref[0:1, :], gate_one, 0.0) + jnp.where(
        labels == routes_ref[1:2, :], gate_two, 0.0
    )
    grad_logits = probs * (grad_probs - jnp.sum(probs * grad_probs, axis=0, keepdims=True))
    grad_logits = grad_logits.astype(BF16)
    route_grad_ref[...] = dot_nn(grad_logits, lowered_ref[...])
    logit_ref[...] = dot_tn(grad_logits, router_ref[...])
    small_ref[...] = jnp.zeros_like(small_ref)
    flat = back_ref[...].reshape(blocks * cap_pad, width)

    def rows(i, carry):
        spot = pl.ds(pl.multiple_of(i * chunk, 16), chunk)
        spots = iota((chunk, blocks * cap_pad), 1)
        hot = jnp.where(
            (spots == col_ref[spot, 0:1]) | (spots == col_ref[spot, 1:2]), 1.0, 0.0
        ).astype(BF16)
        grad = logit_ref[spot, :] + dot_nn(hot, flat)
        scaled, inverse = norm_stats(residual_ref[spot, :])
        small_ref[0:1, :] += jnp.sum(grad * scaled, axis=0, keepdims=True)
        small_ref[1:2, :] += jnp.sum(grad, axis=0, keepdims=True)
        total = cot_ref[spot, :].astype(F32) + norm_grad(grad, scaled, inverse, gain_ref[...])
        grad_ref[spot, :] = total
        low_ref[spot, :] = total.astype(BF16)
        return carry

    lax.fori_loop(0, toks // chunk, rows, 0)


def backward_body(
    first_group,
    kind_ref,
    up_ref,
    wo_ref,
    qkv_ref,
    mix_ref,
    lse_ref,
    grad_ref,
    do_ref,
    delta_ref,
    dq_ref,
    dk_ref,
    dv_ref,
):
    toks = up_ref.shape[0]
    group = pl.program_id(0) + first_group
    do = dot_nt(up_ref[...], wo_ref[...]).astype(BF16)
    do_ref[...] = do
    both = do.astype(F32) * mix_ref[...].astype(F32)
    high = both.astype(BF16)
    rest = (both - high.astype(F32)).astype(BF16)
    owner = jnp.where(iota((16, LANES), 1) // HEAD_DIM == iota((16, LANES), 0), 1.0, 0.0).astype(BF16)
    delta_ref[...] = dot_nt(owner, high) + dot_nt(owner, rest)
    dq_ref[...] = jnp.zeros_like(dq_ref)
    dk_ref[...] = jnp.zeros_like(dk_ref)
    dv_ref[...] = jnp.zeros_like(dv_ref)

    def attend(kind):
        for start, size, lower, upper, masked in kind_regions(kind, toks):
            bias = region_bias(kind, start, size, lower, upper) if masked else None
            spot = slice(start, start + size)

            def head(h, carry):
                mine = (iota((1, LANES), 1) // HEAD_DIM) == h
                queries = jnp.where(mine, qkv_ref[0, spot, 0:LANES], 0) * jnp.asarray(SCALE, BF16)
                keys_all = qkv_ref[0, spot, LANES : 2 * LANES]
                own = jnp.where(mine, do_ref[spot, :], 0)
                logsum = lse_ref[pl.ds(group * GROUP + h, 1), :][:, spot]
                delta = delta_ref[pl.ds(h, 1), :][:, spot]
                scores = dot_nt(keys_all, queries)
                if bias is not None:
                    scores = scores + bias
                weights = jnp.exp(scores - logsum)
                grad_weights = dot_nt(qkv_ref[0, spot, 2 * LANES : 3 * LANES], own)
                grad_scores = (weights * (grad_weights - delta)).astype(BF16)
                dv_ref[spot, :] += dot_nn(weights.astype(BF16), own)
                dk_ref[spot, :] += dot_nn(grad_scores, queries)
                dq_ref[spot, :] += dot_tn(grad_scores, jnp.where(mine, keys_all, 0))
                return carry

            lax.fori_loop(0, GROUP, head, 0)

    @pl.when(kind_ref[0] == 1)
    def _():
        attend(1)

    @pl.when(kind_ref[0] != 1)
    def _():
        attend(0)

    grad_ref[:, 0:LANES] = (dq_ref[...] * SCALE).astype(BF16)
    grad_ref[:, LANES : 2 * LANES] = dk_ref[...].astype(BF16)
    grad_ref[:, 2 * LANES : 3 * LANES] = dv_ref[...].astype(BF16)


def final_body(groups, *refs):
    packed = refs[0:groups]
    weights = refs[groups : 2 * groups]
    x_ref, gain_ref, up_ref, out_ref, small_ref, acc_ref = refs[2 * groups :]
    toks = x_ref.shape[0]
    chunk = row_chunk(toks)
    total = dot_nt(packed[0][...], weights[0][...])
    for i in range(1, groups):
        total = total + dot_nt(packed[i][...], weights[i][...])
    acc_ref[...] = total
    small_ref[...] = jnp.zeros_like(small_ref)

    def rows(i, carry):
        spot = pl.ds(pl.multiple_of(i * chunk, 16), chunk)
        grad = acc_ref[spot, :]
        scaled, inverse = norm_stats(x_ref[spot, :].astype(F32))
        small_ref[0:1, :] += jnp.sum(grad * scaled, axis=0, keepdims=True)
        small_ref[1:2, :] += jnp.sum(grad, axis=0, keepdims=True)
        out_ref[spot, :] = (
            up_ref[spot, :] + norm_grad(grad, scaled, inverse, gain_ref[...])
        ).astype(BF16)
        return carry

    lax.fori_loop(0, toks // chunk, rows, 0)


def swap(values, axis, bit, size):
    return lax.ppermute(values, axis, [(j, j ^ bit) for j in range(size)])


def add_pair(a, b):
    return (a.astype(F32) + b.astype(F32)).astype(a.dtype)


def halve(values, axis, bit, size):
    mine = (lax.axis_index(axis) // bit) % 2
    halves = values.reshape((2, values.shape[0] // 2) + values.shape[1:])
    keep = lax.dynamic_index_in_dim(halves, mine, 0, keepdims=False)
    send = lax.dynamic_index_in_dim(halves, 1 - mine, 0, keepdims=False)
    return add_pair(keep, swap(send, axis, bit, size))


def unhalve(values, axis, bit, size):
    mine = (lax.axis_index(axis) // bit) % 2
    other = swap(values, axis, bit, size)
    return jnp.concatenate(
        [jnp.where(mine == 0, values, other), jnp.where(mine == 0, other, values)], axis=0
    )


def axis_bits(axis, size):
    bits = []
    bit = 1
    while bit < size:
        bits.append((axis, bit, size))
        bit *= 2
    return bits


def sum_all(values, sizes):
    inner = axis_bits("ex", sizes["ex"])
    outer = axis_bits("rep", sizes["rep"])
    core, plane = inner[:1], inner[1:]
    shape = values.shape
    if shape[0] % (2 * sizes["ex"] * sizes["rep"]):
        values = values.reshape(-1, 128)
    half = values.shape[0] // 2
    done = []
    for part, order in (
        (values[:half], core + plane + outer),
        (values[half:], core + plane[::-1] + outer),
    ):
        for hop in order:
            part = halve(part, *hop)
        for hop in order[::-1]:
            part = unhalve(part, *hop)
        done.append(part)
    return jnp.concatenate(done, axis=0).reshape(shape)


def sum_small(values, bits):
    for hop in bits:
        values = values + swap(values, *hop)
    return values


def local(
    sizes,
    tokens,
    gain_one,
    shift_one,
    w_qkv,
    w_out,
    gain_two,
    shift_two,
    w_router,
    w_in,
    bias_in,
    w_back,
    bias_back,
    cotangent,
    routes,
    priority,
    image_kind,
):
    toks, width = tokens.shape
    experts = w_router.shape[1]
    hidden_units = w_in.shape[2]
    cap = (42 * toks + 20 * experts - 1) // (20 * experts)
    cap_pad = -(-(cap + 2) // 16) * 16
    wide = -(-cap_pad // 128) * 128
    groups = HEADS // GROUP
    first_w, second_w = w_in[0], w_back[0]
    routes_row = routes.T
    router_row = w_router.T
    sds = jax.ShapeDtypeStruct
    dispatched = (experts, cap_pad, width)

    slots, slot_col, up_rows = call(
        functools.partial(prep_body, experts, cap, cap_pad),
        (sds((8, toks), jnp.int32), sds((toks, 128), jnp.int32), sds(dispatched, BF16)),
        cost=(4e9, 6e6, 0),
        name="prep",
    )(routes_row, priority, cotangent)
    up_in = lax.all_to_all(up_rows, "ex", split_axis=0, concat_axis=0, tiled=True)

    gains = [a.reshape(1, width) for a in (gain_one, shift_one, gain_two, shift_two)]
    col = lambda offset: pl.BlockSpec((width, LANES), lambda g: (0, offset * groups + g))
    smem = pl.BlockSpec(memory_space=pltpu.SMEM)
    per_group = lambda: pl.BlockSpec((1, toks, 3 * LANES), lambda g: (g, 0, 0))
    qkv, mix, logsum, low_one, residual, lowered, probs, sent = call(
        functools.partial(forward_body, experts, cap_pad),
        (
            sds((groups, toks, 3 * LANES), BF16),
            sds((toks, width), BF16),
            sds((16, toks), F32),
            sds((toks, width), BF16),
            sds((toks, width), F32),
            sds((toks, width), BF16),
            sds((experts, toks), F32),
            sds(dispatched, BF16),
        ),
        in_specs=[
            smem,
            whole((toks, width)),
            whole((1, width)),
            whole((1, width)),
            col(0),
            col(1),
            col(2),
            pl.BlockSpec((LANES, width), lambda g: (g, 0)),
            whole((1, width)),
            whole((1, width)),
            whole((experts, width)),
            whole((2, toks)),
            whole((8, toks)),
        ],
        out_specs=[
            per_group(),
            pl.BlockSpec((toks, LANES), lambda g: (0, g)),
            whole((16, toks)),
            whole((toks, width)),
            whole((toks, width)),
            whole((toks, width)),
            whole((experts, toks)),
            whole(dispatched),
        ],
        grid=(groups,),
        scratch=[
            pltpu.VMEM((toks, width), F32),
            pltpu.VMEM((toks, LANES), F32),
            pltpu.VMEM((-(-toks // 128) * 128, 128), F32),
            pltpu.VMEM((2, 16, toks), BF16),
        ],
        cost=(10e9, 20e6, 4e6),
        name="attend",
    )(
        image_kind,
        tokens,
        gains[0],
        gains[1],
        w_qkv,
        w_qkv,
        w_qkv,
        w_out,
        gains[2],
        gains[3],
        router_row,
        routes_row,
        slots,
    )
    rows_in = lax.all_to_all(sent, "ex", split_axis=0, concat_axis=0, tiled=True)

    blocks = rows_in.shape[0]
    flat_up = up_in.reshape(-1, width)
    z = dot_nt(flat_up, second_w).astype(BF16).reshape(blocks, cap_pad, hidden_units)
    tile = 512 if hidden_units % 512 == 0 else 256
    ff = lambda: pl.BlockSpec((blocks, cap_pad, tile), lambda j: (0, 0, j))
    hidden, grad_pre, grad_slots, grad_gate, bin_sum, bback_sum = call(
        expert_body,
        (
            sds((blocks, cap_pad, hidden_units), BF16),
            sds((blocks, cap_pad, hidden_units), BF16),
            sds((blocks, cap_pad, width), BF16),
            sds((blocks, 8, wide), F32),
            sds((8, hidden_units), F32),
            sds((8, width), F32),
        ),
        in_specs=[
            whole((blocks, cap_pad, width)),
            whole((blocks, cap_pad, width)),
            pl.BlockSpec((width, tile), lambda j: (0, j)),
            pl.BlockSpec((1, tile), lambda j: (0, j)),
            whole((1, width)),
            ff(),
        ],
        out_specs=[
            ff(),
            ff(),
            whole((blocks, cap_pad, width)),
            whole((blocks, 8, wide)),
            pl.BlockSpec((8, tile), lambda j: (0, j)),
            whole((8, width)),
        ],
        grid=(hidden_units // tile,),
        scratch=[
            pltpu.VMEM((blocks, cap_pad, 128), F32),
            pltpu.VMEM((blocks, cap_pad, 128), F32),
        ],
        cost=(8e9, 40e6, 10e6),
        name="expert",
    )(rows_in, up_in, first_w, bias_in, bias_back, z)
    flat_rows = rows_in.reshape(-1, width)
    flat_hidden = hidden.reshape(-1, hidden_units)
    flat_pre = grad_pre.reshape(-1, hidden_units)
    flat_slots = grad_slots.reshape(-1, width)

    gate_row = grad_gate[:, 0:1, :]
    gate_high = gate_row.astype(BF16).astype(F32)
    gate_rows = jnp.concatenate([gate_high, gate_row - gate_high], axis=1)
    gate_rows = jnp.pad(gate_rows, ((0, 0), (cap_pad - 2, 0), (0, width - wide)))
    grad_rows = dot_nt(flat_pre, first_w).reshape(blocks, cap_pad, width)
    tail = lax.broadcasted_iota(jnp.int32, (blocks, cap_pad, width), 1) >= cap_pad - 2
    grad_rows = jnp.where(tail, gate_rows, grad_rows).astype(BF16)
    grad_back = lax.all_to_all(grad_rows, "ex", split_axis=0, concat_axis=0, tiled=True)

    second_grad = dot_tn(flat_hidden, flat_slots).astype(BF16)
    second_out = lax.psum_scatter(second_grad, "rep", scatter_dimension=0, tiled=True)
    first_grad = dot_tn(flat_rows, flat_pre).astype(BF16)
    first_out = lax.psum_scatter(first_grad, "rep", scatter_dimension=0, tiled=True)
    produced = (dot_nn(flat_hidden, second_w) + bias_back).astype(BF16)
    returned = lax.all_to_all(
        produced.reshape(blocks, cap_pad, width), "ex", split_axis=0, concat_axis=0, tiled=True
    )

    reps = sizes["rep"]
    bias_sum = sum_small(
        jnp.concatenate([bin_sum[0], bback_sum[0]]).reshape(-1, 128), axis_bits("rep", reps)
    ).reshape(-1)
    rank = lax.axis_index("rep")
    bin_out = lax.dynamic_slice_in_dim(bias_sum, rank * (hidden_units // reps), hidden_units // reps)
    bback_out = lax.dynamic_slice_in_dim(
        bias_sum, hidden_units + rank * (width // reps), width // reps
    )

    grad_residual, grad_branch, small_two, route_grad = call(
        functools.partial(row_grad_body, experts),
        (
            sds((toks, width), F32),
            sds((toks, width), BF16),
            sds((8, width), F32),
            sds((experts, width), F32),
        ),
        scratch=[pltpu.VMEM((toks, width), F32)],
        cost=(5e9, 12e6, 0),
        name="row_grad",
    )(
        slot_col,
        slots,
        routes_row,
        probs,
        lowered,
        residual,
        cotangent,
        gains[2],
        router_row,
        grad_back,
    )
    out_grad = sum_all(dot_tn(mix, grad_branch).astype(BF16), sizes)

    packed_grads = []
    qkv_sums = []
    for g in range(groups):
        packed = call(
            functools.partial(backward_body, g),
            sds((toks, 3 * LANES), BF16),
            in_specs=[
                smem,
                whole((toks, width)),
                pl.BlockSpec((LANES, width), lambda i, g=g: (g, 0)),
                pl.BlockSpec((1, toks, 3 * LANES), lambda i, g=g: (g, 0, 0)),
                pl.BlockSpec((toks, LANES), lambda i, g=g: (0, g)),
                whole((16, toks)),
            ],
            out_specs=whole((toks, 3 * LANES)),
            grid=(1,),
            scratch=[
                pltpu.VMEM((toks, LANES), BF16),
                pltpu.VMEM((16, toks), F32),
                pltpu.VMEM((toks, LANES), F32),
                pltpu.VMEM((toks, LANES), F32),
                pltpu.VMEM((toks, LANES), F32),
            ],
            cost=(8e9, 6e6, 2e6),
            name="attend_back_" + "abcdef"[g],
        )(image_kind, grad_branch, w_out, qkv, mix, logsum)
        packed_grads.append(packed)
        qkv_sums.append(sum_all(dot_tn(low_one, packed).astype(BF16), sizes))

    w_groups = [
        jnp.concatenate(
            [w_qkv[:, (p * groups + g) * LANES : (p * groups + g + 1) * LANES] for p in range(3)],
            axis=1,
        )
        for g in range(groups)
    ]
    grad_tokens, small_one = call(
        functools.partial(final_body, groups),
        (sds((toks, width), BF16), sds((8, width), F32)),
        scratch=[pltpu.VMEM((toks, width), F32)],
        cost=(3e9, 14e6, 0),
        name="final",
    )(*packed_grads, *w_groups, tokens, gains[0], grad_residual)

    gates = jnp.take_along_axis(probs, routes_row, axis=0)
    gates = gates.T
    result = call(
        functools.partial(combine_body, experts),
        sds((toks, width), BF16),
        cost=(2e9, 8e6, 0),
        name="combine",
    )(slot_col, gates, residual, returned)

    everyone = axis_bits("ex", sizes["ex"]) + axis_bits("rep", reps)
    small_two = sum_small(jnp.concatenate([small_two, route_grad], axis=0), everyone)
    small_one = sum_small(small_one, everyone)
    qkv_grad = jnp.concatenate(
        [
            qkv_sums[g][:, p * LANES : (p + 1) * LANES]
            for p in range(3)
            for g in range(groups)
        ],
        axis=1,
    ).astype(F32)
    return (
        result,
        grad_tokens,
        small_one[0],
        small_one[1],
        qkv_grad,
        out_grad.astype(F32),
        small_two[0],
        small_two[1],
        small_two[8:].T,
        first_out.astype(F32)[None],
        bin_out[None],
        second_out.astype(F32)[None],
        bback_out[None],
    )


def solution(mesh):
    both = ("rep", "ex")
    in_specs = (
        P(both, None),
        P(),
        P(),
        P(),
        P(),
        P(),
        P(),
        P(),
        P("ex", None, None),
        P("ex", None),
        P("ex", None, None),
        P("ex", None),
        P(both, None),
        P(both, None),
        P(both, None),
        P(both),
    )
    out_specs = (
        P(both, None),
        P(both, None),
        P(),
        P(),
        P(),
        P(),
        P(),
        P(),
        P(),
        P("ex", "rep", None),
        P("ex", "rep"),
        P("ex", "rep", None),
        P("ex", "rep"),
    )
    return jax.shard_map(
        functools.partial(local, dict(mesh.shape)),
        mesh=mesh,
        in_specs=in_specs,
        out_specs=out_specs,
        check_vma=False,
    )
```

```python
import functools

import jax
import jax.numpy as jnp
from jax import lax
from jax.experimental import pallas as pl
from jax.experimental.pallas import tpu as pltpu
from jax.sharding import PartitionSpec as P

HEADS = 12
HEAD_DIM = 64
PATCH_S = 196
PATCH_L = 576
GROUP = 4
LANES = GROUP * HEAD_DIM

EPS = 1e-06
NEG = -1e30
SCALE = HEAD_DIM ** (-0.5)
LOG2E = 1.4426950408889634
INV_ROOT_TAU = 0.3989422804014327
PHI_RATE = 0.3
PHI_FIT = (
    0.11962929778234231,
    0.1207539739440115,
    0.09991336806177473,
    0.1285620774229096,
    -0.05368457415108751,
    0.20635459820469867,
    -0.1572037608415104,
    0.03567494667893269,
)
F32 = jnp.float32
BF16 = jnp.bfloat16


def dot_nn(a, b):
    return lax.dot_general(a, b, (((1,), (0,)), ((), ())), preferred_element_type=F32)


def dot_nt(a, b):
    return lax.dot_general(a, b, (((1,), (1,)), ((), ())), preferred_element_type=F32)


def dot_tn(a, b):
    return lax.dot_general(a, b, (((0,), (0,)), ((), ())), preferred_element_type=F32)


def iota(shape, dim):
    return lax.broadcasted_iota(jnp.int32, shape, dim)


def call(
    body, out_shape, in_specs=None, out_specs=None, grid=None, scratch=(), cost=None, name=None, after=()
):
    args = dict(out_shape=out_shape, scratch_shapes=list(scratch), name=name)
    if grid is not None:
        args["grid"] = grid
    if out_specs is not None:
        args["out_specs"] = out_specs
    if cost is not None:
        args["cost_estimate"] = pl.CostEstimate(
            flops=int(cost[0]), bytes_accessed=int(cost[1]), transcendentals=int(cost[2])
        )

    def run(*operands):
        count = len(operands)
        specs = in_specs or [pl.BlockSpec(memory_space=pltpu.VMEM)] * count
        specs = list(specs) + [pl.BlockSpec(memory_space=pl.ANY)] * len(after)

        def inner(*refs):
            body(*refs[:count], *refs[count + len(after) :])

        return pl.pallas_call(
            inner,
            in_specs=specs,
            compiler_params=pltpu.CompilerParams(vmem_limit_bytes=60 * 1024 * 1024),
            **args,
        )(*operands, *after)

    return run


def hold(values, after):
    def nothing(*refs):
        pass

    any_spec = pl.BlockSpec(memory_space=pl.ANY)
    return pl.pallas_call(
        nothing,
        out_shape=jax.ShapeDtypeStruct(values.shape, values.dtype),
        in_specs=[any_spec] * (1 + len(after)),
        out_specs=any_spec,
        input_output_aliases={0: 0},
        name="hold",
    )(values, *after)


def whole(shape, memory_space=None):
    zeros = (0,) * len(shape)
    if memory_space is not None:
        return pl.BlockSpec(shape, lambda *_: zeros, memory_space=memory_space)
    return pl.BlockSpec(shape, lambda *_: zeros)


def norm_stats(values):
    average = jnp.mean(values, axis=-1, keepdims=True)
    centered = values - average
    variance = jnp.mean(centered * centered, axis=-1, keepdims=True)
    inverse = lax.rsqrt(variance + EPS)
    return centered * inverse, inverse


def norm_grad(grad, scaled, inverse, gain):
    through = grad * gain
    first = jnp.mean(through, axis=-1, keepdims=True)
    second = jnp.mean(through * scaled, axis=-1, keepdims=True)
    return inverse * (through - first - scaled * second)


def row_chunk(rows):
    for size in (112, 128, 64, 48, 32, 16):
        if rows % size == 0:
            return size
    return rows


def prep_body(experts, cap, cap_pad, routes_ref, prio_ref, cot_ref, slot_ref, col_ref, out_ref):
    toks = cot_ref.shape[0]
    prio = prio_ref[...].astype(F32)
    prio_col = jnp.sum(
        jnp.where(iota((toks, toks), 0) == iota((toks, toks), 1), prio, 0.0), axis=1, keepdims=True
    )
    below = jnp.where(prio_col < prio, 1.0, 0.0).astype(BF16)
    labels = iota((experts, toks), 0)
    first = routes_ref[0:1, :]
    second = routes_ref[1:2, :]
    hot_one = jnp.where(labels == first, 1.0, 0.0)
    hot_two = jnp.where(labels == second, 1.0, 0.0)
    count_one = dot_nn(hot_one.astype(BF16), below)
    count_two = dot_nn(hot_two.astype(BF16), below)
    total_one = jnp.sum(hot_one, axis=1, keepdims=True)
    place_one = jnp.sum(hot_one * count_one, axis=0, keepdims=True)
    place_two = jnp.sum(hot_two * (count_two + total_one), axis=0, keepdims=True)
    slot_one = jnp.where(
        place_one < cap, first * cap_pad + place_one.astype(jnp.int32), -1
    )
    slot_two = jnp.where(
        place_two < cap, second * cap_pad + place_two.astype(jnp.int32), -1
    )
    slot_ref[0:1, :] = slot_one
    slot_ref[1:2, :] = slot_two
    eye = iota((toks, toks), 0) == iota((toks, toks), 1)
    col_one = jnp.sum(jnp.where(eye, slot_one, 0), axis=1, keepdims=True)
    col_two = jnp.sum(jnp.where(eye, slot_two, 0), axis=1, keepdims=True)
    lane = iota((toks, 128), 1)
    col_ref[...] = jnp.where(lane == 0, col_one, jnp.where(lane == 1, col_two, -1))

    def block(expert, carry):
        spots = iota((cap_pad, toks), 0) + expert * cap_pad
        hot = jnp.where((spots == slot_one) | (spots == slot_two), 1.0, 0.0).astype(BF16)
        out_ref[expert] = dot_nn(hot, cot_ref[...]).astype(BF16)
        return carry

    lax.fori_loop(0, experts, block, 0)


def region_bias(kind, start, size, lower, upper, by_rows=True):
    first = iota((size, size), 0) + start
    second = iota((size, size), 1) + start
    if kind == 1:
        seg = lambda p: jnp.where(p < PATCH_L, 0, jnp.where(p < PATCH_L + PATCH_S, 1, 2))
    else:
        seg = lambda p: (
            jnp.where(p >= PATCH_S, 1, 0)
            + jnp.where(p >= 2 * PATCH_S, 1, 0)
            + jnp.where(p >= 3 * PATCH_S, 1, 0)
        )
    linked = seg(first) == seg(second)
    inside = (first >= lower) & (first < upper)
    return jnp.where(linked & inside, 0.0, NEG)


def kind_regions(kind, toks):
    if kind == 1:
        return ((0, PATCH_L, 0, PATCH_L, False), (PATCH_L, toks - PATCH_L, PATCH_L, toks, True))
    half = 2 * PATCH_S
    size = -(-half // 16) * 16
    begin = toks - size
    return ((0, size, 0, half, True), (begin, size, half, toks, True))


def forward_body(
    experts,
    cap_pad,
    kind_ref,
    x_ref,
    gain_one_ref,
    shift_one_ref,
    wq_ref,
    wk_ref,
    wv_ref,
    wo_ref,
    gain_two_ref,
    shift_two_ref,
    router_ref,
    routes_ref,
    slot_ref,
    qkv_ref,
    mix_ref,
    lse_ref,
    low_ref,
    residual_ref,
    lowered_ref,
    probs_ref,
    send_ref,
    acc_ref,
    out_ref,
    lse_scr,
    kept_ref,
):
    step = pl.program_id(0)
    steps = pl.num_programs(0)
    toks, width = x_ref.shape
    chunk = row_chunk(toks)

    @pl.when(step == 0)
    def _():
        def rows(i, carry):
            spot = pl.ds(pl.multiple_of(i * chunk, 16), chunk)
            scaled, _ = norm_stats(x_ref[spot, :].astype(F32))
            low_ref[spot, :] = (scaled * gain_one_ref[...] + shift_one_ref[...]).astype(BF16)
            return carry

        lax.fori_loop(0, toks // chunk, rows, 0)
        lse_scr[...] = jnp.zeros_like(lse_scr)

    low = low_ref[...]
    qkv_ref[0, :, 0:LANES] = dot_nn(low, wq_ref[...]).astype(BF16)
    qkv_ref[0, :, LANES : 2 * LANES] = dot_nn(low, wk_ref[...]).astype(BF16)
    qkv_ref[0, :, 2 * LANES : 3 * LANES] = dot_nn(low, wv_ref[...]).astype(BF16)

    def attend(kind):
        for start, size, lower, upper, masked in kind_regions(kind, toks):
            bias = region_bias(kind, start, size, lower, upper) if masked else None
            spot = slice(start, start + size)
            out_ref[lower:upper, :] = jnp.zeros((upper - lower, LANES), F32)

            def head(h, carry):
                mine = (iota((1, LANES), 1) // HEAD_DIM) == h
                queries = jnp.where(mine, qkv_ref[0, spot, 0:LANES], 0) * jnp.asarray(SCALE, BF16)
                scores = dot_nt(queries, qkv_ref[0, spot, LANES : 2 * LANES])
                if bias is not None:
                    scores = scores + bias
                top = jnp.max(scores, axis=-1, keepdims=True)
                weights = jnp.exp(scores - top)
                total = jnp.sum(weights, axis=-1, keepdims=True)
                values = jnp.where(mine, qkv_ref[0, spot, 2 * LANES : 3 * LANES], 0)
                mixed = dot_nn(weights.astype(BF16), values) * (1.0 / total)
                logsum = top + jnp.log(total)
                cut = slice(lower - start, upper - start)
                out_ref[lower:upper, :] += mixed[cut]
                lane = iota((upper - lower, 128), 1) == step * GROUP + h
                lse_scr[lower:upper, :] = jnp.where(lane, logsum[cut], lse_scr[lower:upper, :])
                return carry

            lax.fori_loop(0, GROUP, head, 0)

    @pl.when(kind_ref[0] == 1)
    def _():
        attend(1)

    @pl.when(kind_ref[0] != 1)
    def _():
        attend(0)

    mix = out_ref[...].astype(BF16)
    mix_ref[...] = mix
    branch = dot_nn(mix, wo_ref[...])

    @pl.when(step == 0)
    def _():
        acc_ref[...] = x_ref[...].astype(F32) + branch

    @pl.when(step > 0)
    def _():
        acc_ref[...] += branch

    @pl.when(step == steps - 1)
    def _():
        lse_ref[...] = lse_scr[...].T[0 : lse_ref.shape[0], 0:toks]

        def rows(i, carry):
            spot = pl.ds(pl.multiple_of(i * chunk, 16), chunk)
            residual = acc_ref[spot, :]
            residual_ref[spot, :] = residual
            scaled, _ = norm_stats(residual)
            lowered_ref[spot, :] = (scaled * gain_two_ref[...] + shift_two_ref[...]).astype(BF16)
            return carry

        lax.fori_loop(0, toks // chunk, rows, 0)
        lowered = lowered_ref[...]
        logits = dot_nt(router_ref[...], lowered)
        top = jnp.max(logits, axis=0, keepdims=True)
        raised = jnp.exp(logits - top)
        probs = raised / jnp.sum(raised, axis=0, keepdims=True)
        probs_ref[...] = probs
        labels = iota((experts, toks), 0)
        slot_one = slot_ref[0:1, :]
        slot_two = slot_ref[1:2, :]
        gate_one = jnp.sum(jnp.where(labels == routes_ref[0:1, :], probs, 0.0), axis=0, keepdims=True)
        gate_two = jnp.sum(jnp.where(labels == routes_ref[1:2, :], probs, 0.0), axis=0, keepdims=True)
        gate_one = jnp.where(slot_one >= 0, gate_one, 0.0)
        gate_two = jnp.where(slot_two >= 0, gate_two, 0.0)
        which = iota((16, toks), 0)

        def parts(gate):
            high = gate.astype(BF16).astype(F32)
            rest = gate - high
            return jnp.where(which == 0, high, jnp.where(which == 1, rest, 0.0)).astype(BF16)

        kept_ref[0] = parts(gate_one)
        kept_ref[1] = parts(gate_two)
        wide = -(-cap_pad // 128) * 128

        def block(expert, carry):
            spots = iota((wide, toks), 0) + expert * cap_pad
            hot_one = jnp.where(spots == slot_one, 1.0, 0.0)
            hot_two = jnp.where(spots == slot_two, 1.0, 0.0)
            gates = dot_nt(kept_ref[0], hot_one.astype(BF16)) + dot_nt(
                kept_ref[1], hot_two.astype(BF16)
            )
            picked = dot_nn((hot_one + hot_two)[0:cap_pad].astype(BF16), lowered)
            gates = jnp.concatenate([gates, jnp.zeros((16, width - wide), F32)], axis=1)
            row = iota((cap_pad, width), 0)
            picked = jnp.where(
                row == cap_pad - 2, gates[0:1], jnp.where(row == cap_pad - 1, gates[1:2], picked)
            )
            send_ref[expert] = picked.astype(BF16)
            return carry

        lax.fori_loop(0, experts, block, 0)


def phi_parts(v):
    a = jnp.abs(v)
    bell = jnp.exp(-0.5 * (v * v))
    t = 1.0 / (1.0 + PHI_RATE * a)
    poly = PHI_FIT[-1] * t
    for part in PHI_FIT[-2::-1]:
        poly = (poly + part) * t
    tail = poly * bell
    return jnp.where(v > 0, 1.0 - tail, tail), bell


def expert_body(
    x_ref,
    u_ref,
    w_ref,
    bias_ref,
    back_ref,
    z_ref,
    hidden_ref,
    grad_ref,
    g_ref,
    gg_ref,
    bin_ref,
    bback_ref,
    gate_scr,
    acc_scr,
):
    step = pl.program_id(0)
    blocks, cap_pad, width = x_ref.shape
    wide = gg_ref.shape[2]
    tile = w_ref.shape[1]

    @pl.when(step == 0)
    def _():
        bback_ref[...] = jnp.zeros_like(bback_ref)

        def block(b, carry):
            tail = x_ref[b, cap_pad - 16 : cap_pad, 0:wide].astype(F32)
            gate_row = tail[14:15] + tail[15:16]
            same = iota((cap_pad, wide), 0) == iota((cap_pad, wide), 1)
            gate = jnp.sum(jnp.where(same, gate_row, 0.0), axis=1, keepdims=True)
            gate_scr[b] = jnp.broadcast_to(gate, (cap_pad, 128))
            rows = u_ref[b].astype(F32)
            made = (rows * gate).astype(BF16)
            g_ref[b] = made
            bback_ref[0:1, :] += jnp.sum(made.astype(F32), axis=0, keepdims=True)
            part = rows * back_ref[...]
            total = part[:, 0:128]
            for i in range(1, width // 128):
                total = total + part[:, i * 128 : (i + 1) * 128]
            acc_scr[b] = total
            return carry

        lax.fori_loop(0, blocks, block, 0)

    bin_ref[...] = jnp.zeros_like(bin_ref)

    def block(b, carry):
        pre = dot_nn(x_ref[b], w_ref[...]) + bias_ref[...]
        cdf, bell = phi_parts(pre)
        hidden = (pre * cdf).astype(BF16)
        hidden_ref[b] = hidden
        z = z_ref[b].astype(F32)
        part = hidden.astype(F32) * z
        total = acc_scr[b]
        for i in range(tile // 128):
            total = total + part[:, i * 128 : (i + 1) * 128]
        acc_scr[b] = total
        slope = cdf + pre * (bell * INV_ROOT_TAU)
        gate = jnp.concatenate([gate_scr[b]] * (tile // 128), axis=1)
        grad = (gate * z * slope).astype(BF16)
        grad_ref[b] = grad
        bin_ref[0:1, :] += jnp.sum(grad.astype(F32), axis=0, keepdims=True)
        return carry

    lax.fori_loop(0, blocks, block, 0)

    @pl.when(step == pl.num_programs(0) - 1)
    def _():
        def last(b, carry):
            column = jnp.sum(acc_scr[b], axis=1, keepdims=True)
            same = iota((cap_pad, wide), 0) == iota((cap_pad, wide), 1)
            gg_ref[b, 0:1, :] = jnp.sum(jnp.where(same, column, 0.0), axis=0, keepdims=True)
            return carry

        lax.fori_loop(0, blocks, last, 0)


def produce_body(hidden_ref, w_ref, bias_ref, out_ref):
    out_ref[...] = (dot_nn(hidden_ref[...], w_ref[...]) + bias_ref[...]).astype(BF16)


def combine_body(
    experts, kept_ref, slot_ref, routes_ref, probs_ref, residual_ref, back_ref, result_ref
):
    blocks, cap_pad, width = back_ref.shape
    toks = residual_ref.shape[0]
    chunk = row_chunk(toks)
    flat = back_ref[...].reshape(blocks * cap_pad, width)
    labels = iota((experts, toks), 0)
    probs = probs_ref[...]

    def gate(k):
        return jnp.sum(jnp.where(labels == routes_ref[k : k + 1, :], probs, 0.0), axis=0, keepdims=True)

    gate_one, gate_two = gate(0), gate(1)

    def columns(i, carry):
        spot = pl.ds(pl.multiple_of(i * chunk, 16), chunk)
        eye = iota((chunk, toks), 0) + i * chunk == iota((chunk, toks), 1)
        col_one = jnp.sum(jnp.where(eye, gate_one, 0.0), axis=1, keepdims=True)
        col_two = jnp.sum(jnp.where(eye, gate_two, 0.0), axis=1, keepdims=True)
        spots = iota((chunk, blocks * cap_pad), 1)
        hot = jnp.where(spots == kept_ref[spot, 0:1], col_one, 0.0) + jnp.where(
            spots == kept_ref[spot, 1:2], col_two, 0.0
        )
        result_ref[spot, :] = (residual_ref[spot, :] + dot_nn(hot.astype(BF16), flat)).astype(BF16)
        return carry

    lax.fori_loop(0, toks // chunk, columns, 0)


def row_grad_body(
    experts,
    col_ref,
    slot_ref,
    routes_ref,
    probs_ref,
    lowered_ref,
    residual_ref,
    cot_ref,
    gain_ref,
    router_ref,
    back_ref,
    grad_ref,
    low_ref,
    small_ref,
    route_grad_ref,
    logit_ref,
):
    blocks, cap_pad, width = back_ref.shape
    toks = lowered_ref.shape[0]
    chunk = row_chunk(toks)
    labels = iota((experts, toks), 0)
    slot_one = slot_ref[0:1, :]
    slot_two = slot_ref[1:2, :]
    wide = -(-cap_pad // 128) * 128
    gate_one = jnp.zeros((16, toks), F32)
    gate_two = jnp.zeros((16, toks), F32)

    def block(expert, carry):
        one, two = carry
        spots = iota((cap_pad, toks), 0) + expert * cap_pad
        tail = back_ref[expert, cap_pad - 16 : cap_pad, 0:cap_pad]
        hot_one = jnp.where(spots == slot_one, 1.0, 0.0).astype(BF16)
        hot_two = jnp.where(spots == slot_two, 1.0, 0.0).astype(BF16)
        return one + dot_nn(tail, hot_one), two + dot_nn(tail, hot_two)

    gate_one, gate_two = lax.fori_loop(0, experts, block, (gate_one, gate_two))
    gate_one = gate_one[14:15] + gate_one[15:16]
    gate_two = gate_two[14:15] + gate_two[15:16]
    probs = probs_ref[...]
    grad_probs = jnp.where(labels == routes_ref[0:1, :], gate_one, 0.0) + jnp.where(
        labels == routes_ref[1:2, :], gate_two, 0.0
    )
    grad_logits = probs * (grad_probs - jnp.sum(probs * grad_probs, axis=0, keepdims=True))
    grad_logits = grad_logits.astype(BF16)
    route_grad_ref[...] = dot_nn(grad_logits, lowered_ref[...])
    logit_ref[...] = dot_tn(grad_logits, router_ref[...])
    small_ref[...] = jnp.zeros_like(small_ref)
    flat = back_ref[...].reshape(blocks * cap_pad, width)

    def rows(i, carry):
        spot = pl.ds(pl.multiple_of(i * chunk, 16), chunk)
        spots = iota((chunk, blocks * cap_pad), 1)
        hot = jnp.where(
            (spots == col_ref[spot, 0:1]) | (spots == col_ref[spot, 1:2]), 1.0, 0.0
        ).astype(BF16)
        grad = logit_ref[spot, :] + dot_nn(hot, flat)
        scaled, inverse = norm_stats(residual_ref[spot, :])
        small_ref[0:1, :] += jnp.sum(grad * scaled, axis=0, keepdims=True)
        small_ref[1:2, :] += jnp.sum(grad, axis=0, keepdims=True)
        total = cot_ref[spot, :].astype(F32) + norm_grad(grad, scaled, inverse, gain_ref[...])
        grad_ref[spot, :] = total
        low_ref[spot, :] = total.astype(BF16)
        return carry

    lax.fori_loop(0, toks // chunk, rows, 0)


def backward_body(
    first_group,
    kind_ref,
    up_ref,
    wo_ref,
    qkv_ref,
    mix_ref,
    lse_ref,
    grad_ref,
    do_ref,
    delta_ref,
    dq_ref,
    dk_ref,
    dv_ref,
):
    toks = up_ref.shape[0]
    group = pl.program_id(0) + first_group
    do = dot_nt(up_ref[...], wo_ref[...]).astype(BF16)
    do_ref[...] = do
    both = do.astype(F32) * mix_ref[...].astype(F32)
    high = both.astype(BF16)
    rest = (both - high.astype(F32)).astype(BF16)
    owner = jnp.where(iota((16, LANES), 1) // HEAD_DIM == iota((16, LANES), 0), 1.0, 0.0).astype(BF16)
    delta_ref[...] = dot_nt(owner, high) + dot_nt(owner, rest)
    dq_ref[...] = jnp.zeros_like(dq_ref)
    dk_ref[...] = jnp.zeros_like(dk_ref)
    dv_ref[...] = jnp.zeros_like(dv_ref)

    def attend(kind):
        for start, size, lower, upper, masked in kind_regions(kind, toks):
            bias = region_bias(kind, start, size, lower, upper) if masked else None
            spot = slice(start, start + size)

            def head(h, carry):
                mine = (iota((1, LANES), 1) // HEAD_DIM) == h
                queries = jnp.where(mine, qkv_ref[0, spot, 0:LANES], 0) * jnp.asarray(SCALE, BF16)
                keys_all = qkv_ref[0, spot, LANES : 2 * LANES]
                own = jnp.where(mine, do_ref[spot, :], 0)
                logsum = lse_ref[pl.ds(group * GROUP + h, 1), :][:, spot]
                delta = delta_ref[pl.ds(h, 1), :][:, spot]
                scores = dot_nt(keys_all, queries)
                if bias is not None:
                    scores = scores + bias
                weights = jnp.exp(scores - logsum)
                grad_weights = dot_nt(qkv_ref[0, spot, 2 * LANES : 3 * LANES], own)
                grad_scores = (weights * (grad_weights - delta)).astype(BF16)
                dv_ref[spot, :] += dot_nn(weights.astype(BF16), own)
                dk_ref[spot, :] += dot_nn(grad_scores, queries)
                dq_ref[spot, :] += dot_tn(grad_scores, jnp.where(mine, keys_all, 0))
                return carry

            lax.fori_loop(0, GROUP, head, 0)

    @pl.when(kind_ref[0] == 1)
    def _():
        attend(1)

    @pl.when(kind_ref[0] != 1)
    def _():
        attend(0)

    grad_ref[:, 0:LANES] = (dq_ref[...] * SCALE).astype(BF16)
    grad_ref[:, LANES : 2 * LANES] = dk_ref[...].astype(BF16)
    grad_ref[:, 2 * LANES : 3 * LANES] = dv_ref[...].astype(BF16)


def final_body(groups, *refs):
    packed = refs[0:groups]
    weights = refs[groups : 2 * groups]
    x_ref, gain_ref, up_ref, out_ref, small_ref, acc_ref = refs[2 * groups :]
    toks = x_ref.shape[0]
    chunk = row_chunk(toks)
    total = dot_nt(packed[0][...], weights[0][...])
    for i in range(1, groups):
        total = total + dot_nt(packed[i][...], weights[i][...])
    acc_ref[...] = total
    small_ref[...] = jnp.zeros_like(small_ref)

    def rows(i, carry):
        spot = pl.ds(pl.multiple_of(i * chunk, 16), chunk)
        grad = acc_ref[spot, :]
        scaled, inverse = norm_stats(x_ref[spot, :].astype(F32))
        small_ref[0:1, :] += jnp.sum(grad * scaled, axis=0, keepdims=True)
        small_ref[1:2, :] += jnp.sum(grad, axis=0, keepdims=True)
        out_ref[spot, :] = (
            up_ref[spot, :] + norm_grad(grad, scaled, inverse, gain_ref[...])
        ).astype(BF16)
        return carry

    lax.fori_loop(0, toks // chunk, rows, 0)


def place_body(core_ref, own_one, other_one, own_two, other_two, out_ref):
    zero = core_ref[0] == 0
    parts = (
        jnp.where(zero, other_one[...], own_one[...]),
        jnp.where(zero, own_two[...], other_two[...]),
        jnp.where(zero, other_two[...], own_two[...]),
    )
    for k, part in enumerate(parts):
        for p in range(3):
            at = (p * 3 + k) * LANES
            out_ref[:, at : at + LANES] = part[:, p * LANES : (p + 1) * LANES].astype(F32)


def place_qkv(pairs, core):
    rows, cols = pairs[0][0].shape
    tile = rows // 3
    return call(
        place_body,
        jax.ShapeDtypeStruct((rows, 3 * cols), F32),
        in_specs=[pl.BlockSpec(memory_space=pltpu.SMEM)]
        + [pl.BlockSpec((tile, cols), lambda i: (i, 0)) for _ in range(4)],
        out_specs=pl.BlockSpec((tile, 3 * cols), lambda i: (i, 0)),
        grid=(3,),
        name="place_qkv",
        cost=(1e6, 20 * rows * cols, 0),
    )(core.astype(jnp.int32).reshape(1), *[part for pair in pairs for part in pair])


def bits_below(count):
    bits, bit = [], 1
    while bit < count:
        bits.append(bit)
        bit *= 2
    return bits


def send_xor(values, axis, size, distance):
    return lax.ppermute(values, axis, [(j, j ^ distance) for j in range(size)])


def trade_sum(parts, axis, size, stride, mine):
    total = lax.dynamic_index_in_dim(parts, mine, 0, keepdims=False).astype(F32)
    for d in range(1, parts.shape[0]):
        sent = lax.dynamic_index_in_dim(parts, mine ^ d, 0, keepdims=False)
        total = total + send_xor(sent, axis, size, d * stride).astype(F32)
    return total.astype(parts.dtype)


def gather_group(values, axis, size, stride, count, mine):
    got = [values] + [send_xor(values, axis, size, d * stride) for d in range(1, count)]
    for bit in bits_below(count):
        flip = (mine & bit) != 0
        got = [jnp.where(flip, got[k ^ bit], got[k]) for k in range(count)]
    return jnp.concatenate(got, axis=0)


class PairSum:
    def __init__(self, first, second, sizes):
        self.width = first.shape[1]
        self.wide, self.reps = sizes["ex"], sizes["rep"]
        place = lax.axis_index("ex")
        self.core, self.chip = place % 2, place // 2
        self.rep = lax.axis_index("rep")
        self.keep = jnp.where(self.core == 0, first, second)
        self.value = jnp.where(self.core == 0, second, first)
        self.stage = 0

    def split(self, values, count):
        return values.reshape(count, -1, self.width)

    def step(self):
        v = self.value
        chips = self.wide // 2
        if self.stage == 0:
            other = send_xor(v, "ex", self.wide, 1)
            v = (self.keep.astype(F32) + other.astype(F32)).astype(v.dtype)
        elif self.stage == 1:
            v = trade_sum(self.split(v, chips), "ex", self.wide, 2, self.chip)
        elif self.stage == 2:
            v = trade_sum(self.split(v, self.reps), "rep", self.reps, 1, self.rep)
        elif self.stage == 3:
            v = gather_group(v, "rep", self.reps, 1, self.reps, self.rep)
        elif self.stage == 4:
            v = gather_group(v, "ex", self.wide, 2, chips, self.chip)
        self.stage += 1
        self.value = v
        return v

    def finish(self):
        while self.stage < 5:
            self.step()
        return self.value, send_xor(self.value, "ex", self.wide, 1)


def sum_small(values, axes):
    for axis, size in axes:
        for bit in bits_below(size):
            values = values + send_xor(values, axis, size, bit)
    return values


def local(
    sizes,
    tokens,
    gain_one,
    shift_one,
    w_qkv,
    w_out,
    gain_two,
    shift_two,
    w_router,
    w_in,
    bias_in,
    w_back,
    bias_back,
    cotangent,
    routes,
    priority,
    image_kind,
):
    toks, width = tokens.shape
    experts = w_router.shape[1]
    hidden_units = w_in.shape[2]
    cap = (42 * toks + 20 * experts - 1) // (20 * experts)
    cap_pad = -(-(cap + 2) // 16) * 16
    wide = -(-cap_pad // 128) * 128
    groups = HEADS // GROUP
    first_w, second_w = w_in[0], w_back[0]
    routes_row = routes.T
    router_row = w_router.T
    sds = jax.ShapeDtypeStruct
    dispatched = (experts, cap_pad, width)

    slots, slot_col, up_rows = call(
        functools.partial(prep_body, experts, cap, cap_pad),
        (sds((8, toks), jnp.int32), sds((toks, 128), jnp.int32), sds(dispatched, BF16)),
        cost=(4e9, 6e6, 0),
        name="prep",
    )(routes_row, priority, cotangent)
    up_in = lax.all_to_all(up_rows, "ex", split_axis=0, concat_axis=0, tiled=True)

    gains = [a.reshape(1, width) for a in (gain_one, shift_one, gain_two, shift_two)]
    col = lambda offset: pl.BlockSpec((width, LANES), lambda g: (0, offset * groups + g))
    smem = pl.BlockSpec(memory_space=pltpu.SMEM)
    per_group = lambda: pl.BlockSpec((1, toks, 3 * LANES), lambda g: (g, 0, 0))
    qkv, mix, logsum, low_one, residual, lowered, probs, sent = call(
        functools.partial(forward_body, experts, cap_pad),
        (
            sds((groups, toks, 3 * LANES), BF16),
            sds((toks, width), BF16),
            sds((16, toks), F32),
            sds((toks, width), BF16),
            sds((toks, width), F32),
            sds((toks, width), BF16),
            sds((experts, toks), F32),
            sds(dispatched, BF16),
        ),
        in_specs=[
            smem,
            whole((toks, width)),
            whole((1, width)),
            whole((1, width)),
            col(0),
            col(1),
            col(2),
            pl.BlockSpec((LANES, width), lambda g: (g, 0)),
            whole((1, width)),
            whole((1, width)),
            whole((experts, width)),
            whole((2, toks)),
            whole((8, toks)),
        ],
        out_specs=[
            per_group(),
            pl.BlockSpec((toks, LANES), lambda g: (0, g)),
            whole((16, toks)),
            whole((toks, width)),
            whole((toks, width)),
            whole((toks, width)),
            whole((experts, toks)),
            whole(dispatched),
        ],
        grid=(groups,),
        scratch=[
            pltpu.VMEM((toks, width), F32),
            pltpu.VMEM((toks, LANES), F32),
            pltpu.VMEM((-(-toks // 128) * 128, 128), F32),
            pltpu.VMEM((2, 16, toks), BF16),
        ],
        cost=(10e9, 20e6, 4e6),
        name="attend",
    )(
        image_kind,
        tokens,
        gains[0],
        gains[1],
        w_qkv,
        w_qkv,
        w_qkv,
        w_out,
        gains[2],
        gains[3],
        router_row,
        routes_row,
        slots,
    )
    rows_in = lax.all_to_all(sent, "ex", split_axis=0, concat_axis=0, tiled=True)

    blocks = rows_in.shape[0]
    flat_up = up_in.reshape(-1, width)
    z = dot_nt(flat_up, second_w).astype(BF16).reshape(blocks, cap_pad, hidden_units)
    tile = 512 if hidden_units % 512 == 0 else 256
    ff = lambda: pl.BlockSpec((blocks, cap_pad, tile), lambda j: (0, 0, j))
    hidden, grad_pre, grad_slots, grad_gate, bin_sum, bback_sum = call(
        expert_body,
        (
            sds((blocks, cap_pad, hidden_units), BF16),
            sds((blocks, cap_pad, hidden_units), BF16),
            sds((blocks, cap_pad, width), BF16),
            sds((blocks, 8, wide), F32),
            sds((8, hidden_units), F32),
            sds((8, width), F32),
        ),
        in_specs=[
            whole((blocks, cap_pad, width)),
            whole((blocks, cap_pad, width)),
            pl.BlockSpec((width, tile), lambda j: (0, j)),
            pl.BlockSpec((1, tile), lambda j: (0, j)),
            whole((1, width)),
            ff(),
        ],
        out_specs=[
            ff(),
            ff(),
            whole((blocks, cap_pad, width)),
            whole((blocks, 8, wide)),
            pl.BlockSpec((8, tile), lambda j: (0, j)),
            whole((8, width)),
        ],
        grid=(hidden_units // tile,),
        scratch=[
            pltpu.VMEM((blocks, cap_pad, 128), F32),
            pltpu.VMEM((blocks, cap_pad, 128), F32),
        ],
        cost=(8e9, 40e6, 10e6),
        name="expert",
    )(rows_in, up_in, first_w, bias_in, bias_back, z)
    flat_rows = rows_in.reshape(-1, width)
    flat_hidden = hidden.reshape(-1, hidden_units)
    flat_pre = grad_pre.reshape(-1, hidden_units)
    flat_slots = grad_slots.reshape(-1, width)

    gate_row = grad_gate[:, 0:1, :]
    gate_high = gate_row.astype(BF16).astype(F32)
    gate_rows = jnp.concatenate([gate_high, gate_row - gate_high], axis=1)
    gate_rows = jnp.pad(gate_rows, ((0, 0), (cap_pad - 2, 0), (0, width - wide)))
    first_grad = dot_tn(flat_rows, flat_pre).astype(BF16)
    first_out = lax.psum_scatter(first_grad, "rep", scatter_dimension=0, tiled=True).astype(F32)
    flat_pre = hold(flat_pre, [first_grad])
    grad_rows = dot_nt(flat_pre, first_w).reshape(blocks, cap_pad, width)
    tail = lax.broadcasted_iota(jnp.int32, (blocks, cap_pad, width), 1) >= cap_pad - 2
    grad_rows = jnp.where(tail, gate_rows, grad_rows).astype(BF16)
    grad_back = lax.all_to_all(grad_rows, "ex", split_axis=0, concat_axis=0, tiled=True)

    flat_slots = hold(flat_slots, [first_grad, grad_rows])
    second_grad = dot_tn(flat_hidden, flat_slots).astype(BF16)
    second_out = lax.psum_scatter(second_grad, "rep", scatter_dimension=0, tiled=True).astype(F32)
    flat_hidden = hold(flat_hidden, [second_grad])
    tall = blocks * cap_pad // 4
    produced = call(
        produce_body,
        sds((blocks * cap_pad, width), BF16),
        in_specs=[
            pl.BlockSpec((tall, hidden_units), lambda i: (i, 0)),
            whole((hidden_units, width)),
            whole((1, width)),
        ],
        out_specs=pl.BlockSpec((tall, width), lambda i: (i, 0)),
        grid=(4,),
        cost=(1, 1, 0),
        name="produce",
    )(flat_hidden, second_w, bias_back)
    returned = lax.all_to_all(
        produced.reshape(blocks, cap_pad, width), "ex", split_axis=0, concat_axis=0, tiled=True
    )

    reps = sizes["rep"]
    bias_sum = sum_small(
        jnp.concatenate([bin_sum[0], bback_sum[0]]).reshape(-1, 128), [("rep", reps)]
    ).reshape(-1)
    rank = lax.axis_index("rep")
    bin_out = lax.dynamic_slice_in_dim(bias_sum, rank * (hidden_units // reps), hidden_units // reps)
    bback_out = lax.dynamic_slice_in_dim(
        bias_sum, hidden_units + rank * (width // reps), width // reps
    )

    grad_residual, grad_branch, small_two, route_grad = call(
        functools.partial(row_grad_body, experts),
        (
            sds((toks, width), F32),
            sds((toks, width), BF16),
            sds((8, width), F32),
            sds((experts, width), F32),
        ),
        scratch=[pltpu.VMEM((toks, width), F32)],
        cost=(1, 1, 0),
        name="row_grad",
        after=[first_grad, second_grad, produced],
    )(
        slot_col,
        slots,
        routes_row,
        probs,
        lowered,
        residual,
        cotangent,
        gains[2],
        router_row,
        grad_back,
    )
    out_part = dot_tn(mix, grad_branch).astype(BF16)
    sums = []

    def advance():
        return [s.step() for s in sums]

    packed_grads = []
    parts = [out_part]
    waiting = [out_part]
    for g in range(groups):
        if g == 1:
            waiting.append(returned)
        packed = call(
            functools.partial(backward_body, g),
            sds((toks, 3 * LANES), BF16),
            in_specs=[
                smem,
                whole((toks, width)),
                pl.BlockSpec((LANES, width), lambda i, g=g: (g, 0)),
                pl.BlockSpec((1, toks, 3 * LANES), lambda i, g=g: (g, 0, 0)),
                pl.BlockSpec((toks, LANES), lambda i, g=g: (0, g)),
                whole((16, toks)),
            ],
            out_specs=whole((toks, 3 * LANES)),
            grid=(1,),
            scratch=[
                pltpu.VMEM((toks, LANES), BF16),
                pltpu.VMEM((16, toks), F32),
                pltpu.VMEM((toks, LANES), F32),
                pltpu.VMEM((toks, LANES), F32),
                pltpu.VMEM((toks, LANES), F32),
            ],
            cost=(1, 1, 0),
            name="attend_back_" + "abcdef"[g],
            after=waiting,
        )(image_kind, grad_branch, w_out, qkv, mix, logsum)
        packed_grads.append(packed)
        waiting = advance()
        parts.append(dot_tn(low_one, packed).astype(BF16))
        if len(parts) == 2:
            sums.append(PairSum(*parts, sizes))
            parts = []
            waiting.append(sums[-1].value)
        else:
            waiting.append(parts[-1])

    w_groups = [
        jnp.concatenate(
            [w_qkv[:, (p * groups + g) * LANES : (p * groups + g + 1) * LANES] for p in range(3)],
            axis=1,
        )
        for g in range(groups)
    ]
    grad_tokens, small_one = call(
        functools.partial(final_body, groups),
        (sds((toks, width), BF16), sds((8, width), F32)),
        scratch=[pltpu.VMEM((toks, width), F32)],
        cost=(1, 1, 0),
        name="final",
        after=waiting,
    )(*packed_grads, *w_groups, tokens, gains[0], grad_residual)
    last = sums[1]

    result = call(
        functools.partial(combine_body, experts),
        sds((toks, width), BF16),
        cost=(1, 1, 0),
        name="combine",
        after=[last.step()],
    )(slot_col, slots, routes_row, probs, residual, returned)
    last.step()
    last.value = hold(last.value, [result])
    last.step()
    last.step()

    small = sum_small(
        jnp.concatenate([small_one[0:2], small_two[0:2], route_grad], axis=0),
        [("ex", sizes["ex"]), ("rep", reps)],
    )
    pairs = [s.finish() for s in sums]
    core = lax.axis_index("ex") % 2
    out_grad = jnp.where(core == 0, *pairs[0]).astype(F32)
    qkv_grad = place_qkv(pairs, core)
    return (
        result,
        grad_tokens,
        small[0],
        small[1],
        qkv_grad,
        out_grad,
        small[2],
        small[3],
        small[4:].T,
        first_out[None],
        bin_out[None],
        second_out[None],
        bback_out[None],
    )


def solution(mesh):
    both = ("rep", "ex")
    in_specs = (
        P(both, None),
        P(),
        P(),
        P(),
        P(),
        P(),
        P(),
        P(),
        P("ex", None, None),
        P("ex", None),
        P("ex", None, None),
        P("ex", None),
        P(both, None),
        P(both, None),
        P(both, None),
        P(both),
    )
    out_specs = (
        P(both, None),
        P(both, None),
        P(),
        P(),
        P(),
        P(),
        P(),
        P(),
        P(),
        P("ex", "rep", None),
        P("ex", "rep"),
        P("ex", "rep", None),
        P("ex", "rep"),
    )
    return jax.shard_map(
        functools.partial(local, dict(mesh.shape)),
        mesh=mesh,
        in_specs=in_specs,
        out_specs=out_specs,
        check_vma=False,
    )
```

```python
import functools

import jax
import jax.numpy as jnp
from jax import lax
from jax.experimental import pallas as pl
from jax.experimental.pallas import tpu as pltpu
from jax.sharding import PartitionSpec as P

HEADS = 12
HEAD_DIM = 64
PATCH_S = 196
PATCH_L = 576
GROUP = 4
LANES = GROUP * HEAD_DIM

EPS = 1e-06
NEG = -1e30
SCALE = HEAD_DIM ** (-0.5)
LOG2E = 1.4426950408889634
INV_ROOT_TAU = 0.3989422804014327
PHI_RATE = 0.3
PHI_FIT = (
    0.11962929778234231,
    0.1207539739440115,
    0.09991336806177473,
    0.1285620774229096,
    -0.05368457415108751,
    0.20635459820469867,
    -0.1572037608415104,
    0.03567494667893269,
)
F32 = jnp.float32
BF16 = jnp.bfloat16


def dot_nn(a, b):
    return lax.dot_general(a, b, (((1,), (0,)), ((), ())), preferred_element_type=F32)


def dot_nt(a, b):
    return lax.dot_general(a, b, (((1,), (1,)), ((), ())), preferred_element_type=F32)


def dot_tn(a, b):
    return lax.dot_general(a, b, (((0,), (0,)), ((), ())), preferred_element_type=F32)


def iota(shape, dim):
    return lax.broadcasted_iota(jnp.int32, shape, dim)


def call(
    body, out_shape, in_specs=None, out_specs=None, grid=None, scratch=(), cost=None, name=None, after=()
):
    args = dict(out_shape=out_shape, scratch_shapes=list(scratch), name=name)
    if grid is not None:
        args["grid"] = grid
    if out_specs is not None:
        args["out_specs"] = out_specs
    if cost is not None:
        args["cost_estimate"] = pl.CostEstimate(
            flops=int(cost[0]), bytes_accessed=int(cost[1]), transcendentals=int(cost[2])
        )

    def run(*operands):
        count = len(operands)
        specs = in_specs or [pl.BlockSpec(memory_space=pltpu.VMEM)] * count
        specs = list(specs) + [pl.BlockSpec(memory_space=pl.ANY)] * len(after)

        def inner(*refs):
            body(*refs[:count], *refs[count + len(after) :])

        return pl.pallas_call(
            inner,
            in_specs=specs,
            compiler_params=pltpu.CompilerParams(vmem_limit_bytes=60 * 1024 * 1024),
            **args,
        )(*operands, *after)

    return run


def hold(values, after):
    def nothing(*refs):
        pass

    any_spec = pl.BlockSpec(memory_space=pl.ANY)
    return pl.pallas_call(
        nothing,
        out_shape=jax.ShapeDtypeStruct(values.shape, values.dtype),
        in_specs=[any_spec] * (1 + len(after)),
        out_specs=any_spec,
        input_output_aliases={0: 0},
        name="hold",
    )(values, *after)


def whole(shape, memory_space=None):
    zeros = (0,) * len(shape)
    if memory_space is not None:
        return pl.BlockSpec(shape, lambda *_: zeros, memory_space=memory_space)
    return pl.BlockSpec(shape, lambda *_: zeros)


def norm_stats(values):
    average = jnp.mean(values, axis=-1, keepdims=True)
    centered = values - average
    variance = jnp.mean(centered * centered, axis=-1, keepdims=True)
    inverse = lax.rsqrt(variance + EPS)
    return centered * inverse, inverse


def norm_grad(grad, scaled, inverse, gain):
    through = grad * gain
    first = jnp.mean(through, axis=-1, keepdims=True)
    second = jnp.mean(through * scaled, axis=-1, keepdims=True)
    return inverse * (through - first - scaled * second)


def row_chunk(rows):
    for size in (112, 128, 64, 48, 32, 16):
        if rows % size == 0:
            return size
    return rows


def prep_body(experts, cap, cap_pad, routes_ref, prio_ref, cot_ref, slot_ref, col_ref, out_ref):
    toks = cot_ref.shape[0]
    prio = prio_ref[...].astype(F32)
    prio_col = jnp.sum(
        jnp.where(iota((toks, toks), 0) == iota((toks, toks), 1), prio, 0.0), axis=1, keepdims=True
    )
    below = jnp.where(prio_col < prio, 1.0, 0.0).astype(BF16)
    labels = iota((experts, toks), 0)
    first = routes_ref[0:1, :]
    second = routes_ref[1:2, :]
    hot_one = jnp.where(labels == first, 1.0, 0.0)
    hot_two = jnp.where(labels == second, 1.0, 0.0)
    count_one = dot_nn(hot_one.astype(BF16), below)
    count_two = dot_nn(hot_two.astype(BF16), below)
    total_one = jnp.sum(hot_one, axis=1, keepdims=True)
    place_one = jnp.sum(hot_one * count_one, axis=0, keepdims=True)
    place_two = jnp.sum(hot_two * (count_two + total_one), axis=0, keepdims=True)
    slot_one = jnp.where(
        place_one < cap, first * cap_pad + place_one.astype(jnp.int32), -1
    )
    slot_two = jnp.where(
        place_two < cap, second * cap_pad + place_two.astype(jnp.int32), -1
    )
    slot_ref[0:1, :] = slot_one
    slot_ref[1:2, :] = slot_two
    eye = iota((toks, toks), 0) == iota((toks, toks), 1)
    col_one = jnp.sum(jnp.where(eye, slot_one, 0), axis=1, keepdims=True)
    col_two = jnp.sum(jnp.where(eye, slot_two, 0), axis=1, keepdims=True)
    lane = iota((toks, 128), 1)
    col_ref[...] = jnp.where(lane == 0, col_one, jnp.where(lane == 1, col_two, -1))

    def block(expert, carry):
        spots = iota((cap_pad, toks), 0) + expert * cap_pad
        hot = jnp.where((spots == slot_one) | (spots == slot_two), 1.0, 0.0).astype(BF16)
        out_ref[expert] = dot_nn(hot, cot_ref[...]).astype(BF16)
        return carry

    lax.fori_loop(0, experts, block, 0)


def region_bias(kind, start, size, lower, upper, by_rows=True):
    first = iota((size, size), 0) + start
    second = iota((size, size), 1) + start
    if kind == 1:
        seg = lambda p: jnp.where(p < PATCH_L, 0, jnp.where(p < PATCH_L + PATCH_S, 1, 2))
    else:
        seg = lambda p: (
            jnp.where(p >= PATCH_S, 1, 0)
            + jnp.where(p >= 2 * PATCH_S, 1, 0)
            + jnp.where(p >= 3 * PATCH_S, 1, 0)
        )
    linked = seg(first) == seg(second)
    inside = (first >= lower) & (first < upper)
    return jnp.where(linked & inside, 0.0, NEG)


def kind_regions(kind, toks):
    if kind == 1:
        return ((0, PATCH_L, 0, PATCH_L, False), (PATCH_L, toks - PATCH_L, PATCH_L, toks, True))
    half = 2 * PATCH_S
    size = -(-half // 16) * 16
    begin = toks - size
    return ((0, size, 0, half, True), (begin, size, half, toks, True))


def forward_body(
    experts,
    cap_pad,
    kind_ref,
    x_ref,
    gain_one_ref,
    shift_one_ref,
    wq_ref,
    wk_ref,
    wv_ref,
    wo_ref,
    gain_two_ref,
    shift_two_ref,
    router_ref,
    routes_ref,
    slot_ref,
    qkv_ref,
    mix_ref,
    lse_ref,
    low_ref,
    residual_ref,
    lowered_ref,
    probs_ref,
    send_ref,
    acc_ref,
    out_ref,
    lse_scr,
    kept_ref,
):
    step = pl.program_id(0)
    steps = pl.num_programs(0)
    toks, width = x_ref.shape
    chunk = row_chunk(toks)

    @pl.when(step == 0)
    def _():
        def rows(i, carry):
            spot = pl.ds(pl.multiple_of(i * chunk, 16), chunk)
            scaled, _ = norm_stats(x_ref[spot, :].astype(F32))
            low_ref[spot, :] = (scaled * gain_one_ref[...] + shift_one_ref[...]).astype(BF16)
            return carry

        lax.fori_loop(0, toks // chunk, rows, 0)
        lse_scr[...] = jnp.zeros_like(lse_scr)

    low = low_ref[...]
    qkv_ref[0, :, 0:LANES] = dot_nn(low, wq_ref[...]).astype(BF16)
    qkv_ref[0, :, LANES : 2 * LANES] = dot_nn(low, wk_ref[...]).astype(BF16)
    qkv_ref[0, :, 2 * LANES : 3 * LANES] = dot_nn(low, wv_ref[...]).astype(BF16)

    def attend(kind):
        for start, size, lower, upper, masked in kind_regions(kind, toks):
            bias = region_bias(kind, start, size, lower, upper) if masked else None
            spot = slice(start, start + size)
            out_ref[lower:upper, :] = jnp.zeros((upper - lower, LANES), F32)

            def head(h, carry):
                mine = (iota((1, LANES), 1) // HEAD_DIM) == h
                queries = jnp.where(mine, qkv_ref[0, spot, 0:LANES], 0) * jnp.asarray(SCALE, BF16)
                scores = dot_nt(queries, qkv_ref[0, spot, LANES : 2 * LANES])
                if bias is not None:
                    scores = scores + bias
                top = jnp.max(scores, axis=-1, keepdims=True)
                weights = jnp.exp(scores - top)
                total = jnp.sum(weights, axis=-1, keepdims=True)
                values = jnp.where(mine, qkv_ref[0, spot, 2 * LANES : 3 * LANES], 0)
                mixed = dot_nn(weights.astype(BF16), values) * (1.0 / total)
                logsum = top + jnp.log(total)
                cut = slice(lower - start, upper - start)
                out_ref[lower:upper, :] += mixed[cut]
                lane = iota((upper - lower, 128), 1) == step * GROUP + h
                lse_scr[lower:upper, :] = jnp.where(lane, logsum[cut], lse_scr[lower:upper, :])
                return carry

            lax.fori_loop(0, GROUP, head, 0)

    @pl.when(kind_ref[0] == 1)
    def _():
        attend(1)

    @pl.when(kind_ref[0] != 1)
    def _():
        attend(0)

    mix = out_ref[...].astype(BF16)
    mix_ref[...] = mix
    branch = dot_nn(mix, wo_ref[...])

    @pl.when(step == 0)
    def _():
        acc_ref[...] = x_ref[...].astype(F32) + branch

    @pl.when(step > 0)
    def _():
        acc_ref[...] += branch

    @pl.when(step == steps - 1)
    def _():
        lse_ref[...] = lse_scr[...].T[0 : lse_ref.shape[0], 0:toks]

        def rows(i, carry):
            spot = pl.ds(pl.multiple_of(i * chunk, 16), chunk)
            residual = acc_ref[spot, :]
            residual_ref[spot, :] = residual
            scaled, _ = norm_stats(residual)
            lowered_ref[spot, :] = (scaled * gain_two_ref[...] + shift_two_ref[...]).astype(BF16)
            return carry

        lax.fori_loop(0, toks // chunk, rows, 0)
        lowered = lowered_ref[...]
        logits = dot_nt(router_ref[...], lowered)
        top = jnp.max(logits, axis=0, keepdims=True)
        raised = jnp.exp(logits - top)
        probs = raised / jnp.sum(raised, axis=0, keepdims=True)
        probs_ref[...] = probs
        labels = iota((experts, toks), 0)
        slot_one = slot_ref[0:1, :]
        slot_two = slot_ref[1:2, :]
        gate_one = jnp.sum(jnp.where(labels == routes_ref[0:1, :], probs, 0.0), axis=0, keepdims=True)
        gate_two = jnp.sum(jnp.where(labels == routes_ref[1:2, :], probs, 0.0), axis=0, keepdims=True)
        gate_one = jnp.where(slot_one >= 0, gate_one, 0.0)
        gate_two = jnp.where(slot_two >= 0, gate_two, 0.0)
        which = iota((16, toks), 0)

        def parts(gate):
            high = gate.astype(BF16).astype(F32)
            rest = gate - high
            return jnp.where(which == 0, high, jnp.where(which == 1, rest, 0.0)).astype(BF16)

        kept_ref[0] = parts(gate_one)
        kept_ref[1] = parts(gate_two)
        wide = -(-cap_pad // 128) * 128

        def block(expert, carry):
            spots = iota((wide, toks), 0) + expert * cap_pad
            hot_one = jnp.where(spots == slot_one, 1.0, 0.0)
            hot_two = jnp.where(spots == slot_two, 1.0, 0.0)
            gates = dot_nt(kept_ref[0], hot_one.astype(BF16)) + dot_nt(
                kept_ref[1], hot_two.astype(BF16)
            )
            picked = dot_nn((hot_one + hot_two)[0:cap_pad].astype(BF16), lowered)
            gates = jnp.concatenate([gates, jnp.zeros((16, width - wide), F32)], axis=1)
            row = iota((cap_pad, width), 0)
            picked = jnp.where(
                row == cap_pad - 2, gates[0:1], jnp.where(row == cap_pad - 1, gates[1:2], picked)
            )
            send_ref[expert] = picked.astype(BF16)
            return carry

        lax.fori_loop(0, experts, block, 0)


def phi_parts(v):
    a = jnp.abs(v)
    bell = jnp.exp(-0.5 * (v * v))
    t = 1.0 / (1.0 + PHI_RATE * a)
    poly = PHI_FIT[-1] * t
    for part in PHI_FIT[-2::-1]:
        poly = (poly + part) * t
    tail = poly * bell
    return jnp.where(v > 0, 1.0 - tail, tail), bell


def expert_body(
    x_ref,
    u_ref,
    w_ref,
    bias_ref,
    back_ref,
    z_ref,
    hidden_ref,
    grad_ref,
    g_ref,
    gg_ref,
    bin_ref,
    bback_ref,
    gate_scr,
    acc_scr,
):
    step = pl.program_id(0)
    blocks, cap_pad, width = x_ref.shape
    wide = gg_ref.shape[2]
    tile = w_ref.shape[1]

    @pl.when(step == 0)
    def _():
        bback_ref[...] = jnp.zeros_like(bback_ref)

        def block(b, carry):
            tail = x_ref[b, cap_pad - 16 : cap_pad, 0:wide].astype(F32)
            gate_row = tail[14:15] + tail[15:16]
            same = iota((cap_pad, wide), 0) == iota((cap_pad, wide), 1)
            gate = jnp.sum(jnp.where(same, gate_row, 0.0), axis=1, keepdims=True)
            gate_scr[b] = jnp.broadcast_to(gate, (cap_pad, 128))
            rows = u_ref[b].astype(F32)
            made = (rows * gate).astype(BF16)
            g_ref[b] = made
            bback_ref[0:1, :] += jnp.sum(made.astype(F32), axis=0, keepdims=True)
            part = rows * back_ref[...]
            total = part[:, 0:128]
            for i in range(1, width // 128):
                total = total + part[:, i * 128 : (i + 1) * 128]
            acc_scr[b] = total
            return carry

        lax.fori_loop(0, blocks, block, 0)

    bin_ref[...] = jnp.zeros_like(bin_ref)

    def block(b, carry):
        pre = dot_nn(x_ref[b], w_ref[...]) + bias_ref[...]
        cdf, bell = phi_parts(pre)
        hidden = (pre * cdf).astype(BF16)
        hidden_ref[b] = hidden
        z = z_ref[b].astype(F32)
        part = hidden.astype(F32) * z
        total = acc_scr[b]
        for i in range(tile // 128):
            total = total + part[:, i * 128 : (i + 1) * 128]
        acc_scr[b] = total
        slope = cdf + pre * (bell * INV_ROOT_TAU)
        gate = jnp.concatenate([gate_scr[b]] * (tile // 128), axis=1)
        grad = (gate * z * slope).astype(BF16)
        grad_ref[b] = grad
        bin_ref[0:1, :] += jnp.sum(grad.astype(F32), axis=0, keepdims=True)
        return carry

    lax.fori_loop(0, blocks, block, 0)

    @pl.when(step == pl.num_programs(0) - 1)
    def _():
        def last(b, carry):
            column = jnp.sum(acc_scr[b], axis=1, keepdims=True)
            same = iota((cap_pad, wide), 0) == iota((cap_pad, wide), 1)
            gg_ref[b, 0:1, :] = jnp.sum(jnp.where(same, column, 0.0), axis=0, keepdims=True)
            return carry

        lax.fori_loop(0, blocks, last, 0)


def produce_body(hidden_ref, w_ref, bias_ref, out_ref):
    out_ref[...] = (dot_nn(hidden_ref[...], w_ref[...]) + bias_ref[...]).astype(BF16)


def combine_body(
    experts, kept_ref, slot_ref, routes_ref, probs_ref, residual_ref, back_ref, result_ref
):
    blocks, cap_pad, width = back_ref.shape
    toks = residual_ref.shape[0]
    chunk = row_chunk(toks)
    flat = back_ref[...].reshape(blocks * cap_pad, width)
    labels = iota((experts, toks), 0)
    probs = probs_ref[...]

    def gate(k):
        return jnp.sum(jnp.where(labels == routes_ref[k : k + 1, :], probs, 0.0), axis=0, keepdims=True)

    gate_one, gate_two = gate(0), gate(1)

    def columns(i, carry):
        spot = pl.ds(pl.multiple_of(i * chunk, 16), chunk)
        eye = iota((chunk, toks), 0) + i * chunk == iota((chunk, toks), 1)
        col_one = jnp.sum(jnp.where(eye, gate_one, 0.0), axis=1, keepdims=True)
        col_two = jnp.sum(jnp.where(eye, gate_two, 0.0), axis=1, keepdims=True)
        spots = iota((chunk, blocks * cap_pad), 1)
        hot = jnp.where(spots == kept_ref[spot, 0:1], col_one, 0.0) + jnp.where(
            spots == kept_ref[spot, 1:2], col_two, 0.0
        )
        result_ref[spot, :] = (residual_ref[spot, :] + dot_nn(hot.astype(BF16), flat)).astype(BF16)
        return carry

    lax.fori_loop(0, toks // chunk, columns, 0)


def row_grad_body(
    experts,
    col_ref,
    slot_ref,
    routes_ref,
    probs_ref,
    lowered_ref,
    residual_ref,
    cot_ref,
    gain_ref,
    router_ref,
    back_ref,
    grad_ref,
    low_ref,
    small_ref,
    route_grad_ref,
    logit_ref,
):
    blocks, cap_pad, width = back_ref.shape
    toks = lowered_ref.shape[0]
    chunk = row_chunk(toks)
    labels = iota((experts, toks), 0)
    slot_one = slot_ref[0:1, :]
    slot_two = slot_ref[1:2, :]
    wide = -(-cap_pad // 128) * 128
    gate_one = jnp.zeros((16, toks), F32)
    gate_two = jnp.zeros((16, toks), F32)

    def block(expert, carry):
        one, two = carry
        spots = iota((cap_pad, toks), 0) + expert * cap_pad
        tail = back_ref[expert, cap_pad - 16 : cap_pad, 0:cap_pad]
        hot_one = jnp.where(spots == slot_one, 1.0, 0.0).astype(BF16)
        hot_two = jnp.where(spots == slot_two, 1.0, 0.0).astype(BF16)
        return one + dot_nn(tail, hot_one), two + dot_nn(tail, hot_two)

    gate_one, gate_two = lax.fori_loop(0, experts, block, (gate_one, gate_two))
    gate_one = gate_one[14:15] + gate_one[15:16]
    gate_two = gate_two[14:15] + gate_two[15:16]
    probs = probs_ref[...]
    grad_probs = jnp.where(labels == routes_ref[0:1, :], gate_one, 0.0) + jnp.where(
        labels == routes_ref[1:2, :], gate_two, 0.0
    )
    grad_logits = probs * (grad_probs - jnp.sum(probs * grad_probs, axis=0, keepdims=True))
    grad_logits = grad_logits.astype(BF16)
    route_grad_ref[...] = dot_nn(grad_logits, lowered_ref[...])
    logit_ref[...] = dot_tn(grad_logits, router_ref[...])
    small_ref[...] = jnp.zeros_like(small_ref)
    flat = back_ref[...].reshape(blocks * cap_pad, width)

    def rows(i, carry):
        spot = pl.ds(pl.multiple_of(i * chunk, 16), chunk)
        spots = iota((chunk, blocks * cap_pad), 1)
        hot = jnp.where(
            (spots == col_ref[spot, 0:1]) | (spots == col_ref[spot, 1:2]), 1.0, 0.0
        ).astype(BF16)
        grad = logit_ref[spot, :] + dot_nn(hot, flat)
        scaled, inverse = norm_stats(residual_ref[spot, :])
        small_ref[0:1, :] += jnp.sum(grad * scaled, axis=0, keepdims=True)
        small_ref[1:2, :] += jnp.sum(grad, axis=0, keepdims=True)
        total = cot_ref[spot, :].astype(F32) + norm_grad(grad, scaled, inverse, gain_ref[...])
        grad_ref[spot, :] = total
        low_ref[spot, :] = total.astype(BF16)
        return carry

    lax.fori_loop(0, toks // chunk, rows, 0)


def backward_body(
    first_group,
    kind_ref,
    up_ref,
    wo_ref,
    qkv_ref,
    mix_ref,
    lse_ref,
    grad_ref,
    do_ref,
    delta_ref,
    dq_ref,
    dk_ref,
    dv_ref,
):
    toks = up_ref.shape[0]
    group = pl.program_id(0) + first_group
    do = dot_nt(up_ref[...], wo_ref[...]).astype(BF16)
    do_ref[...] = do
    both = do.astype(F32) * mix_ref[...].astype(F32)
    high = both.astype(BF16)
    rest = (both - high.astype(F32)).astype(BF16)
    owner = jnp.where(iota((16, LANES), 1) // HEAD_DIM == iota((16, LANES), 0), 1.0, 0.0).astype(BF16)
    delta_ref[...] = dot_nt(owner, high) + dot_nt(owner, rest)
    dq_ref[...] = jnp.zeros_like(dq_ref)
    dk_ref[...] = jnp.zeros_like(dk_ref)
    dv_ref[...] = jnp.zeros_like(dv_ref)

    def attend(kind):
        for start, size, lower, upper, masked in kind_regions(kind, toks):
            bias = region_bias(kind, start, size, lower, upper) if masked else None
            spot = slice(start, start + size)

            def head(h, carry):
                mine = (iota((1, LANES), 1) // HEAD_DIM) == h
                queries = jnp.where(mine, qkv_ref[0, spot, 0:LANES], 0) * jnp.asarray(SCALE, BF16)
                keys_all = qkv_ref[0, spot, LANES : 2 * LANES]
                own = jnp.where(mine, do_ref[spot, :], 0)
                logsum = lse_ref[pl.ds(group * GROUP + h, 1), :][:, spot]
                delta = delta_ref[pl.ds(h, 1), :][:, spot]
                scores = dot_nt(keys_all, queries)
                if bias is not None:
                    scores = scores + bias
                weights = jnp.exp(scores - logsum)
                grad_weights = dot_nt(qkv_ref[0, spot, 2 * LANES : 3 * LANES], own)
                grad_scores = (weights * (grad_weights - delta)).astype(BF16)
                dv_ref[spot, :] += dot_nn(weights.astype(BF16), own)
                dk_ref[spot, :] += dot_nn(grad_scores, queries)
                dq_ref[spot, :] += dot_tn(grad_scores, jnp.where(mine, keys_all, 0))
                return carry

            lax.fori_loop(0, GROUP, head, 0)

    @pl.when(kind_ref[0] == 1)
    def _():
        attend(1)

    @pl.when(kind_ref[0] != 1)
    def _():
        attend(0)

    grad_ref[:, 0:LANES] = (dq_ref[...] * SCALE).astype(BF16)
    grad_ref[:, LANES : 2 * LANES] = dk_ref[...].astype(BF16)
    grad_ref[:, 2 * LANES : 3 * LANES] = dv_ref[...].astype(BF16)


def final_body(groups, *refs):
    packed = refs[0:groups]
    weights = refs[groups : 2 * groups]
    x_ref, gain_ref, up_ref, out_ref, small_ref, acc_ref = refs[2 * groups :]
    toks = x_ref.shape[0]
    chunk = row_chunk(toks)
    total = dot_nt(packed[0][...], weights[0][...])
    for i in range(1, groups):
        total = total + dot_nt(packed[i][...], weights[i][...])
    acc_ref[...] = total
    small_ref[...] = jnp.zeros_like(small_ref)

    def rows(i, carry):
        spot = pl.ds(pl.multiple_of(i * chunk, 16), chunk)
        grad = acc_ref[spot, :]
        scaled, inverse = norm_stats(x_ref[spot, :].astype(F32))
        small_ref[0:1, :] += jnp.sum(grad * scaled, axis=0, keepdims=True)
        small_ref[1:2, :] += jnp.sum(grad, axis=0, keepdims=True)
        out_ref[spot, :] = (
            up_ref[spot, :] + norm_grad(grad, scaled, inverse, gain_ref[...])
        ).astype(BF16)
        return carry

    lax.fori_loop(0, toks // chunk, rows, 0)


def place_body(core_ref, own_one, other_one, own_two, other_two, out_ref):
    zero = core_ref[0] == 0
    parts = (
        jnp.where(zero, other_one[...], own_one[...]),
        jnp.where(zero, own_two[...], other_two[...]),
        jnp.where(zero, other_two[...], own_two[...]),
    )
    for k, part in enumerate(parts):
        for p in range(3):
            at = (p * 3 + k) * LANES
            out_ref[:, at : at + LANES] = part[:, p * LANES : (p + 1) * LANES].astype(F32)


def place_qkv(pairs, core):
    rows, cols = pairs[0][0].shape
    tile = rows // 3
    return call(
        place_body,
        jax.ShapeDtypeStruct((rows, 3 * cols), F32),
        in_specs=[pl.BlockSpec(memory_space=pltpu.SMEM)]
        + [pl.BlockSpec((tile, cols), lambda i: (i, 0)) for _ in range(4)],
        out_specs=pl.BlockSpec((tile, 3 * cols), lambda i: (i, 0)),
        grid=(3,),
        name="place_qkv",
        cost=(1e6, 20 * rows * cols, 0),
    )(core.astype(jnp.int32).reshape(1), *[part for pair in pairs for part in pair])


def bits_below(count):
    bits, bit = [], 1
    while bit < count:
        bits.append(bit)
        bit *= 2
    return bits


def send_xor(values, axis, size, distance):
    return lax.ppermute(values, axis, [(j, j ^ distance) for j in range(size)])


def trade_sum(parts, axis, size, stride, mine, extra, after):
    def pick(place):
        part = lax.dynamic_index_in_dim(parts, place, 0, keepdims=False)
        return part if extra is None else jnp.concatenate([part, extra], axis=0)

    own = pick(mine)
    if after:
        own = hold(own, after)
    total = own.astype(F32)
    for d in range(1, parts.shape[0]):
        total = total + send_xor(pick(mine ^ d), axis, size, d * stride).astype(F32)
    return total.astype(parts.dtype)


def gather_group(values, axis, size, stride, count, mine):
    got = [values] + [send_xor(values, axis, size, d * stride) for d in range(1, count)]
    for bit in bits_below(count):
        flip = (mine & bit) != 0
        got = [jnp.where(flip, got[k ^ bit], got[k]) for k in range(count)]
    return jnp.concatenate(got, axis=0)


class PairSum:
    def __init__(self, first, second, wide, plan):
        self.width = first.shape[1]
        self.wide = wide
        self.plan = plan
        self.core = lax.axis_index("ex") % 2
        self.keep = jnp.where(self.core == 0, first, second)
        self.value = jnp.where(self.core == 0, second, first)
        self.extra = None
        self.stage = 0

    def step(self, after=()):
        v = self.value
        deep = len(self.plan)
        if self.stage == 0:
            other = send_xor(v, "ex", self.wide, 1)
            keep = hold(self.keep, after) if after else self.keep
            v = (keep.astype(F32) + other.astype(F32)).astype(v.dtype)
        elif self.stage <= deep:
            axis, size, stride, count = self.plan[self.stage - 1]
            mine = (lax.axis_index(axis) // stride) % count
            parts = v.reshape(count, -1, self.width)
            v = trade_sum(parts, axis, size, stride, mine, self.extra, after)
            if self.extra is not None:
                rows = parts.shape[1]
                self.extra = v[rows:]
                v = v[:rows]
        else:
            axis, size, stride, count = self.plan[2 * deep - self.stage]
            mine = (lax.axis_index(axis) // stride) % count
            v = gather_group(v, axis, size, stride, count, mine)
            if after:
                v = hold(v, after)
        self.stage += 1
        self.value = v
        return v

    def left(self):
        return 2 * len(self.plan) + 1 - self.stage

    def finish(self):
        while self.left():
            self.step()
        return self.value, send_xor(self.value, "ex", self.wide, 1)


def local(
    sizes,
    tokens,
    gain_one,
    shift_one,
    w_qkv,
    w_out,
    gain_two,
    shift_two,
    w_router,
    w_in,
    bias_in,
    w_back,
    bias_back,
    cotangent,
    routes,
    priority,
    image_kind,
):
    toks, width = tokens.shape
    experts = w_router.shape[1]
    hidden_units = w_in.shape[2]
    cap = (42 * toks + 20 * experts - 1) // (20 * experts)
    cap_pad = -(-(cap + 2) // 16) * 16
    wide = -(-cap_pad // 128) * 128
    groups = HEADS // GROUP
    first_w, second_w = w_in[0], w_back[0]
    routes_row = routes.T
    router_row = w_router.T
    sds = jax.ShapeDtypeStruct
    dispatched = (experts, cap_pad, width)

    slots, slot_col, up_rows = call(
        functools.partial(prep_body, experts, cap, cap_pad),
        (sds((8, toks), jnp.int32), sds((toks, 128), jnp.int32), sds(dispatched, BF16)),
        cost=(4e9, 6e6, 0),
        name="prep",
    )(routes_row, priority, cotangent)
    up_in = lax.all_to_all(up_rows, "ex", split_axis=0, concat_axis=0, tiled=True)

    gains = [a.reshape(1, width) for a in (gain_one, shift_one, gain_two, shift_two)]
    col = lambda offset: pl.BlockSpec((width, LANES), lambda g: (0, offset * groups + g))
    smem = pl.BlockSpec(memory_space=pltpu.SMEM)
    per_group = lambda: pl.BlockSpec((1, toks, 3 * LANES), lambda g: (g, 0, 0))
    qkv, mix, logsum, low_one, residual, lowered, probs, sent = call(
        functools.partial(forward_body, experts, cap_pad),
        (
            sds((groups, toks, 3 * LANES), BF16),
            sds((toks, width), BF16),
            sds((16, toks), F32),
            sds((toks, width), BF16),
            sds((toks, width), F32),
            sds((toks, width), BF16),
            sds((experts, toks), F32),
            sds(dispatched, BF16),
        ),
        in_specs=[
            smem,
            whole((toks, width)),
            whole((1, width)),
            whole((1, width)),
            col(0),
            col(1),
            col(2),
            pl.BlockSpec((LANES, width), lambda g: (g, 0)),
            whole((1, width)),
            whole((1, width)),
            whole((experts, width)),
            whole((2, toks)),
            whole((8, toks)),
        ],
        out_specs=[
            per_group(),
            pl.BlockSpec((toks, LANES), lambda g: (0, g)),
            whole((16, toks)),
            whole((toks, width)),
            whole((toks, width)),
            whole((toks, width)),
            whole((experts, toks)),
            whole(dispatched),
        ],
        grid=(groups,),
        scratch=[
            pltpu.VMEM((toks, width), F32),
            pltpu.VMEM((toks, LANES), F32),
            pltpu.VMEM((-(-toks // 128) * 128, 128), F32),
            pltpu.VMEM((2, 16, toks), BF16),
        ],
        cost=(10e9, 20e6, 4e6),
        name="attend",
    )(
        image_kind,
        tokens,
        gains[0],
        gains[1],
        w_qkv,
        w_qkv,
        w_qkv,
        w_out,
        gains[2],
        gains[3],
        router_row,
        routes_row,
        slots,
    )
    rows_in = lax.all_to_all(sent, "ex", split_axis=0, concat_axis=0, tiled=True)

    blocks = rows_in.shape[0]
    flat_up = up_in.reshape(-1, width)
    z = dot_nt(flat_up, second_w).astype(BF16).reshape(blocks, cap_pad, hidden_units)
    tile = 512 if hidden_units % 512 == 0 else 256
    ff = lambda: pl.BlockSpec((blocks, cap_pad, tile), lambda j: (0, 0, j))
    hidden, grad_pre, grad_slots, grad_gate, bin_sum, bback_sum = call(
        expert_body,
        (
            sds((blocks, cap_pad, hidden_units), BF16),
            sds((blocks, cap_pad, hidden_units), BF16),
            sds((blocks, cap_pad, width), BF16),
            sds((blocks, 8, wide), F32),
            sds((8, hidden_units), F32),
            sds((8, width), F32),
        ),
        in_specs=[
            whole((blocks, cap_pad, width)),
            whole((blocks, cap_pad, width)),
            pl.BlockSpec((width, tile), lambda j: (0, j)),
            pl.BlockSpec((1, tile), lambda j: (0, j)),
            whole((1, width)),
            ff(),
        ],
        out_specs=[
            ff(),
            ff(),
            whole((blocks, cap_pad, width)),
            whole((blocks, 8, wide)),
            pl.BlockSpec((8, tile), lambda j: (0, j)),
            whole((8, width)),
        ],
        grid=(hidden_units // tile,),
        scratch=[
            pltpu.VMEM((blocks, cap_pad, 128), F32),
            pltpu.VMEM((blocks, cap_pad, 128), F32),
        ],
        cost=(8e9, 40e6, 10e6),
        name="expert",
    )(rows_in, up_in, first_w, bias_in, bias_back, z)
    flat_rows = rows_in.reshape(-1, width)
    flat_hidden = hidden.reshape(-1, hidden_units)
    flat_pre = grad_pre.reshape(-1, hidden_units)
    flat_slots = grad_slots.reshape(-1, width)

    gate_row = grad_gate[:, 0:1, :]
    gate_high = gate_row.astype(BF16).astype(F32)
    gate_rows = jnp.concatenate([gate_high, gate_row - gate_high], axis=1)
    gate_rows = jnp.pad(gate_rows, ((0, 0), (cap_pad - 2, 0), (0, width - wide)))
    first_grad = dot_tn(flat_rows, flat_pre).astype(BF16)
    first_out = lax.psum_scatter(first_grad, "rep", scatter_dimension=0, tiled=True).astype(F32)
    flat_pre = hold(flat_pre, [first_grad])
    grad_rows = dot_nt(flat_pre, first_w).reshape(blocks, cap_pad, width)
    tail = lax.broadcasted_iota(jnp.int32, (blocks, cap_pad, width), 1) >= cap_pad - 2
    grad_rows = jnp.where(tail, gate_rows, grad_rows).astype(BF16)
    grad_back = lax.all_to_all(grad_rows, "ex", split_axis=0, concat_axis=0, tiled=True)

    flat_slots = hold(flat_slots, [first_grad, grad_rows])
    second_grad = dot_tn(flat_hidden, flat_slots).astype(BF16)
    second_out = lax.psum_scatter(second_grad, "rep", scatter_dimension=0, tiled=True).astype(F32)
    flat_hidden = hold(flat_hidden, [second_grad])
    tall = blocks * cap_pad // 4
    produced = call(
        produce_body,
        sds((blocks * cap_pad, width), BF16),
        in_specs=[
            pl.BlockSpec((tall, hidden_units), lambda i: (i, 0)),
            whole((hidden_units, width)),
            whole((1, width)),
        ],
        out_specs=pl.BlockSpec((tall, width), lambda i: (i, 0)),
        grid=(4,),
        cost=(1, 1, 0),
        name="produce",
    )(flat_hidden, second_w, bias_back)
    returned = lax.all_to_all(
        produced.reshape(blocks, cap_pad, width), "ex", split_axis=0, concat_axis=0, tiled=True
    )

    reps = sizes["rep"]
    grad_residual, grad_branch, small_two, route_grad = call(
        functools.partial(row_grad_body, experts),
        (
            sds((toks, width), F32),
            sds((toks, width), BF16),
            sds((8, width), F32),
            sds((experts, width), F32),
        ),
        scratch=[pltpu.VMEM((toks, width), F32)],
        cost=(1, 1, 0),
        name="row_grad",
        after=[first_grad, second_grad, produced],
    )(
        slot_col,
        slots,
        routes_row,
        probs,
        lowered,
        residual,
        cotangent,
        gains[2],
        router_row,
        grad_back,
    )
    out_part = dot_tn(mix, grad_branch).astype(BF16)
    sums = []

    def advance():
        return [s.step() for s in sums]

    reps = sizes["rep"]
    plane_hops = [("ex", sizes["ex"], bit, 2) for bit in bits_below(sizes["ex"])[1:]]
    rep_hops = [("rep", reps, bit, 2) for bit in bits_below(reps)]
    packed_grads = []
    parts = [out_part]
    waiting = [out_part]
    for g in range(groups):
        if g == 1:
            waiting.append(returned)
        packed = call(
            functools.partial(backward_body, g),
            sds((toks, 3 * LANES), BF16),
            in_specs=[
                smem,
                whole((toks, width)),
                pl.BlockSpec((LANES, width), lambda i, g=g: (g, 0)),
                pl.BlockSpec((1, toks, 3 * LANES), lambda i, g=g: (g, 0, 0)),
                pl.BlockSpec((toks, LANES), lambda i, g=g: (0, g)),
                whole((16, toks)),
            ],
            out_specs=whole((toks, 3 * LANES)),
            grid=(1,),
            scratch=[
                pltpu.VMEM((toks, LANES), BF16),
                pltpu.VMEM((16, toks), F32),
                pltpu.VMEM((toks, LANES), F32),
                pltpu.VMEM((toks, LANES), F32),
                pltpu.VMEM((toks, LANES), F32),
            ],
            cost=(8e9, 6e6, 2e6),
            name="attend_back_" + "abcdef"[g],
            after=waiting,
        )(image_kind, grad_branch, w_out, qkv, mix, logsum)
        packed_grads.append(packed)
        waiting = advance()
        parts.append(dot_tn(low_one, packed).astype(BF16))
        if len(parts) == 2:
            order = plane_hops[:: 1 if g == 0 else -1]
            sums.append(PairSum(*parts, sizes["ex"], order + rep_hops))
            parts = []
            waiting.append(sums[-1].value)
        else:
            waiting.append(parts[-1])

    w_groups = [
        jnp.concatenate(
            [w_qkv[:, (p * groups + g) * LANES : (p * groups + g + 1) * LANES] for p in range(3)],
            axis=1,
        )
        for g in range(groups)
    ]
    grad_tokens, small_one = call(
        functools.partial(final_body, groups),
        (sds((toks, width), BF16), sds((8, width), F32)),
        scratch=[pltpu.VMEM((toks, width), F32)],
        cost=(3e9, 14e6, 0),
        name="final",
        after=[sums[1].value],
    )(*packed_grads, *w_groups, tokens, gains[0], grad_residual)
    ahead, last = sums
    small = jnp.concatenate([small_one[0:2], small_two[0:2], route_grad], axis=0)
    small_rows = small.shape[0]
    added = last.step([small_one])
    last.extra = jnp.pad(small, ((0, -small_rows % 16), (0, 0))).astype(BF16)
    result = call(
        functools.partial(combine_body, experts),
        sds((toks, width), BF16),
        cost=(2e9, 8e6, 0),
        name="combine",
        after=[added, ahead.value, first_out],
    )(slot_col, slots, routes_row, probs, residual, returned)
    ahead.step([result])
    last.step([result])
    bin_sum = hold(bin_sum, [result])
    while ahead.stage < len(plane_hops) + 1:
        ahead.step()
        last.step()
    bias_rows = jnp.concatenate([bin_sum[0].reshape(-1, width), bback_sum[0:1]], axis=0)
    bias_rows = jnp.pad(bias_rows, ((0, -bias_rows.shape[0] % 16), (0, 0))).astype(BF16)
    ahead.extra = bias_rows
    while last.left() > 1:
        if ahead.left():
            ahead.step([second_out] if ahead.left() == 1 else ())
        last.step()
    last.step()
    pairs = [ahead.finish(), last.finish()]
    rank = lax.axis_index("rep")
    bias_sum = ahead.extra.astype(F32)
    bin_out = bias_sum[: hidden_units // width].reshape(-1)
    bin_out = lax.dynamic_slice_in_dim(bin_out, rank * (hidden_units // reps), hidden_units // reps)
    bback_out = lax.dynamic_slice_in_dim(
        bias_sum[hidden_units // width], rank * (width // reps), width // reps
    )
    small = last.extra.astype(F32)
    small = small + send_xor(small, "ex", sizes["ex"], 1)
    core = lax.axis_index("ex") % 2
    out_grad = jnp.where(core == 0, *pairs[0]).astype(F32)
    qkv_grad = place_qkv(pairs, core)
    return (
        result,
        grad_tokens,
        small[0],
        small[1],
        qkv_grad,
        out_grad,
        small[2],
        small[3],
        small[4:small_rows].T,
        first_out[None],
        bin_out[None],
        second_out[None],
        bback_out[None],
    )


def solution(mesh):
    both = ("rep", "ex")
    in_specs = (
        P(both, None),
        P(),
        P(),
        P(),
        P(),
        P(),
        P(),
        P(),
        P("ex", None, None),
        P("ex", None),
        P("ex", None, None),
        P("ex", None),
        P(both, None),
        P(both, None),
        P(both, None),
        P(both),
    )
    out_specs = (
        P(both, None),
        P(both, None),
        P(),
        P(),
        P(),
        P(),
        P(),
        P(),
        P(),
        P("ex", "rep", None),
        P("ex", "rep"),
        P("ex", "rep", None),
        P("ex", "rep"),
    )
    return jax.shard_map(
        functools.partial(local, dict(mesh.shape)),
        mesh=mesh,
        in_specs=in_specs,
        out_specs=out_specs,
        check_vma=False,
    )
```

```python
import functools

import jax
import jax.numpy as jnp
from jax import lax
from jax.experimental import pallas as pl
from jax.experimental.pallas import tpu as pltpu
from jax.sharding import PartitionSpec as P

HEADS = 12
HEAD_DIM = 64
PATCH_S = 196
PATCH_L = 576
GROUP = 4
LANES = GROUP * HEAD_DIM

EPS = 1e-06
NEG = -1e30
SCALE = HEAD_DIM ** (-0.5)
LOG2E = 1.4426950408889634
INV_ROOT_TAU = 0.3989422804014327
PHI_RATE = 0.36
PHI_FIT = (
    0.14371304535439455,
    0.14177245494035942,
    0.1397192591115954,
    0.026549327576509053,
    0.18095403137785818,
    -0.17976471959279186,
    0.047056297922502474,
)
F32 = jnp.float32
BF16 = jnp.bfloat16


def dot_nn(a, b):
    return lax.dot_general(a, b, (((1,), (0,)), ((), ())), preferred_element_type=F32)


def dot_nt(a, b):
    return lax.dot_general(a, b, (((1,), (1,)), ((), ())), preferred_element_type=F32)


def dot_tn(a, b):
    return lax.dot_general(a, b, (((0,), (0,)), ((), ())), preferred_element_type=F32)


def iota(shape, dim):
    return lax.broadcasted_iota(jnp.int32, shape, dim)


def call(
    body, out_shape, in_specs=None, out_specs=None, grid=None, scratch=(), cost=None, name=None, after=()
):
    args = dict(out_shape=out_shape, scratch_shapes=list(scratch), name=name)
    if grid is not None:
        args["grid"] = grid
    if out_specs is not None:
        args["out_specs"] = out_specs
    if cost is not None:
        args["cost_estimate"] = pl.CostEstimate(
            flops=int(cost[0]), bytes_accessed=int(cost[1]), transcendentals=int(cost[2])
        )

    def run(*operands):
        count = len(operands)
        specs = in_specs or [pl.BlockSpec(memory_space=pltpu.VMEM)] * count
        specs = list(specs) + [pl.BlockSpec(memory_space=pl.ANY)] * len(after)

        def inner(*refs):
            body(*refs[:count], *refs[count + len(after) :])

        return pl.pallas_call(
            inner,
            in_specs=specs,
            compiler_params=pltpu.CompilerParams(vmem_limit_bytes=60 * 1024 * 1024),
            **args,
        )(*operands, *after)

    return run


def hold(values, after):
    def nothing(*refs):
        pass

    any_spec = pl.BlockSpec(memory_space=pl.ANY)
    return pl.pallas_call(
        nothing,
        out_shape=jax.ShapeDtypeStruct(values.shape, values.dtype),
        in_specs=[any_spec] * (1 + len(after)),
        out_specs=any_spec,
        input_output_aliases={0: 0},
        name="hold",
    )(values, *after)


def whole(shape, memory_space=None):
    zeros = (0,) * len(shape)
    if memory_space is not None:
        return pl.BlockSpec(shape, lambda *_: zeros, memory_space=memory_space)
    return pl.BlockSpec(shape, lambda *_: zeros)


def norm_stats(values):
    average = jnp.mean(values, axis=-1, keepdims=True)
    centered = values - average
    variance = jnp.mean(centered * centered, axis=-1, keepdims=True)
    inverse = lax.rsqrt(variance + EPS)
    return centered * inverse, inverse


def norm_grad(grad, scaled, inverse, gain):
    through = grad * gain
    first = jnp.mean(through, axis=-1, keepdims=True)
    second = jnp.mean(through * scaled, axis=-1, keepdims=True)
    return inverse * (through - first - scaled * second)


def row_chunk(rows):
    for size in (112, 128, 64, 48, 32, 16):
        if rows % size == 0:
            return size
    return rows


def prep_body(experts, cap, cap_pad, routes_ref, prio_ref, cot_ref, slot_ref, col_ref, out_ref):
    toks = cot_ref.shape[0]
    prio = prio_ref[...].astype(F32)
    prio_col = jnp.sum(
        jnp.where(iota((toks, toks), 0) == iota((toks, toks), 1), prio, 0.0), axis=1, keepdims=True
    )
    below = jnp.where(prio_col < prio, 1.0, 0.0).astype(BF16)
    labels = iota((experts, toks), 0)
    first = routes_ref[0:1, :]
    second = routes_ref[1:2, :]
    hot_one = jnp.where(labels == first, 1.0, 0.0)
    hot_two = jnp.where(labels == second, 1.0, 0.0)
    count_one = dot_nn(hot_one.astype(BF16), below)
    count_two = dot_nn(hot_two.astype(BF16), below)
    total_one = jnp.sum(hot_one, axis=1, keepdims=True)
    place_one = jnp.sum(hot_one * count_one, axis=0, keepdims=True)
    place_two = jnp.sum(hot_two * (count_two + total_one), axis=0, keepdims=True)
    slot_one = jnp.where(
        place_one < cap, first * cap_pad + place_one.astype(jnp.int32), -1
    )
    slot_two = jnp.where(
        place_two < cap, second * cap_pad + place_two.astype(jnp.int32), -1
    )
    slot_ref[0:1, :] = slot_one
    slot_ref[1:2, :] = slot_two
    eye = iota((toks, toks), 0) == iota((toks, toks), 1)
    col_one = jnp.sum(jnp.where(eye, slot_one, 0), axis=1, keepdims=True)
    col_two = jnp.sum(jnp.where(eye, slot_two, 0), axis=1, keepdims=True)
    lane = iota((toks, 128), 1)
    col_ref[...] = jnp.where(lane == 0, col_one, jnp.where(lane == 1, col_two, -1))

    def block(expert, carry):
        spots = iota((cap_pad, toks), 0) + expert * cap_pad
        hot = jnp.where((spots == slot_one) | (spots == slot_two), 1.0, 0.0).astype(BF16)
        out_ref[expert] = dot_nn(hot, cot_ref[...]).astype(BF16)
        return carry

    lax.fori_loop(0, experts, block, 0)


def region_bias(kind, start, size, lower, upper, by_rows=True):
    first = iota((size, size), 0) + start
    second = iota((size, size), 1) + start
    if kind == 1:
        seg = lambda p: jnp.where(p < PATCH_L, 0, jnp.where(p < PATCH_L + PATCH_S, 1, 2))
    else:
        seg = lambda p: (
            jnp.where(p >= PATCH_S, 1, 0)
            + jnp.where(p >= 2 * PATCH_S, 1, 0)
            + jnp.where(p >= 3 * PATCH_S, 1, 0)
        )
    linked = seg(first) == seg(second)
    inside = (first >= lower) & (first < upper)
    return jnp.where(linked & inside, 0.0, NEG)


def kind_regions(kind, toks):
    if kind == 1:
        return ((0, PATCH_L, 0, PATCH_L, False), (PATCH_L, toks - PATCH_L, PATCH_L, toks, True))
    half = 2 * PATCH_S
    size = -(-half // 16) * 16
    begin = toks - size
    return ((0, size, 0, half, True), (begin, size, half, toks, True))


def forward_body(
    experts,
    cap_pad,
    kind_ref,
    x_ref,
    gains_ref,
    wq_ref,
    wk_ref,
    wv_ref,
    wo_ref,
    router_ref,
    routes_ref,
    slot_ref,
    qkv_ref,
    mix_ref,
    lse_ref,
    low_ref,
    residual_ref,
    lowered_ref,
    probs_ref,
    send_ref,
    acc_ref,
    out_ref,
    lse_scr,
    kept_ref,
):
    step = pl.program_id(0)
    steps = pl.num_programs(0)
    toks, width = x_ref.shape
    chunk = row_chunk(toks)

    @pl.when(step == 0)
    def _():
        def rows(i, carry):
            spot = pl.ds(pl.multiple_of(i * chunk, 16), chunk)
            scaled, _ = norm_stats(x_ref[spot, :].astype(F32))
            low_ref[spot, :] = (scaled * gains_ref[0:1, :] + gains_ref[1:2, :]).astype(BF16)
            return carry

        lax.fori_loop(0, toks // chunk, rows, 0)
        lse_scr[...] = jnp.zeros_like(lse_scr)

    low = low_ref[...]
    qkv_ref[0, :, 0:LANES] = dot_nn(low, wq_ref[...]).astype(BF16)
    qkv_ref[0, :, LANES : 2 * LANES] = dot_nn(low, wk_ref[...]).astype(BF16)
    qkv_ref[0, :, 2 * LANES : 3 * LANES] = dot_nn(low, wv_ref[...]).astype(BF16)

    def attend(kind):
        for start, size, lower, upper, masked in kind_regions(kind, toks):
            bias = region_bias(kind, start, size, lower, upper) if masked else None
            spot = slice(start, start + size)
            out_ref[lower:upper, :] = jnp.zeros((upper - lower, LANES), F32)

            def head(h, carry):
                mine = (iota((1, LANES), 1) // HEAD_DIM) == h
                queries = jnp.where(mine, qkv_ref[0, spot, 0:LANES], 0) * jnp.asarray(SCALE, BF16)
                scores = dot_nt(queries, qkv_ref[0, spot, LANES : 2 * LANES])
                if bias is not None:
                    scores = scores + bias
                top = jnp.max(scores, axis=-1, keepdims=True)
                weights = jnp.exp(scores - top)
                total = jnp.sum(weights, axis=-1, keepdims=True)
                values = jnp.where(mine, qkv_ref[0, spot, 2 * LANES : 3 * LANES], 0)
                mixed = dot_nn(weights.astype(BF16), values) * (1.0 / total)
                logsum = top + jnp.log(total)
                cut = slice(lower - start, upper - start)
                out_ref[lower:upper, :] += mixed[cut]
                lane = iota((upper - lower, 128), 1) == step * GROUP + h
                lse_scr[lower:upper, :] = jnp.where(lane, logsum[cut], lse_scr[lower:upper, :])
                return carry

            lax.fori_loop(0, GROUP, head, 0)

    @pl.when(kind_ref[0] == 1)
    def _():
        attend(1)

    @pl.when(kind_ref[0] != 1)
    def _():
        attend(0)

    mix = out_ref[...].astype(BF16)
    mix_ref[...] = mix
    branch = dot_nn(mix, wo_ref[...])

    @pl.when(step == 0)
    def _():
        acc_ref[...] = x_ref[...].astype(F32) + branch

    @pl.when(step > 0)
    def _():
        acc_ref[...] += branch

    @pl.when(step == steps - 1)
    def _():
        lse_ref[...] = lse_scr[...].T[0 : lse_ref.shape[0], 0:toks]

        def rows(i, carry):
            spot = pl.ds(pl.multiple_of(i * chunk, 16), chunk)
            residual = acc_ref[spot, :]
            residual_ref[spot, :] = residual
            scaled, _ = norm_stats(residual)
            lowered_ref[spot, :] = (scaled * gains_ref[2:3, :] + gains_ref[3:4, :]).astype(BF16)
            return carry

        lax.fori_loop(0, toks // chunk, rows, 0)
        lowered = lowered_ref[...]
        logits = dot_nt(router_ref[...], lowered)
        top = jnp.max(logits, axis=0, keepdims=True)
        raised = jnp.exp(logits - top)
        probs = raised / jnp.sum(raised, axis=0, keepdims=True)
        probs_ref[...] = probs
        labels = iota((experts, toks), 0)
        slot_one = slot_ref[0:1, :]
        slot_two = slot_ref[1:2, :]
        gate_one = jnp.sum(jnp.where(labels == routes_ref[0:1, :], probs, 0.0), axis=0, keepdims=True)
        gate_two = jnp.sum(jnp.where(labels == routes_ref[1:2, :], probs, 0.0), axis=0, keepdims=True)
        gate_one = jnp.where(slot_one >= 0, gate_one, 0.0)
        gate_two = jnp.where(slot_two >= 0, gate_two, 0.0)
        which = iota((16, toks), 0)

        def parts(gate):
            high = gate.astype(BF16).astype(F32)
            rest = gate - high
            return jnp.where(which == 0, high, jnp.where(which == 1, rest, 0.0)).astype(BF16)

        kept_ref[0] = parts(gate_one)
        kept_ref[1] = parts(gate_two)
        wide = -(-cap_pad // 128) * 128

        def block(expert, carry):
            spots = iota((wide, toks), 0) + expert * cap_pad
            hot_one = jnp.where(spots == slot_one, 1.0, 0.0)
            hot_two = jnp.where(spots == slot_two, 1.0, 0.0)
            gates = dot_nt(kept_ref[0], hot_one.astype(BF16)) + dot_nt(
                kept_ref[1], hot_two.astype(BF16)
            )
            picked = dot_nn((hot_one + hot_two)[0:cap_pad].astype(BF16), lowered)
            gates = jnp.concatenate([gates, jnp.zeros((16, width - wide), F32)], axis=1)
            row = iota((cap_pad, width), 0)
            picked = jnp.where(
                row == cap_pad - 2, gates[0:1], jnp.where(row == cap_pad - 1, gates[1:2], picked)
            )
            send_ref[expert] = picked.astype(BF16)
            return carry

        lax.fori_loop(0, experts, block, 0)


def phi_parts(v):
    a = jnp.abs(v)
    bell = jnp.exp2((-0.5 * LOG2E) * (v * v))
    t = 1.0 / (1.0 + PHI_RATE * a)
    poly = PHI_FIT[-1] * t
    for part in PHI_FIT[-2::-1]:
        poly = (poly + part) * t
    tail = poly * bell
    return jnp.where(v > 0, 1.0 - tail, tail), bell


def expert_body(
    x_ref,
    u_ref,
    w_ref,
    bias_ref,
    back_ref,
    z_ref,
    hidden_ref,
    grad_ref,
    g_ref,
    gg_ref,
    bin_ref,
    bback_ref,
    gate_scr,
    acc_scr,
    even_ref,
    odd_ref,
):
    step = pl.program_id(0)
    blocks, cap_pad, width = x_ref.shape
    wide = gg_ref.shape[2]
    tile = w_ref.shape[1]

    @pl.when(step == 0)
    def _():
        bback_ref[...] = jnp.zeros_like(bback_ref)

        def block(b, carry):
            tail = x_ref[b, cap_pad - 16 : cap_pad, 0:wide].astype(F32)
            gate_row = tail[14:15] + tail[15:16]
            same = iota((cap_pad, wide), 0) == iota((cap_pad, wide), 1)
            gate = jnp.sum(jnp.where(same, gate_row, 0.0), axis=1, keepdims=True)
            gate_scr[b] = jnp.broadcast_to(gate, (cap_pad, 128))
            rows = u_ref[b].astype(F32)
            made = (rows * gate).astype(BF16)
            g_ref[b] = made
            bback_ref[0:1, :] += jnp.sum(made.astype(F32), axis=0, keepdims=True)
            part = rows * back_ref[...]
            total = part[:, 0:128]
            for i in range(1, width // 128):
                total = total + part[:, i * 128 : (i + 1) * 128]
            acc_scr[b] = total
            return carry

        lax.fori_loop(0, blocks, block, 0)

    bin_ref[...] = jnp.zeros_like(bin_ref)

    def work(b, pre_ref):
        pre = pre_ref[...] + bias_ref[...]
        cdf, bell = phi_parts(pre)
        hidden = pre * cdf
        hidden_ref[b] = hidden.astype(BF16)
        z = z_ref[b].astype(F32)
        part = hidden * z
        total = acc_scr[b]
        for i in range(tile // 128):
            total = total + part[:, i * 128 : (i + 1) * 128]
        acc_scr[b] = total
        slope = cdf + pre * (bell * INV_ROOT_TAU)
        gate = jnp.concatenate([gate_scr[b]] * (tile // 128), axis=1)
        grad = (gate * z * slope).astype(BF16)
        grad_ref[b] = grad
        bin_ref[0:1, :] += jnp.sum(grad.astype(F32), axis=0, keepdims=True)

    even_ref[...] = dot_nn(x_ref[0], w_ref[...])

    def pair(i, carry):
        b = 2 * i
        odd_ref[...] = dot_nn(x_ref[b + 1], w_ref[...])
        work(b, even_ref)
        even_ref[...] = dot_nn(x_ref[jnp.minimum(b + 2, blocks - 1)], w_ref[...])
        work(b + 1, odd_ref)
        return carry

    lax.fori_loop(0, blocks // 2, pair, 0)

    @pl.when(step == pl.num_programs(0) - 1)
    def _():
        def last(b, carry):
            column = jnp.sum(acc_scr[b], axis=1, keepdims=True)
            same = iota((cap_pad, wide), 0) == iota((cap_pad, wide), 1)
            gg_ref[b, 0:1, :] = jnp.sum(jnp.where(same, column, 0.0), axis=0, keepdims=True)
            return carry

        lax.fori_loop(0, blocks, last, 0)


def produce_body(hidden_ref, w_ref, bias_ref, out_ref):
    out_ref[...] = (dot_nn(hidden_ref[...], w_ref[...]) + bias_ref[...]).astype(BF16)


def combine_body(
    experts, kept_ref, slot_ref, routes_ref, probs_ref, residual_ref, back_ref, result_ref
):
    blocks, cap_pad, width = back_ref.shape
    toks = residual_ref.shape[0]
    chunk = row_chunk(toks)
    flat = back_ref[...].reshape(blocks * cap_pad, width)
    labels = iota((experts, toks), 0)
    probs = probs_ref[...]

    def gate(k):
        return jnp.sum(jnp.where(labels == routes_ref[k : k + 1, :], probs, 0.0), axis=0, keepdims=True)

    gate_one, gate_two = gate(0), gate(1)

    def columns(i, carry):
        spot = pl.ds(pl.multiple_of(i * chunk, 16), chunk)
        eye = iota((chunk, toks), 0) + i * chunk == iota((chunk, toks), 1)
        col_one = jnp.sum(jnp.where(eye, gate_one, 0.0), axis=1, keepdims=True)
        col_two = jnp.sum(jnp.where(eye, gate_two, 0.0), axis=1, keepdims=True)
        spots = iota((chunk, blocks * cap_pad), 1)
        hot = jnp.where(spots == kept_ref[spot, 0:1], col_one, 0.0) + jnp.where(
            spots == kept_ref[spot, 1:2], col_two, 0.0
        )
        result_ref[spot, :] = (residual_ref[spot, :] + dot_nn(hot.astype(BF16), flat)).astype(BF16)
        return carry

    lax.fori_loop(0, toks // chunk, columns, 0)


def row_grad_body(
    experts,
    col_ref,
    slot_ref,
    routes_ref,
    probs_ref,
    lowered_ref,
    residual_ref,
    cot_ref,
    gain_ref,
    router_ref,
    back_ref,
    grad_ref,
    low_ref,
    small_ref,
    route_grad_ref,
    logit_ref,
):
    blocks, cap_pad, width = back_ref.shape
    toks = lowered_ref.shape[0]
    chunk = row_chunk(toks)
    labels = iota((experts, toks), 0)
    slot_one = slot_ref[0:1, :]
    slot_two = slot_ref[1:2, :]
    wide = -(-cap_pad // 128) * 128
    gate_one = jnp.zeros((16, toks), F32)
    gate_two = jnp.zeros((16, toks), F32)

    def block(expert, carry):
        one, two = carry
        spots = iota((cap_pad, toks), 0) + expert * cap_pad
        tail = back_ref[expert, cap_pad - 16 : cap_pad, 0:cap_pad]
        hot_one = jnp.where(spots == slot_one, 1.0, 0.0).astype(BF16)
        hot_two = jnp.where(spots == slot_two, 1.0, 0.0).astype(BF16)
        return one + dot_nn(tail, hot_one), two + dot_nn(tail, hot_two)

    gate_one, gate_two = lax.fori_loop(0, experts, block, (gate_one, gate_two))
    gate_one = gate_one[14:15] + gate_one[15:16]
    gate_two = gate_two[14:15] + gate_two[15:16]
    probs = probs_ref[...]
    grad_probs = jnp.where(labels == routes_ref[0:1, :], gate_one, 0.0) + jnp.where(
        labels == routes_ref[1:2, :], gate_two, 0.0
    )
    grad_logits = probs * (grad_probs - jnp.sum(probs * grad_probs, axis=0, keepdims=True))
    grad_logits = grad_logits.astype(BF16)
    route_grad_ref[...] = dot_nn(grad_logits, lowered_ref[...])
    logit_ref[...] = dot_tn(grad_logits, router_ref[...])
    small_ref[...] = jnp.zeros_like(small_ref)
    flat = back_ref[...].reshape(blocks * cap_pad, width)

    def rows(i, carry):
        spot = pl.ds(pl.multiple_of(i * chunk, 16), chunk)
        spots = iota((chunk, blocks * cap_pad), 1)
        hot = jnp.where(
            (spots == col_ref[spot, 0:1]) | (spots == col_ref[spot, 1:2]), 1.0, 0.0
        ).astype(BF16)
        grad = logit_ref[spot, :] + dot_nn(hot, flat)
        scaled, inverse = norm_stats(residual_ref[spot, :])
        small_ref[0:1, :] += jnp.sum(grad * scaled, axis=0, keepdims=True)
        small_ref[1:2, :] += jnp.sum(grad, axis=0, keepdims=True)
        total = cot_ref[spot, :].astype(F32) + norm_grad(grad, scaled, inverse, gain_ref[2:3, :])
        grad_ref[spot, :] = total
        low_ref[spot, :] = total.astype(BF16)
        return carry

    lax.fori_loop(0, toks // chunk, rows, 0)


def backward_body(
    first_group,
    kind_ref,
    up_ref,
    wo_ref,
    qkv_ref,
    mix_ref,
    lse_ref,
    grad_ref,
    do_ref,
    delta_ref,
    dq_ref,
    dk_ref,
    dv_ref,
):
    toks = up_ref.shape[0]
    group = pl.program_id(0) + first_group
    do = dot_nt(up_ref[...], wo_ref[...]).astype(BF16)
    do_ref[...] = do
    both = do.astype(F32) * mix_ref[...].astype(F32)
    high = both.astype(BF16)
    rest = (both - high.astype(F32)).astype(BF16)
    owner = jnp.where(iota((16, LANES), 1) // HEAD_DIM == iota((16, LANES), 0), 1.0, 0.0).astype(BF16)
    delta_ref[...] = dot_nt(owner, high) + dot_nt(owner, rest)
    dq_ref[...] = jnp.zeros_like(dq_ref)
    dk_ref[...] = jnp.zeros_like(dk_ref)
    dv_ref[...] = jnp.zeros_like(dv_ref)

    def attend(kind):
        for start, size, lower, upper, masked in kind_regions(kind, toks):
            bias = region_bias(kind, start, size, lower, upper) if masked else None
            spot = slice(start, start + size)

            def head(h, carry):
                mine = (iota((1, LANES), 1) // HEAD_DIM) == h
                queries = jnp.where(mine, qkv_ref[0, spot, 0:LANES], 0) * jnp.asarray(SCALE, BF16)
                keys_all = qkv_ref[0, spot, LANES : 2 * LANES]
                own = jnp.where(mine, do_ref[spot, :], 0)
                logsum = lse_ref[pl.ds(group * GROUP + h, 1), :][:, spot]
                delta = delta_ref[pl.ds(h, 1), :][:, spot]
                scores = dot_nt(keys_all, queries)
                if bias is not None:
                    scores = scores + bias
                weights = jnp.exp(scores - logsum)
                grad_weights = dot_nt(qkv_ref[0, spot, 2 * LANES : 3 * LANES], own)
                grad_scores = (weights * (grad_weights - delta)).astype(BF16)
                dv_ref[spot, :] += dot_nn(weights.astype(BF16), own)
                dk_ref[spot, :] += dot_nn(grad_scores, queries)
                dq_ref[spot, :] += dot_tn(grad_scores, jnp.where(mine, keys_all, 0))
                return carry

            lax.fori_loop(0, GROUP, head, 0)

    @pl.when(kind_ref[0] == 1)
    def _():
        attend(1)

    @pl.when(kind_ref[0] != 1)
    def _():
        attend(0)

    grad_ref[:, 0:LANES] = (dq_ref[...] * SCALE).astype(BF16)
    grad_ref[:, LANES : 2 * LANES] = dk_ref[...].astype(BF16)
    grad_ref[:, 2 * LANES : 3 * LANES] = dv_ref[...].astype(BF16)


def final_body(groups, *refs):
    packed = refs[0:groups]
    weights = refs[groups : 2 * groups]
    x_ref, gain_ref, up_ref, out_ref, small_ref, acc_ref = refs[2 * groups :]
    toks = x_ref.shape[0]
    chunk = row_chunk(toks)
    total = dot_nt(packed[0][...], weights[0][...])
    for i in range(1, groups):
        total = total + dot_nt(packed[i][...], weights[i][...])
    acc_ref[...] = total
    small_ref[...] = jnp.zeros_like(small_ref)

    def rows(i, carry):
        spot = pl.ds(pl.multiple_of(i * chunk, 16), chunk)
        grad = acc_ref[spot, :]
        scaled, inverse = norm_stats(x_ref[spot, :].astype(F32))
        small_ref[0:1, :] += jnp.sum(grad * scaled, axis=0, keepdims=True)
        small_ref[1:2, :] += jnp.sum(grad, axis=0, keepdims=True)
        out_ref[spot, :] = (
            up_ref[spot, :] + norm_grad(grad, scaled, inverse, gain_ref[0:1, :])
        ).astype(BF16)
        return carry

    lax.fori_loop(0, toks // chunk, rows, 0)


def place_body(core_ref, own_one, other_one, own_two, other_two, out_ref):
    zero = core_ref[0] == 0
    parts = (
        jnp.where(zero, other_one[...], own_one[...]),
        jnp.where(zero, own_two[...], other_two[...]),
        jnp.where(zero, other_two[...], own_two[...]),
    )
    for k, part in enumerate(parts):
        for p in range(3):
            at = (p * 3 + k) * LANES
            out_ref[:, at : at + LANES] = part[:, p * LANES : (p + 1) * LANES].astype(F32)


def place_qkv(pairs, core):
    rows, cols = pairs[0][0].shape
    tile = rows // 3
    return call(
        place_body,
        jax.ShapeDtypeStruct((rows, 3 * cols), F32),
        in_specs=[pl.BlockSpec(memory_space=pltpu.SMEM)]
        + [pl.BlockSpec((tile, cols), lambda i: (i, 0)) for _ in range(4)],
        out_specs=pl.BlockSpec((tile, 3 * cols), lambda i: (i, 0)),
        grid=(3,),
        name="place_qkv",
        cost=(1e6, 20 * rows * cols, 0),
    )(core.astype(jnp.int32).reshape(1), *[part for pair in pairs for part in pair])


def bits_below(count):
    bits, bit = [], 1
    while bit < count:
        bits.append(bit)
        bit *= 2
    return bits


def send_xor(values, axis, size, distance):
    return lax.ppermute(values, axis, [(j, j ^ distance) for j in range(size)])


def trade_sum(parts, axis, size, stride, mine, extra, after):
    def pick(place):
        part = lax.dynamic_index_in_dim(parts, place, 0, keepdims=False)
        return part if extra is None else jnp.concatenate([part, extra], axis=0)

    own = pick(mine)
    if after:
        own = hold(own, after)
    total = own.astype(F32)
    for d in range(1, parts.shape[0]):
        total = total + send_xor(pick(mine ^ d), axis, size, d * stride).astype(F32)
    return total.astype(parts.dtype)


def gather_group(values, axis, size, stride, count, mine):
    got = [values] + [send_xor(values, axis, size, d * stride) for d in range(1, count)]
    for bit in bits_below(count):
        flip = (mine & bit) != 0
        got = [jnp.where(flip, got[k ^ bit], got[k]) for k in range(count)]
    return jnp.concatenate(got, axis=0)


class PairSum:
    def __init__(self, first, second, wide, plan):
        self.width = first.shape[1]
        self.wide = wide
        self.plan = plan
        self.core = lax.axis_index("ex") % 2
        self.keep = jnp.where(self.core == 0, first, second)
        self.value = jnp.where(self.core == 0, second, first)
        self.extra = None
        self.stage = 0

    def step(self, after=()):
        v = self.value
        deep = len(self.plan)
        if self.stage == 0:
            other = send_xor(v, "ex", self.wide, 1)
            keep = hold(self.keep, after) if after else self.keep
            v = (keep.astype(F32) + other.astype(F32)).astype(v.dtype)
        elif self.stage <= deep:
            axis, size, stride, count = self.plan[self.stage - 1]
            mine = (lax.axis_index(axis) // stride) % count
            parts = v.reshape(count, -1, self.width)
            v = trade_sum(parts, axis, size, stride, mine, self.extra, after)
            if self.extra is not None:
                rows = parts.shape[1]
                self.extra = v[rows:]
                v = v[:rows]
        else:
            axis, size, stride, count = self.plan[2 * deep - self.stage]
            mine = (lax.axis_index(axis) // stride) % count
            v = gather_group(v, axis, size, stride, count, mine)
            if after:
                v = hold(v, after)
        self.stage += 1
        self.value = v
        return v

    def left(self):
        return 2 * len(self.plan) + 1 - self.stage

    def finish(self):
        while self.left():
            self.step()
        return self.value, send_xor(self.value, "ex", self.wide, 1)


def local(
    sizes,
    tokens,
    gain_one,
    shift_one,
    w_qkv,
    w_out,
    gain_two,
    shift_two,
    w_router,
    w_in,
    bias_in,
    w_back,
    bias_back,
    cotangent,
    routes,
    priority,
    image_kind,
):
    toks, width = tokens.shape
    experts = w_router.shape[1]
    hidden_units = w_in.shape[2]
    cap = (42 * toks + 20 * experts - 1) // (20 * experts)
    cap_pad = -(-(cap + 2) // 16) * 16
    wide = -(-cap_pad // 128) * 128
    groups = HEADS // GROUP
    first_w, second_w = w_in[0], w_back[0]
    routes_row = routes.T
    router_row = w_router.T
    sds = jax.ShapeDtypeStruct
    dispatched = (experts, cap_pad, width)

    slots, slot_col, up_rows = call(
        functools.partial(prep_body, experts, cap, cap_pad),
        (sds((8, toks), jnp.int32), sds((toks, 128), jnp.int32), sds(dispatched, BF16)),
        cost=(4e9, 6e6, 0),
        name="prep",
    )(routes_row, priority, cotangent)
    up_in = lax.all_to_all(up_rows, "ex", split_axis=0, concat_axis=0, tiled=True)

    gains = jnp.stack([gain_one, shift_one, gain_two, shift_two])
    col = lambda offset: pl.BlockSpec((width, LANES), lambda g: (0, offset * groups + g))
    smem = pl.BlockSpec(memory_space=pltpu.SMEM)
    per_group = lambda: pl.BlockSpec((1, toks, 3 * LANES), lambda g: (g, 0, 0))
    qkv, mix, logsum, low_one, residual, lowered, probs, sent = call(
        functools.partial(forward_body, experts, cap_pad),
        (
            sds((groups, toks, 3 * LANES), BF16),
            sds((toks, width), BF16),
            sds((16, toks), F32),
            sds((toks, width), BF16),
            sds((toks, width), F32),
            sds((toks, width), BF16),
            sds((experts, toks), F32),
            sds(dispatched, BF16),
        ),
        in_specs=[
            smem,
            whole((toks, width)),
            whole((4, width)),
            col(0),
            col(1),
            col(2),
            pl.BlockSpec((LANES, width), lambda g: (g, 0)),
            whole((experts, width)),
            whole((2, toks)),
            whole((8, toks)),
        ],
        out_specs=[
            per_group(),
            pl.BlockSpec((toks, LANES), lambda g: (0, g)),
            whole((16, toks)),
            whole((toks, width)),
            whole((toks, width)),
            whole((toks, width)),
            whole((experts, toks)),
            whole(dispatched),
        ],
        grid=(groups,),
        scratch=[
            pltpu.VMEM((toks, width), F32),
            pltpu.VMEM((toks, LANES), F32),
            pltpu.VMEM((-(-toks // 128) * 128, 128), F32),
            pltpu.VMEM((2, 16, toks), BF16),
        ],
        cost=(10e9, 20e6, 4e6),
        name="attend",
    )(
        image_kind,
        tokens,
        gains,
        w_qkv,
        w_qkv,
        w_qkv,
        w_out,
        router_row,
        routes_row,
        slots,
    )
    rows_in = lax.all_to_all(sent, "ex", split_axis=0, concat_axis=0, tiled=True)

    blocks = rows_in.shape[0]
    flat_up = up_in.reshape(-1, width)
    z = dot_nt(flat_up, second_w).astype(BF16).reshape(blocks, cap_pad, hidden_units)
    tile = 512 if hidden_units % 512 == 0 else 256
    ff = lambda: pl.BlockSpec((blocks, cap_pad, tile), lambda j: (0, 0, j))
    hidden, grad_pre, grad_slots, grad_gate, bin_sum, bback_sum = call(
        expert_body,
        (
            sds((blocks, cap_pad, hidden_units), BF16),
            sds((blocks, cap_pad, hidden_units), BF16),
            sds((blocks, cap_pad, width), BF16),
            sds((blocks, 8, wide), F32),
            sds((8, hidden_units), F32),
            sds((8, width), F32),
        ),
        in_specs=[
            whole((blocks, cap_pad, width)),
            whole((blocks, cap_pad, width)),
            pl.BlockSpec((width, tile), lambda j: (0, j)),
            pl.BlockSpec((1, tile), lambda j: (0, j)),
            whole((1, width)),
            ff(),
        ],
        out_specs=[
            ff(),
            ff(),
            whole((blocks, cap_pad, width)),
            whole((blocks, 8, wide)),
            pl.BlockSpec((8, tile), lambda j: (0, j)),
            whole((8, width)),
        ],
        grid=(hidden_units // tile,),
        scratch=[
            pltpu.VMEM((blocks, cap_pad, 128), F32),
            pltpu.VMEM((blocks, cap_pad, 128), F32),
            pltpu.VMEM((cap_pad, tile), F32),
            pltpu.VMEM((cap_pad, tile), F32),
        ],
        cost=(8e9, 40e6, 10e6),
        name="expert",
    )(rows_in, up_in, first_w, bias_in, bias_back, z)
    flat_rows = rows_in.reshape(-1, width)
    flat_hidden = hidden.reshape(-1, hidden_units)
    flat_pre = grad_pre.reshape(-1, hidden_units)
    flat_slots = grad_slots.reshape(-1, width)

    gate_row = grad_gate[:, 0:1, :]
    gate_high = gate_row.astype(BF16).astype(F32)
    gate_rows = jnp.concatenate([gate_high, gate_row - gate_high], axis=1)
    gate_rows = jnp.pad(gate_rows, ((0, 0), (cap_pad - 2, 0), (0, width - wide)))
    first_grad = dot_tn(flat_rows, flat_pre).astype(BF16)
    first_out = lax.psum_scatter(first_grad, "rep", scatter_dimension=0, tiled=True).astype(F32)
    flat_pre = hold(flat_pre, [first_grad])
    grad_rows = dot_nt(flat_pre, first_w).reshape(blocks, cap_pad, width)
    tail = lax.broadcasted_iota(jnp.int32, (blocks, cap_pad, width), 1) >= cap_pad - 2
    grad_rows = jnp.where(tail, gate_rows, grad_rows).astype(BF16)
    grad_back = lax.all_to_all(grad_rows, "ex", split_axis=0, concat_axis=0, tiled=True)

    flat_slots = hold(flat_slots, [first_grad, grad_rows])
    second_grad = dot_tn(flat_hidden, flat_slots).astype(BF16)
    second_out = lax.psum_scatter(second_grad, "rep", scatter_dimension=0, tiled=True).astype(F32)
    flat_hidden = hold(flat_hidden, [second_grad])
    tall = blocks * cap_pad // 4
    produced = call(
        produce_body,
        sds((blocks * cap_pad, width), BF16),
        in_specs=[
            pl.BlockSpec((tall, hidden_units), lambda i: (i, 0)),
            whole((hidden_units, width)),
            whole((1, width)),
        ],
        out_specs=pl.BlockSpec((tall, width), lambda i: (i, 0)),
        grid=(4,),
        cost=(1, 1, 0),
        name="produce",
    )(flat_hidden, second_w, bias_back)
    returned = lax.all_to_all(
        produced.reshape(blocks, cap_pad, width), "ex", split_axis=0, concat_axis=0, tiled=True
    )

    reps = sizes["rep"]
    grad_residual, grad_branch, small_two, route_grad = call(
        functools.partial(row_grad_body, experts),
        (
            sds((toks, width), F32),
            sds((toks, width), BF16),
            sds((8, width), F32),
            sds((experts, width), F32),
        ),
        scratch=[pltpu.VMEM((toks, width), F32)],
        cost=(1, 1, 0),
        name="row_grad",
        after=[first_grad, second_grad, produced],
    )(
        slot_col,
        slots,
        routes_row,
        probs,
        lowered,
        residual,
        cotangent,
        gains,
        router_row,
        grad_back,
    )
    out_part = dot_tn(mix, grad_branch).astype(BF16)
    sums = []

    def advance():
        return [s.step() for s in sums]

    reps = sizes["rep"]
    plane_hops = [("ex", sizes["ex"], bit, 2) for bit in bits_below(sizes["ex"])[1:]]
    rep_hops = [("rep", reps, bit, 2) for bit in bits_below(reps)]
    packed_grads = []
    parts = [out_part]
    waiting = [out_part]
    for g in range(groups):
        if g == 1:
            waiting.append(returned)
        packed = call(
            functools.partial(backward_body, g),
            sds((toks, 3 * LANES), BF16),
            in_specs=[
                smem,
                whole((toks, width)),
                pl.BlockSpec((LANES, width), lambda i, g=g: (g, 0)),
                pl.BlockSpec((1, toks, 3 * LANES), lambda i, g=g: (g, 0, 0)),
                pl.BlockSpec((toks, LANES), lambda i, g=g: (0, g)),
                whole((16, toks)),
            ],
            out_specs=whole((toks, 3 * LANES)),
            grid=(1,),
            scratch=[
                pltpu.VMEM((toks, LANES), BF16),
                pltpu.VMEM((16, toks), F32),
                pltpu.VMEM((toks, LANES), F32),
                pltpu.VMEM((toks, LANES), F32),
                pltpu.VMEM((toks, LANES), F32),
            ],
            cost=(8e9, 6e6, 2e6),
            name="attend_back_" + "abcdef"[g],
            after=waiting,
        )(image_kind, grad_branch, w_out, qkv, mix, logsum)
        packed_grads.append(packed)
        waiting = advance()
        parts.append(dot_tn(low_one, packed).astype(BF16))
        if len(parts) == 2:
            order = plane_hops[:: 1 if g == 0 else -1]
            sums.append(PairSum(*parts, sizes["ex"], order + rep_hops))
            parts = []
            waiting.append(sums[-1].value)
        else:
            waiting.append(parts[-1])

    w_groups = [
        jnp.concatenate(
            [w_qkv[:, (p * groups + g) * LANES : (p * groups + g + 1) * LANES] for p in range(3)],
            axis=1,
        )
        for g in range(groups)
    ]
    grad_tokens, small_one = call(
        functools.partial(final_body, groups),
        (sds((toks, width), BF16), sds((8, width), F32)),
        scratch=[pltpu.VMEM((toks, width), F32)],
        cost=(3e9, 14e6, 0),
        name="final",
        after=[sums[1].value],
    )(*packed_grads, *w_groups, tokens, gains, grad_residual)
    ahead, last = sums
    small = jnp.concatenate([small_one[0:2], small_two[0:2], route_grad], axis=0)
    small_rows = small.shape[0]
    added = last.step([small_one])
    last.extra = jnp.pad(small, ((0, -small_rows % 16), (0, 0))).astype(BF16)
    result = call(
        functools.partial(combine_body, experts),
        sds((toks, width), BF16),
        cost=(2e9, 8e6, 0),
        name="combine",
        after=[added, ahead.value, first_out],
    )(slot_col, slots, routes_row, probs, residual, returned)
    ahead.step([result])
    last.step([result])
    bin_sum = hold(bin_sum, [result])
    while ahead.stage < len(plane_hops) + 1:
        ahead.step()
        last.step()
    bias_rows = jnp.concatenate([bin_sum[0].reshape(-1, width), bback_sum[0:1]], axis=0)
    bias_rows = jnp.pad(bias_rows, ((0, -bias_rows.shape[0] % 16), (0, 0))).astype(BF16)
    ahead.extra = bias_rows
    while last.left() > 1:
        if ahead.left():
            ahead.step([second_out] if ahead.left() == 1 else ())
        last.step()
    last.step()
    pairs = [ahead.finish(), last.finish()]
    rank = lax.axis_index("rep")
    bias_sum = ahead.extra.astype(F32)
    bin_out = bias_sum[: hidden_units // width].reshape(-1)
    bin_out = lax.dynamic_slice_in_dim(bin_out, rank * (hidden_units // reps), hidden_units // reps)
    bback_out = lax.dynamic_slice_in_dim(
        bias_sum[hidden_units // width], rank * (width // reps), width // reps
    )
    small = last.extra.astype(F32)
    small = small + send_xor(small, "ex", sizes["ex"], 1)
    core = lax.axis_index("ex") % 2
    out_grad = jnp.where(core == 0, *pairs[0]).astype(F32)
    qkv_grad = place_qkv(pairs, core)
    return (
        result,
        grad_tokens,
        small[0],
        small[1],
        qkv_grad,
        out_grad,
        small[2],
        small[3],
        small[4:small_rows].T,
        first_out[None],
        bin_out[None],
        second_out[None],
        bback_out[None],
    )


def solution(mesh):
    both = ("rep", "ex")
    in_specs = (
        P(both, None),
        P(),
        P(),
        P(),
        P(),
        P(),
        P(),
        P(),
        P("ex", None, None),
        P("ex", None),
        P("ex", None, None),
        P("ex", None),
        P(both, None),
        P(both, None),
        P(both, None),
        P(both),
    )
    out_specs = (
        P(both, None),
        P(both, None),
        P(),
        P(),
        P(),
        P(),
        P(),
        P(),
        P(),
        P("ex", "rep", None),
        P("ex", "rep"),
        P("ex", "rep", None),
        P("ex", "rep"),
    )
    return jax.shard_map(
        functools.partial(local, dict(mesh.shape)),
        mesh=mesh,
        in_specs=in_specs,
        out_specs=out_specs,
        check_vma=False,
    )
```

```python
import functools

import jax
import jax.numpy as jnp
from jax import lax
from jax.experimental import pallas as pl
from jax.experimental.pallas import tpu as pltpu
from jax.sharding import PartitionSpec as P

HEADS = 12
HEAD_DIM = 64
PATCH_S = 196
PATCH_L = 576
GROUP = 4
LANES = GROUP * HEAD_DIM

EPS = 1e-06
NEG = -1e30
SCALE = HEAD_DIM ** (-0.5)
LOG2E = 1.4426950408889634
INV_ROOT_TAU = 0.3989422804014327
PHI_RATE = 0.36
PHI_FIT = (
    0.14371304535439455,
    0.14177245494035942,
    0.1397192591115954,
    0.026549327576509053,
    0.18095403137785818,
    -0.17976471959279186,
    0.047056297922502474,
)
F32 = jnp.float32
BF16 = jnp.bfloat16


def dot_nn(a, b):
    return lax.dot_general(a, b, (((1,), (0,)), ((), ())), preferred_element_type=F32)


def dot_nt(a, b):
    return lax.dot_general(a, b, (((1,), (1,)), ((), ())), preferred_element_type=F32)


def dot_tn(a, b):
    return lax.dot_general(a, b, (((0,), (0,)), ((), ())), preferred_element_type=F32)


def iota(shape, dim):
    return lax.broadcasted_iota(jnp.int32, shape, dim)


def call(
    body, out_shape, in_specs=None, out_specs=None, grid=None, scratch=(), cost=None, name=None, after=()
):
    args = dict(out_shape=out_shape, scratch_shapes=list(scratch), name=name)
    if grid is not None:
        args["grid"] = grid
    if out_specs is not None:
        args["out_specs"] = out_specs
    if cost is not None:
        args["cost_estimate"] = pl.CostEstimate(
            flops=int(cost[0]), bytes_accessed=int(cost[1]), transcendentals=int(cost[2])
        )

    def run(*operands):
        count = len(operands)
        specs = in_specs or [pl.BlockSpec(memory_space=pltpu.VMEM)] * count
        specs = list(specs) + [pl.BlockSpec(memory_space=pl.ANY)] * len(after)

        def inner(*refs):
            body(*refs[:count], *refs[count + len(after) :])

        return pl.pallas_call(
            inner,
            in_specs=specs,
            compiler_params=pltpu.CompilerParams(vmem_limit_bytes=60 * 1024 * 1024),
            **args,
        )(*operands, *after)

    return run


def hold(values, after):
    def nothing(*refs):
        pass

    any_spec = pl.BlockSpec(memory_space=pl.ANY)
    return pl.pallas_call(
        nothing,
        out_shape=jax.ShapeDtypeStruct(values.shape, values.dtype),
        in_specs=[any_spec] * (1 + len(after)),
        out_specs=any_spec,
        input_output_aliases={0: 0},
        name="hold",
    )(values, *after)


def whole(shape, memory_space=None):
    zeros = (0,) * len(shape)
    if memory_space is not None:
        return pl.BlockSpec(shape, lambda *_: zeros, memory_space=memory_space)
    return pl.BlockSpec(shape, lambda *_: zeros)


def norm_stats(values):
    average = jnp.mean(values, axis=-1, keepdims=True)
    centered = values - average
    variance = jnp.mean(centered * centered, axis=-1, keepdims=True)
    inverse = lax.rsqrt(variance + EPS)
    return centered * inverse, inverse


def norm_grad(grad, scaled, inverse, gain):
    through = grad * gain
    first = jnp.mean(through, axis=-1, keepdims=True)
    second = jnp.mean(through * scaled, axis=-1, keepdims=True)
    return inverse * (through - first - scaled * second)


def row_chunk(rows):
    for size in (112, 128, 64, 48, 32, 16):
        if rows % size == 0:
            return size
    return rows


def prep_body(experts, cap, cap_pad, routes_ref, prio_ref, cot_ref, slot_ref, col_ref, out_ref):
    toks = cot_ref.shape[0]
    prio = prio_ref[...].astype(F32)
    prio_col = jnp.sum(
        jnp.where(iota((toks, toks), 0) == iota((toks, toks), 1), prio, 0.0), axis=1, keepdims=True
    )
    below = jnp.where(prio_col < prio, 1.0, 0.0).astype(BF16)
    labels = iota((experts, toks), 0)
    first = routes_ref[0:1, :]
    second = routes_ref[1:2, :]
    hot_one = jnp.where(labels == first, 1.0, 0.0)
    hot_two = jnp.where(labels == second, 1.0, 0.0)
    count_one = dot_nn(hot_one.astype(BF16), below)
    count_two = dot_nn(hot_two.astype(BF16), below)
    total_one = jnp.sum(hot_one, axis=1, keepdims=True)
    place_one = jnp.sum(hot_one * count_one, axis=0, keepdims=True)
    place_two = jnp.sum(hot_two * (count_two + total_one), axis=0, keepdims=True)
    slot_one = jnp.where(
        place_one < cap, first * cap_pad + place_one.astype(jnp.int32), -1
    )
    slot_two = jnp.where(
        place_two < cap, second * cap_pad + place_two.astype(jnp.int32), -1
    )
    slot_ref[0:1, :] = slot_one
    slot_ref[1:2, :] = slot_two
    eye = iota((toks, toks), 0) == iota((toks, toks), 1)
    col_one = jnp.sum(jnp.where(eye, slot_one, 0), axis=1, keepdims=True)
    col_two = jnp.sum(jnp.where(eye, slot_two, 0), axis=1, keepdims=True)
    lane = iota((toks, 128), 1)
    col_ref[...] = jnp.where(lane == 0, col_one, jnp.where(lane == 1, col_two, -1))

    def block(expert, carry):
        spots = iota((cap_pad, toks), 0) + expert * cap_pad
        hot = jnp.where((spots == slot_one) | (spots == slot_two), 1.0, 0.0).astype(BF16)
        out_ref[expert] = dot_nn(hot, cot_ref[...]).astype(BF16)
        return carry

    lax.fori_loop(0, experts, block, 0)


def region_bias(kind, start, size, lower, upper, by_rows=True):
    first = iota((size, size), 0) + start
    second = iota((size, size), 1) + start
    if kind == 1:
        seg = lambda p: jnp.where(p < PATCH_L, 0, jnp.where(p < PATCH_L + PATCH_S, 1, 2))
    else:
        seg = lambda p: (
            jnp.where(p >= PATCH_S, 1, 0)
            + jnp.where(p >= 2 * PATCH_S, 1, 0)
            + jnp.where(p >= 3 * PATCH_S, 1, 0)
        )
    linked = seg(first) == seg(second)
    inside = (first >= lower) & (first < upper)
    return jnp.where(linked & inside, 0.0, NEG)


def kind_regions(kind, toks):
    if kind == 1:
        return ((0, PATCH_L, 0, PATCH_L, False), (PATCH_L, toks - PATCH_L, PATCH_L, toks, True))
    half = 2 * PATCH_S
    size = -(-half // 16) * 16
    begin = toks - size
    return ((0, size, 0, half, True), (begin, size, half, toks, True))


def forward_body(
    experts,
    cap_pad,
    kind_ref,
    x_ref,
    gains_ref,
    wq_ref,
    wk_ref,
    wv_ref,
    wo_ref,
    router_ref,
    routes_ref,
    slot_ref,
    qkv_ref,
    mix_ref,
    lse_ref,
    low_ref,
    residual_ref,
    lowered_ref,
    probs_ref,
    send_ref,
    acc_ref,
    out_ref,
    lse_scr,
    kept_ref,
):
    step = pl.program_id(0)
    steps = pl.num_programs(0)
    toks, width = x_ref.shape
    chunk = row_chunk(toks)

    @pl.when(step == 0)
    def _():
        def rows(i, carry):
            spot = pl.ds(pl.multiple_of(i * chunk, 16), chunk)
            scaled, _ = norm_stats(x_ref[spot, :].astype(F32))
            low_ref[spot, :] = (scaled * gains_ref[0:1, :] + gains_ref[1:2, :]).astype(BF16)
            return carry

        lax.fori_loop(0, toks // chunk, rows, 0)
        lse_scr[...] = jnp.zeros_like(lse_scr)

    low = low_ref[...]
    qkv_ref[0, :, 0:LANES] = dot_nn(low, wq_ref[...]).astype(BF16)
    qkv_ref[0, :, LANES : 2 * LANES] = dot_nn(low, wk_ref[...]).astype(BF16)
    qkv_ref[0, :, 2 * LANES : 3 * LANES] = dot_nn(low, wv_ref[...]).astype(BF16)

    def attend(kind):
        for start, size, lower, upper, masked in kind_regions(kind, toks):
            bias = region_bias(kind, start, size, lower, upper) if masked else None
            spot = slice(start, start + size)
            out_ref[lower:upper, :] = jnp.zeros((upper - lower, LANES), F32)

            def head(h, carry):
                mine = (iota((1, LANES), 1) // HEAD_DIM) == h
                queries = jnp.where(mine, qkv_ref[0, spot, 0:LANES], 0) * jnp.asarray(SCALE, BF16)
                scores = dot_nt(queries, qkv_ref[0, spot, LANES : 2 * LANES])
                if bias is not None:
                    scores = scores + bias
                top = jnp.max(scores, axis=-1, keepdims=True)
                weights = jnp.exp(scores - top)
                total = jnp.sum(weights, axis=-1, keepdims=True)
                values = jnp.where(mine, qkv_ref[0, spot, 2 * LANES : 3 * LANES], 0)
                mixed = dot_nn(weights.astype(BF16), values) * (1.0 / total)
                logsum = top + jnp.log(total)
                cut = slice(lower - start, upper - start)
                out_ref[lower:upper, :] += mixed[cut]
                lane = iota((upper - lower, 128), 1) == step * GROUP + h
                lse_scr[lower:upper, :] = jnp.where(lane, logsum[cut], lse_scr[lower:upper, :])
                return carry

            lax.fori_loop(0, GROUP, head, 0, unroll=2)

    @pl.when(kind_ref[0] == 1)
    def _():
        attend(1)

    @pl.when(kind_ref[0] != 1)
    def _():
        attend(0)

    mix = out_ref[...].astype(BF16)
    mix_ref[...] = mix
    branch = dot_nn(mix, wo_ref[...])

    @pl.when(step == 0)
    def _():
        acc_ref[...] = x_ref[...].astype(F32) + branch

    @pl.when(step > 0)
    def _():
        acc_ref[...] += branch

    @pl.when(step == steps - 1)
    def _():
        lse_ref[...] = lse_scr[...].T[0 : lse_ref.shape[0], 0:toks]

        def rows(i, carry):
            spot = pl.ds(pl.multiple_of(i * chunk, 16), chunk)
            residual = acc_ref[spot, :]
            residual_ref[spot, :] = residual
            scaled, _ = norm_stats(residual)
            lowered_ref[spot, :] = (scaled * gains_ref[2:3, :] + gains_ref[3:4, :]).astype(BF16)
            return carry

        lax.fori_loop(0, toks // chunk, rows, 0)
        lowered = lowered_ref[...]
        logits = dot_nt(router_ref[...], lowered)
        top = jnp.max(logits, axis=0, keepdims=True)
        raised = jnp.exp(logits - top)
        probs = raised / jnp.sum(raised, axis=0, keepdims=True)
        probs_ref[...] = probs
        labels = iota((experts, toks), 0)
        slot_one = slot_ref[0:1, :]
        slot_two = slot_ref[1:2, :]
        gate_one = jnp.sum(jnp.where(labels == routes_ref[0:1, :], probs, 0.0), axis=0, keepdims=True)
        gate_two = jnp.sum(jnp.where(labels == routes_ref[1:2, :], probs, 0.0), axis=0, keepdims=True)
        gate_one = jnp.where(slot_one >= 0, gate_one, 0.0)
        gate_two = jnp.where(slot_two >= 0, gate_two, 0.0)
        which = iota((16, toks), 0)

        def parts(gate):
            high = gate.astype(BF16).astype(F32)
            rest = gate - high
            return jnp.where(which == 0, high, jnp.where(which == 1, rest, 0.0)).astype(BF16)

        kept_ref[0] = parts(gate_one)
        kept_ref[1] = parts(gate_two)
        wide = -(-cap_pad // 128) * 128

        def block(expert, carry):
            spots = iota((wide, toks), 0) + expert * cap_pad
            hot_one = jnp.where(spots == slot_one, 1.0, 0.0)
            hot_two = jnp.where(spots == slot_two, 1.0, 0.0)
            gates = dot_nt(kept_ref[0], hot_one.astype(BF16)) + dot_nt(
                kept_ref[1], hot_two.astype(BF16)
            )
            picked = dot_nn((hot_one + hot_two)[0:cap_pad].astype(BF16), lowered)
            gates = jnp.concatenate([gates, jnp.zeros((16, width - wide), F32)], axis=1)
            row = iota((cap_pad, width), 0)
            picked = jnp.where(
                row == cap_pad - 2, gates[0:1], jnp.where(row == cap_pad - 1, gates[1:2], picked)
            )
            send_ref[expert] = picked.astype(BF16)
            return carry

        lax.fori_loop(0, experts, block, 0)


def phi_parts(v):
    a = jnp.abs(v)
    bell = jnp.exp2((-0.5 * LOG2E) * (v * v))
    t = 1.0 / (1.0 + PHI_RATE * a)
    poly = PHI_FIT[-1] * t
    for part in PHI_FIT[-2::-1]:
        poly = (poly + part) * t
    tail = poly * bell
    return jnp.where(v > 0, 1.0 - tail, tail), bell


def expert_body(
    x_ref,
    u_ref,
    w_ref,
    bias_ref,
    back_ref,
    z_ref,
    hidden_ref,
    grad_ref,
    g_ref,
    gg_ref,
    bin_ref,
    bback_ref,
    gate_scr,
    acc_scr,
    even_ref,
    odd_ref,
):
    step = pl.program_id(0)
    blocks, cap_pad, width = x_ref.shape
    wide = gg_ref.shape[2]
    tile = w_ref.shape[1]

    @pl.when(step == 0)
    def _():
        bback_ref[...] = jnp.zeros_like(bback_ref)

        def block(b, carry):
            tail = x_ref[b, cap_pad - 16 : cap_pad, 0:wide].astype(F32)
            gate_row = tail[14:15] + tail[15:16]
            same = iota((cap_pad, wide), 0) == iota((cap_pad, wide), 1)
            gate = jnp.sum(jnp.where(same, gate_row, 0.0), axis=1, keepdims=True)
            gate_scr[b] = jnp.broadcast_to(gate, (cap_pad, 128))
            rows = u_ref[b].astype(F32)
            made = (rows * gate).astype(BF16)
            g_ref[b] = made
            bback_ref[0:1, :] += jnp.sum(made.astype(F32), axis=0, keepdims=True)
            part = rows * back_ref[...]
            total = part[:, 0:128]
            for i in range(1, width // 128):
                total = total + part[:, i * 128 : (i + 1) * 128]
            acc_scr[b] = total
            return carry

        lax.fori_loop(0, blocks, block, 0)

    bin_ref[...] = jnp.zeros_like(bin_ref)

    def work(b, pre_ref):
        pre = pre_ref[...] + bias_ref[...]
        cdf, bell = phi_parts(pre)
        hidden = pre * cdf
        hidden_ref[b] = hidden.astype(BF16)
        z = z_ref[b].astype(F32)
        part = hidden * z
        total = acc_scr[b]
        for i in range(tile // 128):
            total = total + part[:, i * 128 : (i + 1) * 128]
        acc_scr[b] = total
        slope = cdf + pre * (bell * INV_ROOT_TAU)
        gate = jnp.concatenate([gate_scr[b]] * (tile // 128), axis=1)
        grad = (gate * z * slope).astype(BF16)
        grad_ref[b] = grad
        bin_ref[0:1, :] += jnp.sum(grad.astype(F32), axis=0, keepdims=True)

    even_ref[...] = dot_nn(x_ref[0], w_ref[...])

    def pair(i, carry):
        b = 2 * i
        odd_ref[...] = dot_nn(x_ref[b + 1], w_ref[...])
        work(b, even_ref)
        even_ref[...] = dot_nn(x_ref[jnp.minimum(b + 2, blocks - 1)], w_ref[...])
        work(b + 1, odd_ref)
        return carry

    lax.fori_loop(0, blocks // 2, pair, 0)

    @pl.when(step == pl.num_programs(0) - 1)
    def _():
        def last(b, carry):
            column = jnp.sum(acc_scr[b], axis=1, keepdims=True)
            same = iota((cap_pad, wide), 0) == iota((cap_pad, wide), 1)
            gg_ref[b, 0:1, :] = jnp.sum(jnp.where(same, column, 0.0), axis=0, keepdims=True)
            return carry

        lax.fori_loop(0, blocks, last, 0)


def produce_body(hidden_ref, w_ref, bias_ref, out_ref):
    out_ref[...] = (dot_nn(hidden_ref[...], w_ref[...]) + bias_ref[...]).astype(BF16)


def combine_body(
    experts, kept_ref, slot_ref, routes_ref, probs_ref, residual_ref, back_ref, result_ref
):
    blocks, cap_pad, width = back_ref.shape
    toks = residual_ref.shape[0]
    chunk = row_chunk(toks)
    flat = back_ref[...].reshape(blocks * cap_pad, width)
    labels = iota((experts, toks), 0)
    probs = probs_ref[...]

    def gate(k):
        return jnp.sum(jnp.where(labels == routes_ref[k : k + 1, :], probs, 0.0), axis=0, keepdims=True)

    gate_one, gate_two = gate(0), gate(1)

    def columns(i, carry):
        spot = pl.ds(pl.multiple_of(i * chunk, 16), chunk)
        eye = iota((chunk, toks), 0) + i * chunk == iota((chunk, toks), 1)
        col_one = jnp.sum(jnp.where(eye, gate_one, 0.0), axis=1, keepdims=True)
        col_two = jnp.sum(jnp.where(eye, gate_two, 0.0), axis=1, keepdims=True)
        spots = iota((chunk, blocks * cap_pad), 1)
        hot = jnp.where(spots == kept_ref[spot, 0:1], col_one, 0.0) + jnp.where(
            spots == kept_ref[spot, 1:2], col_two, 0.0
        )
        result_ref[spot, :] = (residual_ref[spot, :] + dot_nn(hot.astype(BF16), flat)).astype(BF16)
        return carry

    lax.fori_loop(0, toks // chunk, columns, 0)


def row_grad_body(
    experts,
    col_ref,
    slot_ref,
    routes_ref,
    probs_ref,
    lowered_ref,
    residual_ref,
    cot_ref,
    gain_ref,
    router_ref,
    back_ref,
    grad_ref,
    low_ref,
    small_ref,
    route_grad_ref,
    logit_ref,
):
    blocks, cap_pad, width = back_ref.shape
    toks = lowered_ref.shape[0]
    chunk = row_chunk(toks)
    labels = iota((experts, toks), 0)
    slot_one = slot_ref[0:1, :]
    slot_two = slot_ref[1:2, :]
    wide = -(-cap_pad // 128) * 128
    gate_one = jnp.zeros((16, toks), F32)
    gate_two = jnp.zeros((16, toks), F32)

    def block(expert, carry):
        one, two = carry
        spots = iota((cap_pad, toks), 0) + expert * cap_pad
        tail = back_ref[expert, cap_pad - 16 : cap_pad, 0:cap_pad]
        hot_one = jnp.where(spots == slot_one, 1.0, 0.0).astype(BF16)
        hot_two = jnp.where(spots == slot_two, 1.0, 0.0).astype(BF16)
        return one + dot_nn(tail, hot_one), two + dot_nn(tail, hot_two)

    gate_one, gate_two = lax.fori_loop(0, experts, block, (gate_one, gate_two))
    gate_one = gate_one[14:15] + gate_one[15:16]
    gate_two = gate_two[14:15] + gate_two[15:16]
    probs = probs_ref[...]
    grad_probs = jnp.where(labels == routes_ref[0:1, :], gate_one, 0.0) + jnp.where(
        labels == routes_ref[1:2, :], gate_two, 0.0
    )
    grad_logits = probs * (grad_probs - jnp.sum(probs * grad_probs, axis=0, keepdims=True))
    grad_logits = grad_logits.astype(BF16)
    route_grad_ref[...] = dot_nn(grad_logits, lowered_ref[...])
    logit_ref[...] = dot_tn(grad_logits, router_ref[...])
    small_ref[...] = jnp.zeros_like(small_ref)
    flat = back_ref[...].reshape(blocks * cap_pad, width)

    def rows(i, carry):
        spot = pl.ds(pl.multiple_of(i * chunk, 16), chunk)
        spots = iota((chunk, blocks * cap_pad), 1)
        hot = jnp.where(
            (spots == col_ref[spot, 0:1]) | (spots == col_ref[spot, 1:2]), 1.0, 0.0
        ).astype(BF16)
        grad = logit_ref[spot, :] + dot_nn(hot, flat)
        scaled, inverse = norm_stats(residual_ref[spot, :])
        small_ref[0:1, :] += jnp.sum(grad * scaled, axis=0, keepdims=True)
        small_ref[1:2, :] += jnp.sum(grad, axis=0, keepdims=True)
        total = cot_ref[spot, :].astype(F32) + norm_grad(grad, scaled, inverse, gain_ref[2:3, :])
        grad_ref[spot, :] = total
        low_ref[spot, :] = total.astype(BF16)
        return carry

    lax.fori_loop(0, toks // chunk, rows, 0)


def backward_body(
    first_group,
    kind_ref,
    up_ref,
    wo_ref,
    qkv_ref,
    mix_ref,
    lse_ref,
    grad_ref,
    do_ref,
    delta_ref,
    dq_ref,
    dk_ref,
    dv_ref,
):
    toks = up_ref.shape[0]
    group = pl.program_id(0) + first_group
    do = dot_nt(up_ref[...], wo_ref[...]).astype(BF16)
    do_ref[...] = do
    both = do.astype(F32) * mix_ref[...].astype(F32)
    high = both.astype(BF16)
    rest = (both - high.astype(F32)).astype(BF16)
    owner = jnp.where(iota((16, LANES), 1) // HEAD_DIM == iota((16, LANES), 0), 1.0, 0.0).astype(BF16)
    delta_ref[...] = dot_nt(owner, high) + dot_nt(owner, rest)
    dq_ref[...] = jnp.zeros_like(dq_ref)
    dk_ref[...] = jnp.zeros_like(dk_ref)
    dv_ref[...] = jnp.zeros_like(dv_ref)

    def attend(kind):
        for start, size, lower, upper, masked in kind_regions(kind, toks):
            bias = region_bias(kind, start, size, lower, upper) if masked else None
            spot = slice(start, start + size)

            def head(h, carry):
                mine = (iota((1, LANES), 1) // HEAD_DIM) == h
                queries = jnp.where(mine, qkv_ref[0, spot, 0:LANES], 0) * jnp.asarray(SCALE, BF16)
                keys_all = qkv_ref[0, spot, LANES : 2 * LANES]
                own = jnp.where(mine, do_ref[spot, :], 0)
                logsum = lse_ref[pl.ds(group * GROUP + h, 1), :][:, spot]
                delta = delta_ref[pl.ds(h, 1), :][:, spot]
                scores = dot_nt(keys_all, queries)
                if bias is not None:
                    scores = scores + bias
                weights = jnp.exp(scores - logsum)
                grad_weights = dot_nt(qkv_ref[0, spot, 2 * LANES : 3 * LANES], own)
                grad_scores = (weights * (grad_weights - delta)).astype(BF16)
                dv_ref[spot, :] += dot_nn(weights.astype(BF16), own)
                dk_ref[spot, :] += dot_nn(grad_scores, queries)
                dq_ref[spot, :] += dot_tn(grad_scores, jnp.where(mine, keys_all, 0))
                return carry

            lax.fori_loop(0, GROUP, head, 0, unroll=2)

    @pl.when(kind_ref[0] == 1)
    def _():
        attend(1)

    @pl.when(kind_ref[0] != 1)
    def _():
        attend(0)

    grad_ref[:, 0:LANES] = (dq_ref[...] * SCALE).astype(BF16)
    grad_ref[:, LANES : 2 * LANES] = dk_ref[...].astype(BF16)
    grad_ref[:, 2 * LANES : 3 * LANES] = dv_ref[...].astype(BF16)


def final_body(groups, *refs):
    packed = refs[0:groups]
    weights = refs[groups : 2 * groups]
    x_ref, gain_ref, up_ref, out_ref, small_ref, acc_ref = refs[2 * groups :]
    toks = x_ref.shape[0]
    chunk = row_chunk(toks)
    total = dot_nt(packed[0][...], weights[0][...])
    for i in range(1, groups):
        total = total + dot_nt(packed[i][...], weights[i][...])
    acc_ref[...] = total
    small_ref[...] = jnp.zeros_like(small_ref)

    def rows(i, carry):
        spot = pl.ds(pl.multiple_of(i * chunk, 16), chunk)
        grad = acc_ref[spot, :]
        scaled, inverse = norm_stats(x_ref[spot, :].astype(F32))
        small_ref[0:1, :] += jnp.sum(grad * scaled, axis=0, keepdims=True)
        small_ref[1:2, :] += jnp.sum(grad, axis=0, keepdims=True)
        out_ref[spot, :] = (
            up_ref[spot, :] + norm_grad(grad, scaled, inverse, gain_ref[0:1, :])
        ).astype(BF16)
        return carry

    lax.fori_loop(0, toks // chunk, rows, 0)


def place_body(core_ref, own_one, other_one, own_two, other_two, out_ref):
    zero = core_ref[0] == 0
    parts = (
        jnp.where(zero, other_one[...], own_one[...]),
        jnp.where(zero, own_two[...], other_two[...]),
        jnp.where(zero, other_two[...], own_two[...]),
    )
    for k, part in enumerate(parts):
        for p in range(3):
            at = (p * 3 + k) * LANES
            out_ref[:, at : at + LANES] = part[:, p * LANES : (p + 1) * LANES].astype(F32)


def place_qkv(pairs, core):
    rows, cols = pairs[0][0].shape
    tile = rows // 3
    return call(
        place_body,
        jax.ShapeDtypeStruct((rows, 3 * cols), F32),
        in_specs=[pl.BlockSpec(memory_space=pltpu.SMEM)]
        + [pl.BlockSpec((tile, cols), lambda i: (i, 0)) for _ in range(4)],
        out_specs=pl.BlockSpec((tile, 3 * cols), lambda i: (i, 0)),
        grid=(3,),
        name="place_qkv",
        cost=(1e6, 20 * rows * cols, 0),
    )(core.astype(jnp.int32).reshape(1), *[part for pair in pairs for part in pair])


def bits_below(count):
    bits, bit = [], 1
    while bit < count:
        bits.append(bit)
        bit *= 2
    return bits


def send_xor(values, axis, size, distance):
    return lax.ppermute(values, axis, [(j, j ^ distance) for j in range(size)])


def trade_sum(parts, axis, size, stride, mine, extra, after):
    def pick(place):
        part = lax.dynamic_index_in_dim(parts, place, 0, keepdims=False)
        return part if extra is None else jnp.concatenate([part, extra], axis=0)

    own = pick(mine)
    if after:
        own = hold(own, after)
    total = own.astype(F32)
    for d in range(1, parts.shape[0]):
        total = total + send_xor(pick(mine ^ d), axis, size, d * stride).astype(F32)
    return total.astype(parts.dtype)


def gather_group(values, axis, size, stride, count, mine):
    got = [values] + [send_xor(values, axis, size, d * stride) for d in range(1, count)]
    for bit in bits_below(count):
        flip = (mine & bit) != 0
        got = [jnp.where(flip, got[k ^ bit], got[k]) for k in range(count)]
    return jnp.concatenate(got, axis=0)


class PairSum:
    def __init__(self, first, second, wide, plan):
        self.width = first.shape[1]
        self.wide = wide
        self.plan = plan
        self.core = lax.axis_index("ex") % 2
        self.keep = jnp.where(self.core == 0, first, second)
        self.value = jnp.where(self.core == 0, second, first)
        self.extra = None
        self.stage = 0

    def step(self, after=()):
        v = self.value
        deep = len(self.plan)
        if self.stage == 0:
            other = send_xor(v, "ex", self.wide, 1)
            keep = hold(self.keep, after) if after else self.keep
            v = (keep.astype(F32) + other.astype(F32)).astype(v.dtype)
        elif self.stage <= deep:
            axis, size, stride, count = self.plan[self.stage - 1]
            mine = (lax.axis_index(axis) // stride) % count
            parts = v.reshape(count, -1, self.width)
            v = trade_sum(parts, axis, size, stride, mine, self.extra, after)
            if self.extra is not None:
                rows = parts.shape[1]
                self.extra = v[rows:]
                v = v[:rows]
        else:
            axis, size, stride, count = self.plan[2 * deep - self.stage]
            mine = (lax.axis_index(axis) // stride) % count
            v = gather_group(v, axis, size, stride, count, mine)
            if after:
                v = hold(v, after)
        self.stage += 1
        self.value = v
        return v

    def left(self):
        return 2 * len(self.plan) + 1 - self.stage

    def finish(self):
        while self.left():
            self.step()
        return self.value, send_xor(self.value, "ex", self.wide, 1)


def local(
    sizes,
    tokens,
    gain_one,
    shift_one,
    w_qkv,
    w_out,
    gain_two,
    shift_two,
    w_router,
    w_in,
    bias_in,
    w_back,
    bias_back,
    cotangent,
    routes,
    priority,
    image_kind,
):
    toks, width = tokens.shape
    experts = w_router.shape[1]
    hidden_units = w_in.shape[2]
    cap = (42 * toks + 20 * experts - 1) // (20 * experts)
    cap_pad = -(-(cap + 2) // 16) * 16
    wide = -(-cap_pad // 128) * 128
    groups = HEADS // GROUP
    first_w, second_w = w_in[0], w_back[0]
    routes_row = routes.T
    router_row = w_router.T
    sds = jax.ShapeDtypeStruct
    dispatched = (experts, cap_pad, width)

    slots, slot_col, up_rows = call(
        functools.partial(prep_body, experts, cap, cap_pad),
        (sds((8, toks), jnp.int32), sds((toks, 128), jnp.int32), sds(dispatched, BF16)),
        cost=(4e9, 6e6, 0),
        name="prep",
    )(routes_row, priority, cotangent)
    up_in = lax.all_to_all(up_rows, "ex", split_axis=0, concat_axis=0, tiled=True)

    gains = jnp.stack([gain_one, shift_one, gain_two, shift_two])
    col = lambda offset: pl.BlockSpec((width, LANES), lambda g: (0, offset * groups + g))
    smem = pl.BlockSpec(memory_space=pltpu.SMEM)
    per_group = lambda: pl.BlockSpec((1, toks, 3 * LANES), lambda g: (g, 0, 0))
    qkv, mix, logsum, low_one, residual, lowered, probs, sent = call(
        functools.partial(forward_body, experts, cap_pad),
        (
            sds((groups, toks, 3 * LANES), BF16),
            sds((toks, width), BF16),
            sds((16, toks), F32),
            sds((toks, width), BF16),
            sds((toks, width), F32),
            sds((toks, width), BF16),
            sds((experts, toks), F32),
            sds(dispatched, BF16),
        ),
        in_specs=[
            smem,
            whole((toks, width)),
            whole((4, width)),
            col(0),
            col(1),
            col(2),
            pl.BlockSpec((LANES, width), lambda g: (g, 0)),
            whole((experts, width)),
            whole((2, toks)),
            whole((8, toks)),
        ],
        out_specs=[
            per_group(),
            pl.BlockSpec((toks, LANES), lambda g: (0, g)),
            whole((16, toks)),
            whole((toks, width)),
            whole((toks, width)),
            whole((toks, width)),
            whole((experts, toks)),
            whole(dispatched),
        ],
        grid=(groups,),
        scratch=[
            pltpu.VMEM((toks, width), F32),
            pltpu.VMEM((toks, LANES), F32),
            pltpu.VMEM((-(-toks // 128) * 128, 128), F32),
            pltpu.VMEM((2, 16, toks), BF16),
        ],
        cost=(10e9, 20e6, 4e6),
        name="attend",
    )(
        image_kind,
        tokens,
        gains,
        w_qkv,
        w_qkv,
        w_qkv,
        w_out,
        router_row,
        routes_row,
        slots,
    )
    rows_in = lax.all_to_all(sent, "ex", split_axis=0, concat_axis=0, tiled=True)

    blocks = rows_in.shape[0]
    flat_up = up_in.reshape(-1, width)
    z = dot_nt(flat_up, second_w).astype(BF16).reshape(blocks, cap_pad, hidden_units)
    tile = 512 if hidden_units % 512 == 0 else 256
    ff = lambda: pl.BlockSpec((blocks, cap_pad, tile), lambda j: (0, 0, j))
    hidden, grad_pre, grad_slots, grad_gate, bin_sum, bback_sum = call(
        expert_body,
        (
            sds((blocks, cap_pad, hidden_units), BF16),
            sds((blocks, cap_pad, hidden_units), BF16),
            sds((blocks, cap_pad, width), BF16),
            sds((blocks, 8, wide), F32),
            sds((8, hidden_units), F32),
            sds((8, width), F32),
        ),
        in_specs=[
            whole((blocks, cap_pad, width)),
            whole((blocks, cap_pad, width)),
            pl.BlockSpec((width, tile), lambda j: (0, j)),
            pl.BlockSpec((1, tile), lambda j: (0, j)),
            whole((1, width)),
            ff(),
        ],
        out_specs=[
            ff(),
            ff(),
            whole((blocks, cap_pad, width)),
            whole((blocks, 8, wide)),
            pl.BlockSpec((8, tile), lambda j: (0, j)),
            whole((8, width)),
        ],
        grid=(hidden_units // tile,),
        scratch=[
            pltpu.VMEM((blocks, cap_pad, 128), F32),
            pltpu.VMEM((blocks, cap_pad, 128), F32),
            pltpu.VMEM((cap_pad, tile), F32),
            pltpu.VMEM((cap_pad, tile), F32),
        ],
        cost=(8e9, 40e6, 10e6),
        name="expert",
    )(rows_in, up_in, first_w, bias_in, bias_back, z)
    flat_rows = rows_in.reshape(-1, width)
    flat_hidden = hidden.reshape(-1, hidden_units)
    flat_pre = grad_pre.reshape(-1, hidden_units)
    flat_slots = grad_slots.reshape(-1, width)

    gate_row = grad_gate[:, 0:1, :]
    gate_high = gate_row.astype(BF16).astype(F32)
    gate_rows = jnp.concatenate([gate_high, gate_row - gate_high], axis=1)
    gate_rows = jnp.pad(gate_rows, ((0, 0), (cap_pad - 2, 0), (0, width - wide)))
    first_grad = dot_tn(flat_rows, flat_pre).astype(BF16)
    first_out = lax.psum_scatter(first_grad, "rep", scatter_dimension=0, tiled=True).astype(F32)
    flat_pre = hold(flat_pre, [first_grad])
    grad_rows = dot_nt(flat_pre, first_w).reshape(blocks, cap_pad, width)
    tail = lax.broadcasted_iota(jnp.int32, (blocks, cap_pad, width), 1) >= cap_pad - 2
    grad_rows = jnp.where(tail, gate_rows, grad_rows).astype(BF16)
    grad_back = lax.all_to_all(grad_rows, "ex", split_axis=0, concat_axis=0, tiled=True)

    flat_slots = hold(flat_slots, [first_grad, grad_rows])
    second_grad = dot_tn(flat_hidden, flat_slots).astype(BF16)
    second_out = lax.psum_scatter(second_grad, "rep", scatter_dimension=0, tiled=True).astype(F32)
    flat_hidden = hold(flat_hidden, [second_grad])
    tall = blocks * cap_pad // 4
    produced = call(
        produce_body,
        sds((blocks * cap_pad, width), BF16),
        in_specs=[
            pl.BlockSpec((tall, hidden_units), lambda i: (i, 0)),
            whole((hidden_units, width)),
            whole((1, width)),
        ],
        out_specs=pl.BlockSpec((tall, width), lambda i: (i, 0)),
        grid=(4,),
        cost=(1, 1, 0),
        name="produce",
    )(flat_hidden, second_w, bias_back)
    returned = lax.all_to_all(
        produced.reshape(blocks, cap_pad, width), "ex", split_axis=0, concat_axis=0, tiled=True
    )

    reps = sizes["rep"]
    grad_residual, grad_branch, small_two, route_grad = call(
        functools.partial(row_grad_body, experts),
        (
            sds((toks, width), F32),
            sds((toks, width), BF16),
            sds((8, width), F32),
            sds((experts, width), F32),
        ),
        scratch=[pltpu.VMEM((toks, width), F32)],
        cost=(1, 1, 0),
        name="row_grad",
        after=[first_grad, second_grad, produced],
    )(
        slot_col,
        slots,
        routes_row,
        probs,
        lowered,
        residual,
        cotangent,
        gains,
        router_row,
        grad_back,
    )
    out_part = dot_tn(mix, grad_branch).astype(BF16)
    sums = []

    def advance():
        return [s.step() for s in sums]

    reps = sizes["rep"]
    plane_hops = [("ex", sizes["ex"], bit, 2) for bit in bits_below(sizes["ex"])[1:]]
    rep_hops = [("rep", reps, bit, 2) for bit in bits_below(reps)]
    packed_grads = []
    parts = [out_part]
    waiting = [out_part]
    for g in range(groups):
        if g == 1:
            waiting.append(returned)
        packed = call(
            functools.partial(backward_body, g),
            sds((toks, 3 * LANES), BF16),
            in_specs=[
                smem,
                whole((toks, width)),
                pl.BlockSpec((LANES, width), lambda i, g=g: (g, 0)),
                pl.BlockSpec((1, toks, 3 * LANES), lambda i, g=g: (g, 0, 0)),
                pl.BlockSpec((toks, LANES), lambda i, g=g: (0, g)),
                whole((16, toks)),
            ],
            out_specs=whole((toks, 3 * LANES)),
            grid=(1,),
            scratch=[
                pltpu.VMEM((toks, LANES), BF16),
                pltpu.VMEM((16, toks), F32),
                pltpu.VMEM((toks, LANES), F32),
                pltpu.VMEM((toks, LANES), F32),
                pltpu.VMEM((toks, LANES), F32),
            ],
            cost=(8e9, 6e6, 2e6),
            name="attend_back_" + "abcdef"[g],
            after=waiting,
        )(image_kind, grad_branch, w_out, qkv, mix, logsum)
        packed_grads.append(packed)
        waiting = advance()
        parts.append(dot_tn(low_one, packed).astype(BF16))
        if len(parts) == 2:
            order = plane_hops[:: 1 if g == 0 else -1]
            sums.append(PairSum(*parts, sizes["ex"], order + rep_hops))
            parts = []
            waiting.append(sums[-1].value)
        else:
            waiting.append(parts[-1])

    w_groups = [
        jnp.concatenate(
            [w_qkv[:, (p * groups + g) * LANES : (p * groups + g + 1) * LANES] for p in range(3)],
            axis=1,
        )
        for g in range(groups)
    ]
    grad_tokens, small_one = call(
        functools.partial(final_body, groups),
        (sds((toks, width), BF16), sds((8, width), F32)),
        scratch=[pltpu.VMEM((toks, width), F32)],
        cost=(3e9, 14e6, 0),
        name="final",
        after=[sums[1].value],
    )(*packed_grads, *w_groups, tokens, gains, grad_residual)
    ahead, last = sums
    small = jnp.concatenate([small_one[0:2], small_two[0:2], route_grad], axis=0)
    small_rows = small.shape[0]
    added = last.step([small_one])
    last.extra = jnp.pad(small, ((0, -small_rows % 16), (0, 0))).astype(BF16)
    result = call(
        functools.partial(combine_body, experts),
        sds((toks, width), BF16),
        cost=(2e9, 8e6, 0),
        name="combine",
        after=[added, ahead.value, first_out],
    )(slot_col, slots, routes_row, probs, residual, returned)
    ahead.step([result])
    last.step([result])
    bin_sum = hold(bin_sum, [result])
    while ahead.stage < len(plane_hops) + 1:
        ahead.step()
        last.step()
    bias_rows = jnp.concatenate([bin_sum[0].reshape(-1, width), bback_sum[0:1]], axis=0)
    bias_rows = jnp.pad(bias_rows, ((0, -bias_rows.shape[0] % 16), (0, 0))).astype(BF16)
    ahead.extra = bias_rows
    while last.left() > 1:
        if ahead.left():
            ahead.step([second_out] if ahead.left() == 1 else ())
        last.step()
    last.step()
    pairs = [ahead.finish(), last.finish()]
    rank = lax.axis_index("rep")
    bias_sum = ahead.extra.astype(F32)
    bin_out = bias_sum[: hidden_units // width].reshape(-1)
    bin_out = lax.dynamic_slice_in_dim(bin_out, rank * (hidden_units // reps), hidden_units // reps)
    bback_out = lax.dynamic_slice_in_dim(
        bias_sum[hidden_units // width], rank * (width // reps), width // reps
    )
    small = last.extra.astype(F32)
    small = small + send_xor(small, "ex", sizes["ex"], 1)
    core = lax.axis_index("ex") % 2
    out_grad = jnp.where(core == 0, *pairs[0]).astype(F32)
    qkv_grad = place_qkv(pairs, core)
    return (
        result,
        grad_tokens,
        small[0],
        small[1],
        qkv_grad,
        out_grad,
        small[2],
        small[3],
        small[4:small_rows].T,
        first_out[None],
        bin_out[None],
        second_out[None],
        bback_out[None],
    )


def solution(mesh):
    both = ("rep", "ex")
    in_specs = (
        P(both, None),
        P(),
        P(),
        P(),
        P(),
        P(),
        P(),
        P(),
        P("ex", None, None),
        P("ex", None),
        P("ex", None, None),
        P("ex", None),
        P(both, None),
        P(both, None),
        P(both, None),
        P(both),
    )
    out_specs = (
        P(both, None),
        P(both, None),
        P(),
        P(),
        P(),
        P(),
        P(),
        P(),
        P(),
        P("ex", "rep", None),
        P("ex", "rep"),
        P("ex", "rep", None),
        P("ex", "rep"),
    )
    return jax.shard_map(
        functools.partial(local, dict(mesh.shape)),
        mesh=mesh,
        in_specs=in_specs,
        out_specs=out_specs,
        check_vma=False,
    )
```

```python
import functools

import jax
import jax.numpy as jnp
from jax import lax
from jax.experimental import pallas as pl
from jax.experimental.pallas import tpu as pltpu
from jax.sharding import PartitionSpec as P

HEADS = 12
HEAD_DIM = 64
PATCH_S = 196
PATCH_L = 576
GROUP = 4
LANES = GROUP * HEAD_DIM

EPS = 1e-06
NEG = -1e30
SCALE = HEAD_DIM ** (-0.5)
LOG2E = 1.4426950408889634
INV_ROOT_TAU = 0.3989422804014327
PHI_RATE = 0.36
PHI_FIT = (
    0.14371304535439455,
    0.14177245494035942,
    0.1397192591115954,
    0.026549327576509053,
    0.18095403137785818,
    -0.17976471959279186,
    0.047056297922502474,
)
F32 = jnp.float32
BF16 = jnp.bfloat16


def dot_nn(a, b):
    return lax.dot_general(a, b, (((1,), (0,)), ((), ())), preferred_element_type=F32)


def dot_nt(a, b):
    return lax.dot_general(a, b, (((1,), (1,)), ((), ())), preferred_element_type=F32)


def dot_tn(a, b):
    return lax.dot_general(a, b, (((0,), (0,)), ((), ())), preferred_element_type=F32)


def iota(shape, dim):
    return lax.broadcasted_iota(jnp.int32, shape, dim)


def call(
    body, out_shape, in_specs=None, out_specs=None, grid=None, scratch=(), cost=None, name=None, after=()
):
    args = dict(out_shape=out_shape, scratch_shapes=list(scratch), name=name)
    if grid is not None:
        args["grid"] = grid
    if out_specs is not None:
        args["out_specs"] = out_specs
    if cost is not None:
        args["cost_estimate"] = pl.CostEstimate(
            flops=int(cost[0]), bytes_accessed=int(cost[1]), transcendentals=int(cost[2])
        )

    def run(*operands):
        count = len(operands)
        specs = in_specs or [pl.BlockSpec(memory_space=pltpu.VMEM)] * count
        specs = list(specs) + [pl.BlockSpec(memory_space=pl.ANY)] * len(after)

        def inner(*refs):
            body(*refs[:count], *refs[count + len(after) :])

        return pl.pallas_call(
            inner,
            in_specs=specs,
            compiler_params=pltpu.CompilerParams(vmem_limit_bytes=60 * 1024 * 1024),
            **args,
        )(*operands, *after)

    return run


def hold(values, after):
    def nothing(*refs):
        pass

    any_spec = pl.BlockSpec(memory_space=pl.ANY)
    return pl.pallas_call(
        nothing,
        out_shape=jax.ShapeDtypeStruct(values.shape, values.dtype),
        in_specs=[any_spec] * (1 + len(after)),
        out_specs=any_spec,
        input_output_aliases={0: 0},
        name="hold",
    )(values, *after)


def whole(shape, memory_space=None):
    zeros = (0,) * len(shape)
    if memory_space is not None:
        return pl.BlockSpec(shape, lambda *_: zeros, memory_space=memory_space)
    return pl.BlockSpec(shape, lambda *_: zeros)


def norm_stats(values):
    average = jnp.mean(values, axis=-1, keepdims=True)
    centered = values - average
    variance = jnp.mean(centered * centered, axis=-1, keepdims=True)
    inverse = lax.rsqrt(variance + EPS)
    return centered * inverse, inverse


def norm_grad(grad, scaled, inverse, gain):
    through = grad * gain
    first = jnp.mean(through, axis=-1, keepdims=True)
    second = jnp.mean(through * scaled, axis=-1, keepdims=True)
    return inverse * (through - first - scaled * second)


def row_chunk(rows):
    for size in (112, 128, 64, 48, 32, 16):
        if rows % size == 0:
            return size
    return rows


def prep_body(experts, cap, cap_pad, routes_ref, prio_ref, cot_ref, slot_ref, col_ref, out_ref):
    toks = cot_ref.shape[0]
    prio = prio_ref[...].astype(F32)
    prio_col = jnp.sum(
        jnp.where(iota((toks, toks), 0) == iota((toks, toks), 1), prio, 0.0), axis=1, keepdims=True
    )
    below = jnp.where(prio_col < prio, 1.0, 0.0).astype(BF16)
    labels = iota((experts, toks), 0)
    first = routes_ref[0:1, :]
    second = routes_ref[1:2, :]
    hot_one = jnp.where(labels == first, 1.0, 0.0)
    hot_two = jnp.where(labels == second, 1.0, 0.0)
    count_one = dot_nn(hot_one.astype(BF16), below)
    count_two = dot_nn(hot_two.astype(BF16), below)
    total_one = jnp.sum(hot_one, axis=1, keepdims=True)
    place_one = jnp.sum(hot_one * count_one, axis=0, keepdims=True)
    place_two = jnp.sum(hot_two * (count_two + total_one), axis=0, keepdims=True)
    slot_one = jnp.where(
        place_one < cap, first * cap_pad + place_one.astype(jnp.int32), -1
    )
    slot_two = jnp.where(
        place_two < cap, second * cap_pad + place_two.astype(jnp.int32), -1
    )
    slot_ref[0:1, :] = slot_one
    slot_ref[1:2, :] = slot_two
    eye = iota((toks, toks), 0) == iota((toks, toks), 1)
    col_one = jnp.sum(jnp.where(eye, slot_one, 0), axis=1, keepdims=True)
    col_two = jnp.sum(jnp.where(eye, slot_two, 0), axis=1, keepdims=True)
    lane = iota((toks, 128), 1)
    col_ref[...] = jnp.where(lane == 0, col_one, jnp.where(lane == 1, col_two, -1))

    def block(expert, carry):
        spots = iota((cap_pad, toks), 0) + expert * cap_pad
        hot = jnp.where((spots == slot_one) | (spots == slot_two), 1.0, 0.0).astype(BF16)
        out_ref[expert] = dot_nn(hot, cot_ref[...]).astype(BF16)
        return carry

    lax.fori_loop(0, experts, block, 0)


def region_bias(kind, start, size, lower, upper, by_rows=True):
    first = iota((size, size), 0) + start
    second = iota((size, size), 1) + start
    if kind == 1:
        seg = lambda p: jnp.where(p < PATCH_L, 0, jnp.where(p < PATCH_L + PATCH_S, 1, 2))
    else:
        seg = lambda p: (
            jnp.where(p >= PATCH_S, 1, 0)
            + jnp.where(p >= 2 * PATCH_S, 1, 0)
            + jnp.where(p >= 3 * PATCH_S, 1, 0)
        )
    linked = seg(first) == seg(second)
    inside = (first >= lower) & (first < upper)
    return jnp.where(linked & inside, 0.0, NEG)


def kind_regions(kind, toks):
    if kind == 1:
        return ((0, PATCH_L, 0, PATCH_L, False), (PATCH_L, toks - PATCH_L, PATCH_L, toks, True))
    half = 2 * PATCH_S
    size = -(-half // 16) * 16
    begin = toks - size
    return ((0, size, 0, half, True), (begin, size, half, toks, True))


def forward_body(
    experts,
    cap_pad,
    kind_ref,
    x_ref,
    gains_ref,
    wq_ref,
    wk_ref,
    wv_ref,
    wo_ref,
    router_ref,
    routes_ref,
    slot_ref,
    qkv_ref,
    mix_ref,
    lse_ref,
    low_ref,
    residual_ref,
    lowered_ref,
    probs_ref,
    send_ref,
    acc_ref,
    out_ref,
    lse_scr,
    kept_ref,
):
    step = pl.program_id(0)
    steps = pl.num_programs(0)
    toks, width = x_ref.shape
    chunk = row_chunk(toks)

    @pl.when(step == 0)
    def _():
        def rows(i, carry):
            spot = pl.ds(pl.multiple_of(i * chunk, 16), chunk)
            scaled, _ = norm_stats(x_ref[spot, :].astype(F32))
            low_ref[spot, :] = (scaled * gains_ref[0:1, :] + gains_ref[1:2, :]).astype(BF16)
            return carry

        lax.fori_loop(0, toks // chunk, rows, 0)
        lse_scr[...] = jnp.zeros_like(lse_scr)

    low = low_ref[...]
    qkv_ref[0, :, 0:LANES] = dot_nn(low, wq_ref[...]).astype(BF16)
    qkv_ref[0, :, LANES : 2 * LANES] = dot_nn(low, wk_ref[...]).astype(BF16)
    qkv_ref[0, :, 2 * LANES : 3 * LANES] = dot_nn(low, wv_ref[...]).astype(BF16)

    def attend(kind):
        for start, size, lower, upper, masked in kind_regions(kind, toks):
            bias = region_bias(kind, start, size, lower, upper) if masked else None
            spot = slice(start, start + size)
            out_ref[lower:upper, :] = jnp.zeros((upper - lower, LANES), F32)

            def head(h, carry):
                mine = (iota((1, LANES), 1) // HEAD_DIM) == h
                queries = jnp.where(mine, qkv_ref[0, spot, 0:LANES], 0) * jnp.asarray(SCALE, BF16)
                scores = dot_nt(queries, qkv_ref[0, spot, LANES : 2 * LANES])
                if bias is not None:
                    scores = scores + bias
                top = jnp.max(scores, axis=-1, keepdims=True)
                weights = jnp.exp(scores - top)
                total = jnp.sum(weights, axis=-1, keepdims=True)
                values = jnp.where(mine, qkv_ref[0, spot, 2 * LANES : 3 * LANES], 0)
                mixed = dot_nn(weights.astype(BF16), values) * (1.0 / total)
                logsum = top + jnp.log(total)
                cut = slice(lower - start, upper - start)
                out_ref[lower:upper, :] += mixed[cut]
                lane = iota((upper - lower, 128), 1) == step * GROUP + h
                lse_scr[lower:upper, :] = jnp.where(lane, logsum[cut], lse_scr[lower:upper, :])
                return carry

            lax.fori_loop(0, GROUP, head, 0, unroll=4)

    @pl.when(kind_ref[0] == 1)
    def _():
        attend(1)

    @pl.when(kind_ref[0] != 1)
    def _():
        attend(0)

    mix = out_ref[...].astype(BF16)
    mix_ref[...] = mix
    branch = dot_nn(mix, wo_ref[...])

    @pl.when(step == 0)
    def _():
        acc_ref[...] = x_ref[...].astype(F32) + branch

    @pl.when(step > 0)
    def _():
        acc_ref[...] += branch

    @pl.when(step == steps - 1)
    def _():
        lse_ref[...] = lse_scr[...].T[0 : lse_ref.shape[0], 0:toks]

        def rows(i, carry):
            spot = pl.ds(pl.multiple_of(i * chunk, 16), chunk)
            residual = acc_ref[spot, :]
            residual_ref[spot, :] = residual
            scaled, _ = norm_stats(residual)
            lowered_ref[spot, :] = (scaled * gains_ref[2:3, :] + gains_ref[3:4, :]).astype(BF16)
            return carry

        lax.fori_loop(0, toks // chunk, rows, 0)
        lowered = lowered_ref[...]
        logits = dot_nt(router_ref[...], lowered)
        top = jnp.max(logits, axis=0, keepdims=True)
        raised = jnp.exp(logits - top)
        probs = raised / jnp.sum(raised, axis=0, keepdims=True)
        probs_ref[...] = probs
        labels = iota((experts, toks), 0)
        slot_one = slot_ref[0:1, :]
        slot_two = slot_ref[1:2, :]
        gate_one = jnp.sum(jnp.where(labels == routes_ref[0:1, :], probs, 0.0), axis=0, keepdims=True)
        gate_two = jnp.sum(jnp.where(labels == routes_ref[1:2, :], probs, 0.0), axis=0, keepdims=True)
        gate_one = jnp.where(slot_one >= 0, gate_one, 0.0)
        gate_two = jnp.where(slot_two >= 0, gate_two, 0.0)
        which = iota((16, toks), 0)

        def parts(gate):
            high = gate.astype(BF16).astype(F32)
            rest = gate - high
            return jnp.where(which == 0, high, jnp.where(which == 1, rest, 0.0)).astype(BF16)

        kept_ref[0] = parts(gate_one)
        kept_ref[1] = parts(gate_two)
        wide = -(-cap_pad // 128) * 128

        def block(expert, carry):
            spots = iota((wide, toks), 0) + expert * cap_pad
            hot_one = jnp.where(spots == slot_one, 1.0, 0.0)
            hot_two = jnp.where(spots == slot_two, 1.0, 0.0)
            gates = dot_nt(kept_ref[0], hot_one.astype(BF16)) + dot_nt(
                kept_ref[1], hot_two.astype(BF16)
            )
            picked = dot_nn((hot_one + hot_two)[0:cap_pad].astype(BF16), lowered)
            gates = jnp.concatenate([gates, jnp.zeros((16, width - wide), F32)], axis=1)
            row = iota((cap_pad, width), 0)
            picked = jnp.where(
                row == cap_pad - 2, gates[0:1], jnp.where(row == cap_pad - 1, gates[1:2], picked)
            )
            send_ref[expert] = picked.astype(BF16)
            return carry

        lax.fori_loop(0, experts, block, 0)


def phi_parts(v):
    a = jnp.abs(v)
    bell = jnp.exp2((-0.5 * LOG2E) * (v * v))
    t = 1.0 / (1.0 + PHI_RATE * a)
    poly = PHI_FIT[-1] * t
    for part in PHI_FIT[-2::-1]:
        poly = (poly + part) * t
    tail = poly * bell
    return jnp.where(v > 0, 1.0 - tail, tail), bell


def expert_body(
    x_ref,
    u_ref,
    w_ref,
    bias_ref,
    back_ref,
    z_ref,
    hidden_ref,
    grad_ref,
    g_ref,
    gg_ref,
    bin_ref,
    bback_ref,
    gate_scr,
    acc_scr,
    even_ref,
    odd_ref,
):
    step = pl.program_id(0)
    blocks, cap_pad, width = x_ref.shape
    wide = gg_ref.shape[2]
    tile = w_ref.shape[1]

    @pl.when(step == 0)
    def _():
        bback_ref[...] = jnp.zeros_like(bback_ref)

        def block(b, carry):
            tail = x_ref[b, cap_pad - 16 : cap_pad, 0:wide].astype(F32)
            gate_row = tail[14:15] + tail[15:16]
            same = iota((cap_pad, wide), 0) == iota((cap_pad, wide), 1)
            gate = jnp.sum(jnp.where(same, gate_row, 0.0), axis=1, keepdims=True)
            gate_scr[b] = jnp.broadcast_to(gate, (cap_pad, 128))
            rows = u_ref[b].astype(F32)
            made = (rows * gate).astype(BF16)
            g_ref[b] = made
            bback_ref[0:1, :] += jnp.sum(made.astype(F32), axis=0, keepdims=True)
            part = rows * back_ref[...]
            total = part[:, 0:128]
            for i in range(1, width // 128):
                total = total + part[:, i * 128 : (i + 1) * 128]
            acc_scr[b] = total
            return carry

        lax.fori_loop(0, blocks, block, 0)

    bin_ref[...] = jnp.zeros_like(bin_ref)

    def work(b, pre_ref):
        pre = pre_ref[...] + bias_ref[...]
        cdf, bell = phi_parts(pre)
        hidden = pre * cdf
        hidden_ref[b] = hidden.astype(BF16)
        z = z_ref[b].astype(F32)
        part = hidden * z
        total = acc_scr[b]
        for i in range(tile // 128):
            total = total + part[:, i * 128 : (i + 1) * 128]
        acc_scr[b] = total
        slope = cdf + pre * (bell * INV_ROOT_TAU)
        gate = jnp.concatenate([gate_scr[b]] * (tile // 128), axis=1)
        grad = (gate * z * slope).astype(BF16)
        grad_ref[b] = grad
        bin_ref[0:1, :] += jnp.sum(grad.astype(F32), axis=0, keepdims=True)

    even_ref[...] = dot_nn(x_ref[0], w_ref[...])

    def pair(i, carry):
        b = 2 * i
        odd_ref[...] = dot_nn(x_ref[b + 1], w_ref[...])
        work(b, even_ref)
        even_ref[...] = dot_nn(x_ref[jnp.minimum(b + 2, blocks - 1)], w_ref[...])
        work(b + 1, odd_ref)
        return carry

    lax.fori_loop(0, blocks // 2, pair, 0)

    @pl.when(step == pl.num_programs(0) - 1)
    def _():
        def last(b, carry):
            column = jnp.sum(acc_scr[b], axis=1, keepdims=True)
            same = iota((cap_pad, wide), 0) == iota((cap_pad, wide), 1)
            gg_ref[b, 0:1, :] = jnp.sum(jnp.where(same, column, 0.0), axis=0, keepdims=True)
            return carry

        lax.fori_loop(0, blocks, last, 0)


def produce_body(hidden_ref, w_ref, bias_ref, out_ref):
    out_ref[...] = (dot_nn(hidden_ref[...], w_ref[...]) + bias_ref[...]).astype(BF16)


def combine_body(
    experts, kept_ref, slot_ref, routes_ref, probs_ref, residual_ref, back_ref, result_ref
):
    blocks, cap_pad, width = back_ref.shape
    toks = residual_ref.shape[0]
    chunk = row_chunk(toks)
    flat = back_ref[...].reshape(blocks * cap_pad, width)
    labels = iota((experts, toks), 0)
    probs = probs_ref[...]

    def gate(k):
        return jnp.sum(jnp.where(labels == routes_ref[k : k + 1, :], probs, 0.0), axis=0, keepdims=True)

    gate_one, gate_two = gate(0), gate(1)

    def columns(i, carry):
        spot = pl.ds(pl.multiple_of(i * chunk, 16), chunk)
        eye = iota((chunk, toks), 0) + i * chunk == iota((chunk, toks), 1)
        col_one = jnp.sum(jnp.where(eye, gate_one, 0.0), axis=1, keepdims=True)
        col_two = jnp.sum(jnp.where(eye, gate_two, 0.0), axis=1, keepdims=True)
        spots = iota((chunk, blocks * cap_pad), 1)
        hot = jnp.where(spots == kept_ref[spot, 0:1], col_one, 0.0) + jnp.where(
            spots == kept_ref[spot, 1:2], col_two, 0.0
        )
        result_ref[spot, :] = (residual_ref[spot, :] + dot_nn(hot.astype(BF16), flat)).astype(BF16)
        return carry

    lax.fori_loop(0, toks // chunk, columns, 0)


def row_grad_body(
    experts,
    col_ref,
    slot_ref,
    routes_ref,
    probs_ref,
    lowered_ref,
    residual_ref,
    cot_ref,
    gain_ref,
    router_ref,
    back_ref,
    grad_ref,
    low_ref,
    small_ref,
    route_grad_ref,
    logit_ref,
):
    blocks, cap_pad, width = back_ref.shape
    toks = lowered_ref.shape[0]
    chunk = row_chunk(toks)
    labels = iota((experts, toks), 0)
    slot_one = slot_ref[0:1, :]
    slot_two = slot_ref[1:2, :]
    wide = -(-cap_pad // 128) * 128
    gate_one = jnp.zeros((16, toks), F32)
    gate_two = jnp.zeros((16, toks), F32)

    def block(expert, carry):
        one, two = carry
        spots = iota((cap_pad, toks), 0) + expert * cap_pad
        tail = back_ref[expert, cap_pad - 16 : cap_pad, 0:cap_pad]
        hot_one = jnp.where(spots == slot_one, 1.0, 0.0).astype(BF16)
        hot_two = jnp.where(spots == slot_two, 1.0, 0.0).astype(BF16)
        return one + dot_nn(tail, hot_one), two + dot_nn(tail, hot_two)

    gate_one, gate_two = lax.fori_loop(0, experts, block, (gate_one, gate_two))
    gate_one = gate_one[14:15] + gate_one[15:16]
    gate_two = gate_two[14:15] + gate_two[15:16]
    probs = probs_ref[...]
    grad_probs = jnp.where(labels == routes_ref[0:1, :], gate_one, 0.0) + jnp.where(
        labels == routes_ref[1:2, :], gate_two, 0.0
    )
    grad_logits = probs * (grad_probs - jnp.sum(probs * grad_probs, axis=0, keepdims=True))
    grad_logits = grad_logits.astype(BF16)
    route_grad_ref[...] = dot_nn(grad_logits, lowered_ref[...])
    logit_ref[...] = dot_tn(grad_logits, router_ref[...])
    small_ref[...] = jnp.zeros_like(small_ref)
    flat = back_ref[...].reshape(blocks * cap_pad, width)

    def rows(i, carry):
        spot = pl.ds(pl.multiple_of(i * chunk, 16), chunk)
        spots = iota((chunk, blocks * cap_pad), 1)
        hot = jnp.where(
            (spots == col_ref[spot, 0:1]) | (spots == col_ref[spot, 1:2]), 1.0, 0.0
        ).astype(BF16)
        grad = logit_ref[spot, :] + dot_nn(hot, flat)
        scaled, inverse = norm_stats(residual_ref[spot, :])
        small_ref[0:1, :] += jnp.sum(grad * scaled, axis=0, keepdims=True)
        small_ref[1:2, :] += jnp.sum(grad, axis=0, keepdims=True)
        total = cot_ref[spot, :].astype(F32) + norm_grad(grad, scaled, inverse, gain_ref[2:3, :])
        grad_ref[spot, :] = total
        low_ref[spot, :] = total.astype(BF16)
        return carry

    lax.fori_loop(0, toks // chunk, rows, 0)


def backward_body(
    first_group,
    kind_ref,
    up_ref,
    wo_ref,
    qkv_ref,
    mix_ref,
    lse_ref,
    grad_ref,
    do_ref,
    delta_ref,
    dq_ref,
    dk_ref,
    dv_ref,
):
    toks = up_ref.shape[0]
    group = pl.program_id(0) + first_group
    do = dot_nt(up_ref[...], wo_ref[...]).astype(BF16)
    do_ref[...] = do
    both = do.astype(F32) * mix_ref[...].astype(F32)
    high = both.astype(BF16)
    rest = (both - high.astype(F32)).astype(BF16)
    owner = jnp.where(iota((16, LANES), 1) // HEAD_DIM == iota((16, LANES), 0), 1.0, 0.0).astype(BF16)
    delta_ref[...] = dot_nt(owner, high) + dot_nt(owner, rest)
    dq_ref[...] = jnp.zeros_like(dq_ref)
    dk_ref[...] = jnp.zeros_like(dk_ref)
    dv_ref[...] = jnp.zeros_like(dv_ref)

    def attend(kind):
        for start, size, lower, upper, masked in kind_regions(kind, toks):
            bias = region_bias(kind, start, size, lower, upper) if masked else None
            spot = slice(start, start + size)

            def head(h, carry):
                mine = (iota((1, LANES), 1) // HEAD_DIM) == h
                queries = jnp.where(mine, qkv_ref[0, spot, 0:LANES], 0) * jnp.asarray(SCALE, BF16)
                keys_all = qkv_ref[0, spot, LANES : 2 * LANES]
                own = jnp.where(mine, do_ref[spot, :], 0)
                logsum = lse_ref[pl.ds(group * GROUP + h, 1), :][:, spot]
                delta = delta_ref[pl.ds(h, 1), :][:, spot]
                scores = dot_nt(keys_all, queries)
                if bias is not None:
                    scores = scores + bias
                weights = jnp.exp(scores - logsum)
                grad_weights = dot_nt(qkv_ref[0, spot, 2 * LANES : 3 * LANES], own)
                grad_scores = (weights * (grad_weights - delta)).astype(BF16)
                dv_ref[spot, :] += dot_nn(weights.astype(BF16), own)
                dk_ref[spot, :] += dot_nn(grad_scores, queries)
                dq_ref[spot, :] += dot_tn(grad_scores, jnp.where(mine, keys_all, 0))
                return carry

            lax.fori_loop(0, GROUP, head, 0, unroll=2)

    @pl.when(kind_ref[0] == 1)
    def _():
        attend(1)

    @pl.when(kind_ref[0] != 1)
    def _():
        attend(0)

    grad_ref[:, 0:LANES] = (dq_ref[...] * SCALE).astype(BF16)
    grad_ref[:, LANES : 2 * LANES] = dk_ref[...].astype(BF16)
    grad_ref[:, 2 * LANES : 3 * LANES] = dv_ref[...].astype(BF16)


def final_body(groups, *refs):
    packed = refs[0:groups]
    weights = refs[groups : 2 * groups]
    x_ref, gain_ref, up_ref, out_ref, small_ref, acc_ref = refs[2 * groups :]
    toks = x_ref.shape[0]
    chunk = row_chunk(toks)
    total = dot_nt(packed[0][...], weights[0][...])
    for i in range(1, groups):
        total = total + dot_nt(packed[i][...], weights[i][...])
    acc_ref[...] = total
    small_ref[...] = jnp.zeros_like(small_ref)

    def rows(i, carry):
        spot = pl.ds(pl.multiple_of(i * chunk, 16), chunk)
        grad = acc_ref[spot, :]
        scaled, inverse = norm_stats(x_ref[spot, :].astype(F32))
        small_ref[0:1, :] += jnp.sum(grad * scaled, axis=0, keepdims=True)
        small_ref[1:2, :] += jnp.sum(grad, axis=0, keepdims=True)
        out_ref[spot, :] = (
            up_ref[spot, :] + norm_grad(grad, scaled, inverse, gain_ref[0:1, :])
        ).astype(BF16)
        return carry

    lax.fori_loop(0, toks // chunk, rows, 0)


def place_body(core_ref, own_one, other_one, own_two, other_two, out_ref):
    zero = core_ref[0] == 0
    parts = (
        jnp.where(zero, other_one[...], own_one[...]),
        jnp.where(zero, own_two[...], other_two[...]),
        jnp.where(zero, other_two[...], own_two[...]),
    )
    for k, part in enumerate(parts):
        for p in range(3):
            at = (p * 3 + k) * LANES
            out_ref[:, at : at + LANES] = part[:, p * LANES : (p + 1) * LANES].astype(F32)


def place_qkv(pairs, core):
    rows, cols = pairs[0][0].shape
    tile = rows // 3
    return call(
        place_body,
        jax.ShapeDtypeStruct((rows, 3 * cols), F32),
        in_specs=[pl.BlockSpec(memory_space=pltpu.SMEM)]
        + [pl.BlockSpec((tile, cols), lambda i: (i, 0)) for _ in range(4)],
        out_specs=pl.BlockSpec((tile, 3 * cols), lambda i: (i, 0)),
        grid=(3,),
        name="place_qkv",
        cost=(1e6, 20 * rows * cols, 0),
    )(core.astype(jnp.int32).reshape(1), *[part for pair in pairs for part in pair])


def bits_below(count):
    bits, bit = [], 1
    while bit < count:
        bits.append(bit)
        bit *= 2
    return bits


def send_xor(values, axis, size, distance):
    return lax.ppermute(values, axis, [(j, j ^ distance) for j in range(size)])


def trade_sum(parts, axis, size, stride, mine, extra, after):
    def pick(place):
        part = lax.dynamic_index_in_dim(parts, place, 0, keepdims=False)
        return part if extra is None else jnp.concatenate([part, extra], axis=0)

    own = pick(mine)
    if after:
        own = hold(own, after)
    total = own.astype(F32)
    for d in range(1, parts.shape[0]):
        total = total + send_xor(pick(mine ^ d), axis, size, d * stride).astype(F32)
    return total.astype(parts.dtype)


def gather_group(values, axis, size, stride, count, mine):
    got = [values] + [send_xor(values, axis, size, d * stride) for d in range(1, count)]
    for bit in bits_below(count):
        flip = (mine & bit) != 0
        got = [jnp.where(flip, got[k ^ bit], got[k]) for k in range(count)]
    return jnp.concatenate(got, axis=0)


class PairSum:
    def __init__(self, first, second, wide, plan):
        self.width = first.shape[1]
        self.wide = wide
        self.plan = plan
        self.core = lax.axis_index("ex") % 2
        self.keep = jnp.where(self.core == 0, first, second)
        self.value = jnp.where(self.core == 0, second, first)
        self.extra = None
        self.stage = 0

    def step(self, after=()):
        v = self.value
        deep = len(self.plan)
        if self.stage == 0:
            other = send_xor(v, "ex", self.wide, 1)
            keep = hold(self.keep, after) if after else self.keep
            v = (keep.astype(F32) + other.astype(F32)).astype(v.dtype)
        elif self.stage <= deep:
            axis, size, stride, count = self.plan[self.stage - 1]
            mine = (lax.axis_index(axis) // stride) % count
            parts = v.reshape(count, -1, self.width)
            v = trade_sum(parts, axis, size, stride, mine, self.extra, after)
            if self.extra is not None:
                rows = parts.shape[1]
                self.extra = v[rows:]
                v = v[:rows]
        else:
            axis, size, stride, count = self.plan[2 * deep - self.stage]
            mine = (lax.axis_index(axis) // stride) % count
            v = gather_group(v, axis, size, stride, count, mine)
            if after:
                v = hold(v, after)
        self.stage += 1
        self.value = v
        return v

    def left(self):
        return 2 * len(self.plan) + 1 - self.stage

    def finish(self):
        while self.left():
            self.step()
        return self.value, send_xor(self.value, "ex", self.wide, 1)


def local(
    sizes,
    tokens,
    gain_one,
    shift_one,
    w_qkv,
    w_out,
    gain_two,
    shift_two,
    w_router,
    w_in,
    bias_in,
    w_back,
    bias_back,
    cotangent,
    routes,
    priority,
    image_kind,
):
    toks, width = tokens.shape
    experts = w_router.shape[1]
    hidden_units = w_in.shape[2]
    cap = (42 * toks + 20 * experts - 1) // (20 * experts)
    cap_pad = -(-(cap + 2) // 16) * 16
    wide = -(-cap_pad // 128) * 128
    groups = HEADS // GROUP
    first_w, second_w = w_in[0], w_back[0]
    routes_row = routes.T
    router_row = w_router.T
    sds = jax.ShapeDtypeStruct
    dispatched = (experts, cap_pad, width)

    slots, slot_col, up_rows = call(
        functools.partial(prep_body, experts, cap, cap_pad),
        (sds((8, toks), jnp.int32), sds((toks, 128), jnp.int32), sds(dispatched, BF16)),
        cost=(4e9, 6e6, 0),
        name="prep",
    )(routes_row, priority, cotangent)
    up_in = lax.all_to_all(up_rows, "ex", split_axis=0, concat_axis=0, tiled=True)

    gains = jnp.stack([gain_one, shift_one, gain_two, shift_two])
    col = lambda offset: pl.BlockSpec((width, LANES), lambda g: (0, offset * groups + g))
    smem = pl.BlockSpec(memory_space=pltpu.SMEM)
    per_group = lambda: pl.BlockSpec((1, toks, 3 * LANES), lambda g: (g, 0, 0))
    qkv, mix, logsum, low_one, residual, lowered, probs, sent = call(
        functools.partial(forward_body, experts, cap_pad),
        (
            sds((groups, toks, 3 * LANES), BF16),
            sds((toks, width), BF16),
            sds((16, toks), F32),
            sds((toks, width), BF16),
            sds((toks, width), F32),
            sds((toks, width), BF16),
            sds((experts, toks), F32),
            sds(dispatched, BF16),
        ),
        in_specs=[
            smem,
            whole((toks, width)),
            whole((4, width)),
            col(0),
            col(1),
            col(2),
            pl.BlockSpec((LANES, width), lambda g: (g, 0)),
            whole((experts, width)),
            whole((2, toks)),
            whole((8, toks)),
        ],
        out_specs=[
            per_group(),
            pl.BlockSpec((toks, LANES), lambda g: (0, g)),
            whole((16, toks)),
            whole((toks, width)),
            whole((toks, width)),
            whole((toks, width)),
            whole((experts, toks)),
            whole(dispatched),
        ],
        grid=(groups,),
        scratch=[
            pltpu.VMEM((toks, width), F32),
            pltpu.VMEM((toks, LANES), F32),
            pltpu.VMEM((-(-toks // 128) * 128, 128), F32),
            pltpu.VMEM((2, 16, toks), BF16),
        ],
        cost=(10e9, 20e6, 4e6),
        name="attend",
    )(
        image_kind,
        tokens,
        gains,
        w_qkv,
        w_qkv,
        w_qkv,
        w_out,
        router_row,
        routes_row,
        slots,
    )
    rows_in = lax.all_to_all(sent, "ex", split_axis=0, concat_axis=0, tiled=True)

    blocks = rows_in.shape[0]
    flat_up = up_in.reshape(-1, width)
    z = dot_nt(flat_up, second_w).astype(BF16).reshape(blocks, cap_pad, hidden_units)
    tile = 512 if hidden_units % 512 == 0 else 256
    ff = lambda: pl.BlockSpec((blocks, cap_pad, tile), lambda j: (0, 0, j))
    hidden, grad_pre, grad_slots, grad_gate, bin_sum, bback_sum = call(
        expert_body,
        (
            sds((blocks, cap_pad, hidden_units), BF16),
            sds((blocks, cap_pad, hidden_units), BF16),
            sds((blocks, cap_pad, width), BF16),
            sds((blocks, 8, wide), F32),
            sds((8, hidden_units), F32),
            sds((8, width), F32),
        ),
        in_specs=[
            whole((blocks, cap_pad, width)),
            whole((blocks, cap_pad, width)),
            pl.BlockSpec((width, tile), lambda j: (0, j)),
            pl.BlockSpec((1, tile), lambda j: (0, j)),
            whole((1, width)),
            ff(),
        ],
        out_specs=[
            ff(),
            ff(),
            whole((blocks, cap_pad, width)),
            whole((blocks, 8, wide)),
            pl.BlockSpec((8, tile), lambda j: (0, j)),
            whole((8, width)),
        ],
        grid=(hidden_units // tile,),
        scratch=[
            pltpu.VMEM((blocks, cap_pad, 128), F32),
            pltpu.VMEM((blocks, cap_pad, 128), F32),
            pltpu.VMEM((cap_pad, tile), F32),
            pltpu.VMEM((cap_pad, tile), F32),
        ],
        cost=(8e9, 40e6, 10e6),
        name="expert",
    )(rows_in, up_in, first_w, bias_in, bias_back, z)
    flat_rows = rows_in.reshape(-1, width)
    flat_hidden = hidden.reshape(-1, hidden_units)
    flat_pre = grad_pre.reshape(-1, hidden_units)
    flat_slots = grad_slots.reshape(-1, width)

    gate_row = grad_gate[:, 0:1, :]
    gate_high = gate_row.astype(BF16).astype(F32)
    gate_rows = jnp.concatenate([gate_high, gate_row - gate_high], axis=1)
    gate_rows = jnp.pad(gate_rows, ((0, 0), (cap_pad - 2, 0), (0, width - wide)))
    first_grad = dot_tn(flat_rows, flat_pre).astype(BF16)
    first_out = lax.psum_scatter(first_grad, "rep", scatter_dimension=0, tiled=True).astype(F32)
    flat_pre = hold(flat_pre, [first_grad])
    grad_rows = dot_nt(flat_pre, first_w).reshape(blocks, cap_pad, width)
    tail = lax.broadcasted_iota(jnp.int32, (blocks, cap_pad, width), 1) >= cap_pad - 2
    grad_rows = jnp.where(tail, gate_rows, grad_rows).astype(BF16)
    grad_back = lax.all_to_all(grad_rows, "ex", split_axis=0, concat_axis=0, tiled=True)

    flat_slots = hold(flat_slots, [first_grad, grad_rows])
    second_grad = dot_tn(flat_hidden, flat_slots).astype(BF16)
    second_out = lax.psum_scatter(second_grad, "rep", scatter_dimension=0, tiled=True).astype(F32)
    flat_hidden = hold(flat_hidden, [second_grad])
    tall = blocks * cap_pad // 4
    produced = call(
        produce_body,
        sds((blocks * cap_pad, width), BF16),
        in_specs=[
            pl.BlockSpec((tall, hidden_units), lambda i: (i, 0)),
            whole((hidden_units, width)),
            whole((1, width)),
        ],
        out_specs=pl.BlockSpec((tall, width), lambda i: (i, 0)),
        grid=(4,),
        cost=(1, 1, 0),
        name="produce",
    )(flat_hidden, second_w, bias_back)
    returned = lax.all_to_all(
        produced.reshape(blocks, cap_pad, width), "ex", split_axis=0, concat_axis=0, tiled=True
    )

    reps = sizes["rep"]
    grad_residual, grad_branch, small_two, route_grad = call(
        functools.partial(row_grad_body, experts),
        (
            sds((toks, width), F32),
            sds((toks, width), BF16),
            sds((8, width), F32),
            sds((experts, width), F32),
        ),
        scratch=[pltpu.VMEM((toks, width), F32)],
        cost=(1, 1, 0),
        name="row_grad",
        after=[first_grad, second_grad, produced],
    )(
        slot_col,
        slots,
        routes_row,
        probs,
        lowered,
        residual,
        cotangent,
        gains,
        router_row,
        grad_back,
    )
    out_part = dot_tn(mix, grad_branch).astype(BF16)
    sums = []

    def advance():
        return [s.step() for s in sums]

    reps = sizes["rep"]
    plane_hops = [("ex", sizes["ex"], bit, 2) for bit in bits_below(sizes["ex"])[1:]]
    rep_hops = [("rep", reps, bit, 2) for bit in bits_below(reps)]
    packed_grads = []
    parts = [out_part]
    waiting = [out_part]
    for g in range(groups):
        if g == 1:
            waiting.append(returned)
        packed = call(
            functools.partial(backward_body, g),
            sds((toks, 3 * LANES), BF16),
            in_specs=[
                smem,
                whole((toks, width)),
                pl.BlockSpec((LANES, width), lambda i, g=g: (g, 0)),
                pl.BlockSpec((1, toks, 3 * LANES), lambda i, g=g: (g, 0, 0)),
                pl.BlockSpec((toks, LANES), lambda i, g=g: (0, g)),
                whole((16, toks)),
            ],
            out_specs=whole((toks, 3 * LANES)),
            grid=(1,),
            scratch=[
                pltpu.VMEM((toks, LANES), BF16),
                pltpu.VMEM((16, toks), F32),
                pltpu.VMEM((toks, LANES), F32),
                pltpu.VMEM((toks, LANES), F32),
                pltpu.VMEM((toks, LANES), F32),
            ],
            cost=(8e9, 6e6, 2e6),
            name="attend_back_" + "abcdef"[g],
            after=waiting,
        )(image_kind, grad_branch, w_out, qkv, mix, logsum)
        packed_grads.append(packed)
        waiting = advance()
        parts.append(dot_tn(low_one, packed).astype(BF16))
        if len(parts) == 2:
            order = plane_hops[:: 1 if g == 0 else -1]
            sums.append(PairSum(*parts, sizes["ex"], order + rep_hops))
            parts = []
            waiting.append(sums[-1].value)
        else:
            waiting.append(parts[-1])

    w_groups = [
        jnp.concatenate(
            [w_qkv[:, (p * groups + g) * LANES : (p * groups + g + 1) * LANES] for p in range(3)],
            axis=1,
        )
        for g in range(groups)
    ]
    grad_tokens, small_one = call(
        functools.partial(final_body, groups),
        (sds((toks, width), BF16), sds((8, width), F32)),
        scratch=[pltpu.VMEM((toks, width), F32)],
        cost=(3e9, 14e6, 0),
        name="final",
        after=[sums[1].value],
    )(*packed_grads, *w_groups, tokens, gains, grad_residual)
    ahead, last = sums
    small = jnp.concatenate([small_one[0:2], small_two[0:2], route_grad], axis=0)
    small_rows = small.shape[0]
    added = last.step([small_one])
    last.extra = jnp.pad(small, ((0, -small_rows % 16), (0, 0))).astype(BF16)
    result = call(
        functools.partial(combine_body, experts),
        sds((toks, width), BF16),
        cost=(2e9, 8e6, 0),
        name="combine",
        after=[added, ahead.value, first_out],
    )(slot_col, slots, routes_row, probs, residual, returned)
    ahead.step([result])
    last.step([result])
    bin_sum = hold(bin_sum, [result])
    while ahead.stage < len(plane_hops) + 1:
        ahead.step()
        last.step()
    bias_rows = jnp.concatenate([bin_sum[0].reshape(-1, width), bback_sum[0:1]], axis=0)
    bias_rows = jnp.pad(bias_rows, ((0, -bias_rows.shape[0] % 16), (0, 0))).astype(BF16)
    ahead.extra = bias_rows
    while last.left() > 1:
        if ahead.left():
            ahead.step([second_out] if ahead.left() == 1 else ())
        last.step()
    last.step()
    pairs = [ahead.finish(), last.finish()]
    rank = lax.axis_index("rep")
    bias_sum = ahead.extra.astype(F32)
    bin_out = bias_sum[: hidden_units // width].reshape(-1)
    bin_out = lax.dynamic_slice_in_dim(bin_out, rank * (hidden_units // reps), hidden_units // reps)
    bback_out = lax.dynamic_slice_in_dim(
        bias_sum[hidden_units // width], rank * (width // reps), width // reps
    )
    small = last.extra.astype(F32)
    small = small + send_xor(small, "ex", sizes["ex"], 1)
    core = lax.axis_index("ex") % 2
    out_grad = jnp.where(core == 0, *pairs[0]).astype(F32)
    qkv_grad = place_qkv(pairs, core)
    return (
        result,
        grad_tokens,
        small[0],
        small[1],
        qkv_grad,
        out_grad,
        small[2],
        small[3],
        small[4:small_rows].T,
        first_out[None],
        bin_out[None],
        second_out[None],
        bback_out[None],
    )


def solution(mesh):
    both = ("rep", "ex")
    in_specs = (
        P(both, None),
        P(),
        P(),
        P(),
        P(),
        P(),
        P(),
        P(),
        P("ex", None, None),
        P("ex", None),
        P("ex", None, None),
        P("ex", None),
        P(both, None),
        P(both, None),
        P(both, None),
        P(both),
    )
    out_specs = (
        P(both, None),
        P(both, None),
        P(),
        P(),
        P(),
        P(),
        P(),
        P(),
        P(),
        P("ex", "rep", None),
        P("ex", "rep"),
        P("ex", "rep", None),
        P("ex", "rep"),
    )
    return jax.shard_map(
        functools.partial(local, dict(mesh.shape)),
        mesh=mesh,
        in_specs=in_specs,
        out_specs=out_specs,
        check_vma=False,
    )
```
